32 devices in a mesh: dp: 8 (over z, x), tensor: 4 (over y, core).
Axes of the slice: x: 2, y: 2, z: 4, core: 2. Of those that a mesh axis runs over, the one named last changes fastest.
Arguments:
- inputs: bfloat16 [3, 8, 1280, 512], P(None, 'dp', 'tensor'), may hold values from -6 to 6
- attention_norm_gain: float32 [512], replicated, may hold values from 0.5 to 1.5
- attention_norm_bias: float32 [512], replicated, may hold values from -1 to 1
- query_weight: bfloat16 [512, 512], P('dp', 'tensor'), may hold values from -0.25 to 0.25
- key_weight: bfloat16 [512, 512], P('dp', 'tensor'), may hold values from -0.25 to 0.25
- value_weight: bfloat16 [512, 512], P('dp', 'tensor'), may hold values from -0.25 to 0.25
- relative_weight: bfloat16 [512, 512], P('dp', 'tensor'), may hold values from -0.5 to 0.5
- head_bias: float32 [2, 512], P(None, 'tensor'), may hold values from -3 to 3
- output_weight: bfloat16 [512, 512], P('tensor', 'dp'), may hold values from -3 to 3
- feedforward_norm_gain: float32 [512], replicated, may hold values from 0.5 to 1.5
- feedforward_norm_bias: float32 [512], replicated, may hold values from -1 to 1
- up_weight: bfloat16 [512, 2048], P('dp', 'tensor'), may hold values from -0.25 to 0.25
- up_bias: float32 [2048], P('tensor'), may hold values from -1 to 1
- down_weight: bfloat16 [2048, 512], P('tensor', 'dp'), may hold values from -0.125 to 0.125
- down_bias: float32 [512], replicated, may hold values from -1 to 1
- parents: int32 [3, 8, 8], P(None, 'dp'), may hold values from 0 to 4, as said below
- positions: int32 [3, 8, 1280], P(None, 'dp'), may hold values from 0 to 639, as said below
- cotangent: bfloat16 [3, 8, 1280, 512], P(None, 'dp', 'tensor'), may hold values from -6 to 6
Outputs:
- output: float32 [3, 8, 1280, 512], P(None, 'dp', 'tensor')
- input_grad: float32 [3, 8, 1280, 512], P(None, 'dp', 'tensor')
- mixer_gain_grad: float32 [512], P(('dp', 'tensor'))
- mixer_shift_grad: float32 [512], P(('dp', 'tensor'))
- query_weight_grad: float32 [512, 512], P('dp', 'tensor')
- key_weight_grad: float32 [512, 512], P('dp', 'tensor')
- value_weight_grad: float32 [512, 512], P('dp', 'tensor')
- relative_weight_grad: float32 [512, 512], P('dp', 'tensor')
- head_bias_grad: float32 [2, 512], P(None, ('dp', 'tensor'))
- output_weight_grad: float32 [512, 512], P('tensor', 'dp')
- feed_gain_grad: float32 [512], P(('dp', 'tensor'))
- feed_shift_grad: float32 [512], P(('dp', 'tensor'))
- up_weight_grad: float32 [512, 2048], P('dp', 'tensor')
- up_bias_grad: float32 [2048], P(('dp', 'tensor'))
- down_weight_grad: float32 [2048, 512], P('tensor', 'dp')
- down_bias_grad: float32 [512], P(('dp', 'tensor'))
The draws below stay inside these ranges and needn't reach their ends.
Inputs may be any that keep to these rules, and one draw needn't show every extreme that they name: `parents`: 0 names the trunk and b = 1 .. 4 names branch b. `positions`: trunk token i has position i; the o-th token of a branch has 512 + o; the o-th token of a leaf has 512 + o if its parent is the trunk, else 512 + 64 + o.
All inputs are finite; a program needn't handle non-finite values.
Results may differ from the reference program's by a relative error of at most 0.015.
Values may be sent and summed in bfloat16 or wider, within the bound.
No kernel may reach another device: no remote copies, remote signals or barrier semaphores. Data moves between devices by JAX's collectives and lax.ppermute only.
A program may use at most 192 MiB of HBM per device.

```python
import math
import jax
import jax.numpy as jnp
from jax import lax

D = 512
HEADS = 8
HD = 64
FF = 2048
TRUNK = 512
SEG = 64
BRANCHES = 4
LEAVES = 8
MB = 3
TREE = 1280
TREES = 8


def leaf_hosts(key):
    return jax.random.randint(jax.random.fold_in(key, 11), (MB, TREES, LEAVES), 0, BRANCHES + 1).astype(jnp.int32)


def draw_parents(key, part):
    return leaf_hosts(key)


def draw_positions(key, part):
    hosts = leaf_hosts(key)
    index = jnp.arange(TREE, dtype=jnp.int32)
    offset = (index - TRUNK) % SEG
    segment = jnp.where(index < TRUNK, 0, 1 + (index - TRUNK) // SEG)
    leaf = segment - 1 - BRANCHES
    host_token = jnp.take(hosts, jnp.clip(leaf, 0, LEAVES - 1), axis=-1)
    leaf_pos = TRUNK + offset + SEG * (host_token > 0).astype(jnp.int32)
    inner = jnp.where(leaf[None, None, :] < 0, TRUNK + offset[None, None, :], leaf_pos)
    return jnp.where(index[None, None, :] < TRUNK, index[None, None, :], inner).astype(jnp.int32)


def levels(key, shape, pieces, least, high):
    gain = 1.0
    for axis_at, parts in pieces:
        heights = jax.random.uniform(jax.random.fold_in(jax.random.fold_in(key, 6), axis_at), (parts,), jnp.float32, least / len(pieces), high / len(pieces))
        gain = gain * jnp.repeat(jnp.exp(heights), shape[axis_at] // parts).reshape((-1,) + (1,) * (len(shape) - 1 - axis_at))
    return gain


def scatter_about(stream_key, extent, scale, bound, cuts=(), kind=jnp.bfloat16):
    values = jax.random.normal(stream_key, extent, jnp.float32) * scale
    if len(cuts) > 0:
        values = levels(stream_key, extent, cuts, -0.22, 0.18) * values
    return jnp.clip(values, min=-bound, max=bound).astype(kind)


def setup_inputs(seed: int = 0) -> dict:
    key_list = jax.random.split(jax.random.key(seed), 19)
    return {
        "inputs": scatter_about(key_list[0], (MB, TREES, TREE, D), 1.0, 6.0, ((1, 8), (2, 4))),
        "attention_norm_gain": jnp.clip(1.0 + 0.1 * jax.random.normal(key_list[1], (D,), jnp.float32), 0.5, 1.5),
        "attention_norm_bias": scatter_about(key_list[2], (D,), 0.2, 1.0, (), jnp.float32),
        "query_weight": scatter_about(key_list[3], (D, D), D ** -0.5, 0.25, ((0, 8), (1, 4))),
        "key_weight": scatter_about(key_list[4], (D, D), D ** -0.5, 0.25, ((0, 8), (1, 4))),
        "value_weight": scatter_about(key_list[5], (D, D), D ** -0.5, 0.25, ((0, 8), (1, 4))),
        "relative_weight": scatter_about(key_list[6], (D, D), (D // 4) ** -0.5, 0.5, ((0, 8), (1, 4))),
        "head_bias": scatter_about(key_list[7], (2, D), 0.5, 3.0, ((1, 4),), jnp.float32),
        "output_weight": scatter_about(key_list[8], (D, D), (D // 128) ** -0.5, 3.0, ((0, 4), (1, 8))),
        "feedforward_norm_gain": jnp.clip(1.0 + 0.1 * jax.random.normal(key_list[9], (D,), jnp.float32), 0.5, 1.5),
        "feedforward_norm_bias": scatter_about(key_list[10], (D,), 0.2, 1.0, (), jnp.float32),
        "up_weight": scatter_about(key_list[11], (D, FF), D ** -0.5, 0.25, ((0, 8), (1, 4))),
        "up_bias": scatter_about(key_list[12], (FF,), 0.2, 1.0, ((0, 4),), jnp.float32),
        "down_weight": scatter_about(key_list[13], (FF, D), FF ** -0.5, 0.125, ((0, 4), (1, 8))),
        "down_bias": scatter_about(key_list[14], (D,), 0.2, 1.0, (), jnp.float32),
        "parents": draw_parents(jax.random.fold_in(key_list[18], 71), 0),
        "positions": draw_positions(jax.random.fold_in(key_list[18], 71), 0),
        "cotangent": scatter_about(key_list[17], (MB, TREES, TREE, D), 1.0, 6.0, ((1, 8), (2, 4))),
    }


@jax.custom_vjp
def low(v):
    return lax.optimization_barrier(v.astype(jnp.bfloat16)).astype(jnp.float32)

@jax.custom_vjp
def low_back(v):
    return v

def low_keep(v):
    return (low(v), None)

def low_pass(kept, grad):
    return (grad,)

def back_keep(v):
    return (v, None)

def back_low(kept, grad):
    return (low(grad),)
low.defvjp(low_keep, low_pass)
low_back.defvjp(back_keep, back_low)
HIGHEST = lax.Precision.HIGHEST

def matmul(left, right):
    return jnp.dot(left, right, precision=HIGHEST, preferred_element_type=jnp.float32)

def layer_norm_rows(values_in, norm_gain, norm_bias):
    centered_rows = values_in - lax.optimization_barrier(jnp.mean(values_in, axis=-1, keepdims=True))
    spread = lax.optimization_barrier(jnp.mean(centered_rows * centered_rows, axis=-1, keepdims=True))
    return centered_rows * lax.rsqrt(spread + 1e-05) * norm_gain + norm_bias

def gelu_value(preact):
    return 0.5 * preact * (1.0 + lax.erf(preact * 0.7071067811865476))

def sinusoid(pos):
    steps = jnp.arange(D // 2, dtype=jnp.float32)
    freq = jnp.exp(steps * (-2.0 * math.log(10000.0) / D))
    angle = pos.astype(jnp.float32)[:, None] * freq[None, :]
    return (jnp.sin(angle), jnp.cos(angle))

def visible(hosts):
    index = jnp.arange(TREE, dtype=jnp.int32)
    segment = jnp.where(index < TRUNK, 0, 1 + (index - TRUNK) // SEG)
    leaf = segment - 1 - BRANCHES
    match = leaf[:, None] == jnp.arange(LEAVES, dtype=jnp.int32)[None, :]
    host = lax.optimization_barrier(jnp.sum(jnp.where(match, hosts[None, :], 0), axis=1))
    host = jnp.where(leaf >= 0, host, -1)
    same = (segment[:, None] == segment[None, :]) & (index[None, :] <= index[:, None])
    above = (segment[:, None] > 0) & (segment[None, :] == 0)
    hosted = host[:, None] == segment[None, :]
    return same | above | hosted

def tree_layer(weights, tree_input, hosts, pos):
    attention_norm_gain, attention_norm_bias, query_weight, key_weight, value_weight, relative_weight, head_bias, output_weight, feedforward_norm_gain, feedforward_norm_bias, up_weight, up_bias, down_weight, down_bias = weights
    normed = low(layer_norm_rows(tree_input, attention_norm_gain, attention_norm_bias))
    query = low_back(matmul(normed, query_weight))
    keys = low(low_back(matmul(normed, key_weight))).reshape(TREE, HEADS, HD)
    values = low(low_back(matmul(normed, value_weight))).reshape(TREE, HEADS, HD)
    content = low(query + head_bias[0]).reshape(TREE, HEADS, HD)
    position = low(query + head_bias[1]).reshape(TREE, HEADS, HD)
    sines, cosines = sinusoid(pos)
    table = low(jnp.concatenate([cosines, sines], axis=-1))
    relative = low_back(jnp.einsum('thd,rhd->htr', position, relative_weight.reshape(D, HEADS, HD), precision=HIGHEST))
    half = D // 2
    rsin = relative[..., :half]
    rcos = relative[..., half:]
    shifted = low(jnp.concatenate([rsin * sines + rcos * cosines, rcos * sines - rsin * cosines], axis=-1))
    raw = jnp.einsum('thd,shd->hts', content, keys, precision=HIGHEST) + jnp.einsum('htr,sr->hts', shifted, table, precision=HIGHEST)
    scores = low_back(raw * (1.0 / math.sqrt(HD)))
    mask = visible(hosts)
    scores = jnp.where(mask[None], scores, -1e+30)
    peak = lax.optimization_barrier(jnp.max(scores, axis=-1, keepdims=True))
    expd = jnp.exp(scores - peak)
    probs = expd / lax.optimization_barrier(jnp.sum(expd, axis=-1, keepdims=True))
    attended = jnp.einsum('hts,shd->thd', low(probs), values, precision=HIGHEST).reshape(TREE, D)
    attended = low(low_back(attended))
    residual_middle = tree_input + low_back(matmul(attended, output_weight))
    normed2 = low(layer_norm_rows(residual_middle, feedforward_norm_gain, feedforward_norm_bias))
    preact = low_back(matmul(normed2, up_weight) + up_bias)
    hidden = low(gelu_value(preact))
    return residual_middle + low_back(matmul(hidden, down_weight)) + down_bias

def forward(flat_in, weights, hosts, pos):
    step = jax.checkpoint(tree_layer)
    return lax.map(lambda item: step(weights, item[0], item[1], item[2]), (flat_in, hosts, pos))

def reference(inputs, attention_norm_gain, attention_norm_bias, query_weight, key_weight, value_weight, relative_weight, head_bias, output_weight, feedforward_norm_gain, feedforward_norm_bias, up_weight, up_bias, down_weight, down_bias, parents, positions, cotangent):
    count = MB * TREES
    flat_in = inputs.astype(jnp.float32).reshape(count, TREE, D)
    weights = (attention_norm_gain.astype(jnp.float32), attention_norm_bias.astype(jnp.float32), query_weight.astype(jnp.float32), key_weight.astype(jnp.float32), value_weight.astype(jnp.float32), relative_weight.astype(jnp.float32), head_bias.astype(jnp.float32), output_weight.astype(jnp.float32), feedforward_norm_gain.astype(jnp.float32), feedforward_norm_bias.astype(jnp.float32), up_weight.astype(jnp.float32), up_bias.astype(jnp.float32), down_weight.astype(jnp.float32), down_bias.astype(jnp.float32))
    hosts = parents.reshape(count, LEAVES)
    pos = positions.reshape(count, TREE)

    def run(flat_values, weight_set):
        return forward(flat_values, weight_set, hosts, pos)
    result, pull = jax.vjp(run, flat_in, weights)
    flat_grad, weight_grads = pull(cotangent.astype(jnp.float32).reshape(count, TREE, D))
    g_mixer_gain, g_mixer_shift, g_query, g_key, g_value, g_relative, g_head, g_output, g_feed_gain, g_feed_shift, g_up, g_up_bias, g_down, g_down_bias = weight_grads
    return (result.reshape(MB, TREES, TREE, D), flat_grad.reshape(MB, TREES, TREE, D), g_mixer_gain, g_mixer_shift, g_query, g_key, g_value, g_relative, g_head, g_output, g_feed_gain, g_feed_shift, g_up, g_up_bias, g_down, g_down_bias)
```

```python
import functools
import math

import jax
import jax.numpy as jnp
from jax import lax
from jax.experimental import pallas as pl
from jax.experimental.pallas import tpu as pltpu
from jax.sharding import PartitionSpec as P

D = 512
HD = 64
FF = 2048
TRUNK = 512
SEG = 64
BRANCHES = 4
LEAVES = 8
MB = 3
TREE = 1280
DEPTH = 640
COLS = 128
QUARTER = 320
PADDED = 1024
QB = 256
EPS = 1e-05
BF = jnp.bfloat16
F32 = jnp.float32

CHUNKS = (
    ((0, "causal"),),
    ((0, None), (256, "causal")),
    ((0, None), (256, None), (512, "segment")),
    ((0, None), (256, None), (512, "host"), (768, "segment")),
    ((0, None), (256, None), (512, "host"), (1024, "segment")),
)
OFFSETS = (0, 256, 768, 1536, 2560)
SAVED = 3584


def nn(a, b):
    return lax.dot_general(a, b, (((1,), (0,)), ((), ())), preferred_element_type=F32)


def nt(a, b):
    return lax.dot_general(a, b, (((1,), (1,)), ((), ())), preferred_element_type=F32)


def key_runs(block):
    runs = []
    for n, (start, _) in enumerate(CHUNKS[block]):
        if runs and runs[-1][0] + runs[-1][1] == start:
            runs[-1][1] += 256
        else:
            runs.append([start, 256, n * 256])
    return runs


def chunk_mask(kind, block, parents, micro):
    key = lax.broadcasted_iota(jnp.int32, (256, QB), 0)
    query = lax.broadcasted_iota(jnp.int32, (256, QB), 1)
    if kind == "causal":
        return key <= query
    if kind == "segment":
        return (key <= query) & (key // SEG == query // SEG)
    lane = lax.broadcasted_iota(jnp.int32, (1, QB), 1) // SEG
    first = (block - 3) * 4
    host = jnp.zeros((1, QB), jnp.int32)
    for n in range(4):
        host = jnp.where(lane == n, parents[micro * LEAVES + first + n], host)
    return (key // SEG + 1) == host


def raised(parents, micro, leaf):
    return (parents[micro * LEAVES + leaf] > 0).astype(jnp.int32)


def per_token_columns(table_ref, out_ref, rows, parents, micro):
    out_ref[rows, 0:TRUNK] = table_ref[:, 0:TRUNK]
    last = table_ref[:, TRUNK:DEPTH]
    turned = pltpu.roll(last, SEG, 1)
    lane = lax.broadcasted_iota(jnp.int32, (1, 128), 1)
    low = jnp.where(lane < SEG, last, turned)
    out_ref[rows, TRUNK : TRUNK + 128] = low
    out_ref[rows, TRUNK + 128 : TRUNK + 256] = low
    for pair in range(LEAVES // 2):
        left = raised(parents, micro, 2 * pair)
        right = raised(parents, micro, 2 * pair + 1)
        straight = jnp.where(lane < SEG, 1 - left, right)
        at = TRUNK + 256 + pair * 128
        out_ref[rows, at : at + 128] = jnp.where(straight > 0, last, turned)


def norm_kernel(x_ref, gain_ref, bias_ref, *outs):
    for n in range(MB):
        x = x_ref[n, 0].astype(F32)
        centered = x - jnp.mean(x, axis=-1, keepdims=True)
        spread = jnp.mean(centered * centered, axis=-1, keepdims=True)
        outs[n][...] = (
            centered * lax.rsqrt(spread + EPS) * gain_ref[...] + bias_ref[...]
        ).astype(BF)


def forward_kernel(
    micro, ids, parents, x0, x1, x2, x3, w, hb, sincos, table,
    att0, att1, att2, att3, probs, inverse, natural, turned,
    kcat, vt, ct, sct, qt, scores, att_t,
):
    head = pl.program_id(0)

    @pl.when(head == 0)
    def _():
        for n, x in enumerate((x0, x1, x2, x3)):
            y = nn(x[...], w[:, 0 : 3 * COLS])
            rows = pl.ds(pl.multiple_of(ids[n] * QUARTER, SEG), QUARTER)
            q = y[:, 0:COLS]
            natural[0, rows, :] = (q + hb[0:1, :]).astype(BF)
            natural[1, rows, :] = (q + hb[1:2, :]).astype(BF)
            kcat[rows, D : D + COLS] = y[:, COLS : 2 * COLS].astype(BF)
            natural[2, rows, :] = y[:, 2 * COLS : 3 * COLS].astype(BF)
        ct[...] = jnp.transpose(natural[0])
        turned[0] = jnp.transpose(kcat[:, D : D + COLS])
        vt[...] = jnp.transpose(natural[2])
        kcat[0 : TRUNK + SEG, 0:D] = table[0 : TRUNK + SEG, :]
        for n in range(1, BRANCHES):
            kcat[TRUNK + n * SEG : TRUNK + (n + 1) * SEG, 0:D] = table[TRUNK : TRUNK + SEG, :]
        for n in range(LEAVES):
            at = TRUNK + (BRANCHES + n) * SEG
            row = pl.multiple_of(TRUNK + SEG * raised(parents, micro, n), SEG)
            kcat[at : at + SEG, 0:D] = table[pl.ds(row, SEG), :]
        per_token_columns(sincos, sct, slice(None), parents, micro)

    mine = lax.broadcasted_iota(jnp.int32, (1, COLS), 1) // HD == head
    mine_t = lax.broadcasted_iota(jnp.int32, (COLS, 1), 0) // HD == head
    factor = math.log2(math.e) / math.sqrt(HD)
    for block in range(5):
        at = block * QB
        cols = slice(at, at + QB)
        position = jnp.where(mine, natural[1, cols, :], 0)
        relative = nt(w[:, 3 * COLS : 4 * COLS], position)
        rs, rc = relative[0:256], relative[256:512]
        sines, cosines = sct[0:256, cols], sct[256:512, cols]
        qt[0:256, :] = (rs * sines + rc * cosines).astype(BF)
        qt[256:512, :] = (rc * sines - rs * cosines).astype(BF)
        qt[512:640, :] = jnp.where(mine_t, ct[:, cols], 0)
        peak = None
        for n, (start, kind) in enumerate(CHUNKS[block]):
            s = nn(kcat[start : start + 256, :], qt[...])
            if kind is not None:
                s = jnp.where(chunk_mask(kind, block, parents, micro), s, -1e30)
            scores[n * 256 : (n + 1) * 256, :] = s
            high = jnp.max(s, axis=0, keepdims=True)
            peak = high if peak is None else jnp.maximum(peak, high)
        total = jnp.zeros((1, QB), F32)
        for n in range(len(CHUNKS[block])):
            e = jnp.exp2((scores[n * 256 : (n + 1) * 256, :] - peak) * factor)
            total = total + jnp.sum(e, axis=0, keepdims=True)
            row = OFFSETS[block] + n * 256
            probs[0, row : row + 256, :] = e.astype(BF)
        out = None
        for start, keys, row in key_runs(block):
            row = OFFSETS[block] + row
            term = nn(vt[:, start : start + keys], probs[0, row : row + keys, :])
            out = term if out is None else out + term
        over = 1.0 / total
        inverse[0, :, cols] = jnp.broadcast_to(over, (8, QB))
        att_t[:, cols] = jnp.where(mine_t, out * over, att_t[:, cols])

    @pl.when(head == 1)
    def _():
        full = att_t[...].astype(BF)
        turned[1] = full
        kcat[:, 0:COLS] = jnp.transpose(full)
        for n, out in enumerate((att0, att1, att2, att3)):
            rows = pl.ds(pl.multiple_of(ids[n] * QUARTER, SEG), QUARTER)
            out[...] = kcat[rows, 0:COLS]


def middle_kernel(
    ids, a0, a1, a2, a3, x, cot, wud, wo, gain, bias, up_bias, down_bias,
    in0, in1, in2, in3, in4, in5,
    out, hid, pg, n2_out, mix_out, att_out, mgrad, g0, g1, g2, g3, small, ubg,
    mid, xhat, rstd, n2, ffn, n2g,
):
    step = pl.program_id(0)
    groups, rows = wo.shape[0], wo.shape[2]

    @pl.when(step == 0)
    def _():
        m = x[0, 0].astype(F32)
        for n, a in enumerate((a0, a1, a2, a3)):
            m = m + nt(a[...], wo[:, ids[n]].reshape(groups * rows, COLS))
            lanes = pl.ds(pl.multiple_of(ids[n] * COLS, COLS), COLS)
            att_out[:, lanes] = a[...]
        mid[...] = m
        centered = m - jnp.mean(m, axis=-1, keepdims=True)
        spread = jnp.mean(centered * centered, axis=-1, keepdims=True)
        inv = lax.rsqrt(spread + EPS)
        xh = centered * inv
        rstd[...] = inv
        xhat[...] = xh
        n2[...] = (xh * gain[...] + bias[...]).astype(BF)
        n2_out[...] = n2[...]
        ffn[...] = jnp.zeros_like(ffn)
        n2g[...] = jnp.zeros_like(n2g)

    up = wud[:, 0, :, 0:D].reshape(D, D)
    down = wud[:, 0, :, D : 2 * D].reshape(D, D)
    pre = nn(n2[...], up) + up_bias[pl.ds(step, 1), :]
    cdf = 0.5 * (1.0 + lax.erf(pre * 0.7071067811865476))
    h = (pre * cdf).astype(BF)
    hid[...] = h
    slope = cdf + pre * jnp.exp(-0.5 * pre * pre) * 0.3989422804014327
    hg = nn(cot[0, 0], down)
    p = (hg * slope).astype(BF)
    pg[...] = p
    ubg[pl.ds(step, 1), :] = jnp.sum(p.astype(F32), axis=0, keepdims=True)
    ffn[...] += nt(h, down)
    n2g[...] += nt(p, up)

    @pl.when(step == 3)
    def _():
        out[0, 0] = mid[...] + ffn[...] + down_bias[...]
        g = n2g[...]
        xh = xhat[...]
        c = cot[0, 0].astype(F32)
        small[0:1, :] = jnp.sum(g * xh, axis=0, keepdims=True)
        small[1:2, :] = jnp.sum(g, axis=0, keepdims=True)
        small[2:3, :] = jnp.sum(c, axis=0, keepdims=True)
        e = g * gain[...]
        mg = c + rstd[...] * (
            e
            - jnp.mean(e, axis=-1, keepdims=True)
            - xh * jnp.mean(e * xh, axis=-1, keepdims=True)
        )
        mgrad[...] = mg
        mixed = mg.astype(BF)
        mix_out[...] = mixed
        for n, g_out in enumerate((g0, g1, g2, g3)):
            g_out[...] = nn(mixed, wo[:, ids[n]].reshape(groups * rows, COLS)).astype(BF)


def weights_kernel(ids, n2, cot, mix, hid, pg, att, keep, send, n2t, cott, mixt):
    step = pl.program_id(0)

    @pl.when(step == 0)
    def _():
        n2t[...] = jnp.transpose(n2[...])
        cott[...] = jnp.transpose(cot[...])
        mixt[...] = jnp.transpose(mix[...])

    def write(ref):
        ref[0, :, 0:D] = nn(n2t[...], pg[...]).astype(BF)
        ref[0, :, D : 2 * D] = nn(cott[...], hid[...]).astype(BF)
        ref[0, :, 2 * D :] = nn(mixt[...], att[...]).astype(BF)

    @pl.when(step < 2)
    def _():
        write(send)

    @pl.when(step >= 2)
    def _():
        write(keep)


def backward_kernel(
    micro, ids, parents, d0, d1, d2, d3, x0, x1, x2, x3, w, sincos,
    probs, inverse, natural, turned, acc_w, acc_r, acc_s,
    keep, send, out_w, out_r, out_s,
    do, dot, kcat_t, sct, ds, dk, dv, dq_t, hc, hp, dall, xall,
):
    head = pl.program_id(0)

    @pl.when(head == 0)
    def _():
        for n, d in enumerate((d0, d1, d2, d3)):
            rows = pl.ds(pl.multiple_of(ids[n] * QUARTER, SEG), QUARTER)
            do[rows, :] = d[...]
        dot[...] = jnp.transpose(do[...])
        per_token_columns(sincos, sct, slice(None), parents, micro)
        kcat_t[0:256, :] = sct[256:512, :].astype(BF)
        kcat_t[256:512, :] = sct[0:256, :].astype(BF)
        kcat_t[512:640, :] = turned[0]
        dk[...] = jnp.zeros_like(dk)
        dv[...] = jnp.zeros_like(dv)
        hc[...] = jnp.zeros_like(hc)
        hp[...] = jnp.zeros_like(hp)
        out_r[...] = acc_r[...]

    mine = lax.broadcasted_iota(jnp.int32, (1, COLS), 1) // HD == head
    mine_t = lax.broadcasted_iota(jnp.int32, (COLS, 1), 0) // HD == head
    factor = 1.0 / math.sqrt(HD)
    for block in range(5):
        at = block * QB
        cols = slice(at, at + QB)
        over = inverse[0, 0:1, cols]
        grad = jnp.where(mine_t, dot[:, cols].astype(F32), 0.0) * over
        delta = jnp.sum(grad * turned[1, :, cols].astype(F32), axis=0, keepdims=True)
        grad_t = grad.astype(BF)
        grad_n = jnp.transpose(grad_t)
        content = jnp.where(mine, natural[0, cols, :], 0)
        position = jnp.where(mine, natural[1, cols, :], 0)
        for n, (start, _) in enumerate(CHUNKS[block]):
            row = OFFSETS[block] + n * 256
            p = probs[0, row : row + 256, :]
            keys = slice(start, start + 256)
            dp = nn(natural[2, keys, :], grad_t)
            s = (p.astype(F32) * (dp - delta)).astype(BF)
            ds[n * 256 : (n + 1) * 256, :] = s
            dv[keys, :] += nn(p, grad_n)
            dk[keys, :] += nn(s, content)
        dq = None
        for start, keys, row in key_runs(block):
            term = nn(kcat_t[:, start : start + keys], ds[row : row + keys, :])
            dq = term if dq is None else dq + term
        dq = dq * factor
        s1, s2 = dq[0:256], dq[256:512]
        sines, cosines = sct[0:256, cols], sct[256:512, cols]
        relative = jnp.concatenate(
            [(s1 * sines - s2 * cosines).astype(BF), (s1 * cosines + s2 * sines).astype(BF)],
            axis=0,
        )
        w_rel = w[:, 3 * COLS : 4 * COLS]
        pgrad = lax.dot_general(
            w_rel, relative, (((0,), (0,)), ((), ())), preferred_element_type=F32
        )
        out_r[...] += nn(relative, position)
        pgrad = jnp.where(mine_t, pgrad, 0.0)
        cgrad = jnp.where(mine_t, dq[512:640], 0.0)
        hp[...] += pgrad
        hc[...] += cgrad
        dq_t[:, cols] = jnp.where(mine_t, (pgrad + cgrad).astype(BF), dq_t[:, cols])

    @pl.when(head == 1)
    def _():
        dall[:, 0:COLS] = jnp.transpose(dq_t[...])
        dall[:, COLS : 2 * COLS] = (dk[...] * factor).astype(BF)
        dall[:, 2 * COLS :] = dv[...].astype(BF)
        w_in = w[:, 0 : 3 * COLS]
        gain_sum = acc_s[0:1, :]
        shift_sum = acc_s[1:2, :]
        for n, (x, out) in enumerate(
            ((x0, keep.at[0]), (x1, send.at[0]), (x2, keep.at[1]), (x3, send.at[1]))
        ):
            rows = pl.ds(pl.multiple_of(ids[n] * QUARTER, SEG), QUARTER)
            g = nt(dall[rows, :], w_in)
            out[...] = g.astype(BF)
            xv = x[...]
            xall[rows, :] = xv
            gain_sum = gain_sum + jnp.sum(g * xv.astype(F32), axis=0, keepdims=True)
            shift_sum = shift_sum + jnp.sum(g, axis=0, keepdims=True)
        out_w[...] = acc_w[...] + lax.dot_general(
            dall[...], xall[...], (((0,), (0,)), ((), ())), preferred_element_type=F32
        )
        out_s[0:1, :] = gain_sum
        out_s[1:2, :] = shift_sum
        both = []
        for n, h in enumerate((hc, hp)):
            v = jnp.transpose(h[:, 0:128] + h[:, 128:256])
            both.append(jnp.sum(v, axis=0, keepdims=True))
        out_s[2:3, 0:COLS] = acc_s[2:3, 0:COLS] + both[0]
        out_s[3:4, 0:COLS] = acc_s[3:4, 0:COLS] + both[1]


def tail_kernel(x, gain, mgrad, own, near, far, _, out):
    g = own[0].astype(F32) + near[0].astype(F32) + far[...].astype(F32)
    xf = x[0, 0].astype(F32)
    centered = xf - jnp.mean(xf, axis=-1, keepdims=True)
    spread = jnp.mean(centered * centered, axis=-1, keepdims=True)
    inv = lax.rsqrt(spread + EPS)
    xh = centered * inv
    e = g * gain[...]
    out[0, 0] = mgrad[...] + inv * (
        e - jnp.mean(e, axis=-1, keepdims=True) - xh * jnp.mean(e * xh, axis=-1, keepdims=True)
    )


def whole(shape):
    return pl.BlockSpec(shape, lambda i, *_: (0,) * len(shape))


def cost(flops, nbytes, trans=0):
    return pl.CostEstimate(flops=int(flops), bytes_accessed=int(nbytes), transcendentals=int(trans))


def struct(shape, dtype):
    return jax.ShapeDtypeStruct(shape, dtype)


def call(kernel, grid, prefetch, in_specs, out_specs, out_shape, scratch, estimate, alias=None):
    return pl.pallas_call(
        kernel,
        out_shape=out_shape,
        grid_spec=pltpu.PrefetchScalarGridSpec(
            num_scalar_prefetch=prefetch,
            grid=grid,
            in_specs=in_specs,
            out_specs=out_specs,
            scratch_shapes=scratch,
        ),
        input_output_aliases=alias or {},
        cost_estimate=estimate,
        compiler_params=pltpu.CompilerParams(
            dimension_semantics=("arbitrary",) * len(grid), vmem_limit_bytes=56 << 20
        ),
    )


def swap(value, bits):
    return lax.ppermute(value, "tensor", [(n, n ^ bits) for n in range(4)])


def body(
    inputs,
    attention_norm_gain,
    attention_norm_bias,
    query_weight,
    key_weight,
    value_weight,
    relative_weight,
    head_bias,
    output_weight,
    feedforward_norm_gain,
    feedforward_norm_bias,
    up_weight,
    up_bias,
    down_weight,
    down_bias,
    parents,
    positions,
    cotangent,
):
    del positions
    n_dp = lax.axis_size("dp")
    rows = query_weight.shape[0]
    me = lax.axis_index("tensor").astype(jnp.int32)
    ids = me ^ jnp.arange(4, dtype=jnp.int32)
    hosts = parents.reshape(-1)
    gain1 = attention_norm_gain.reshape(1, D)
    bias1 = attention_norm_bias.reshape(1, D)
    gain2 = feedforward_norm_gain.reshape(1, D)
    bias2 = feedforward_norm_bias.reshape(1, D)

    shard = jnp.concatenate([query_weight, key_weight, value_weight, relative_weight], axis=1)
    w_heads = lax.all_to_all(
        jnp.broadcast_to(shard[None], (n_dp, rows, 4 * COLS)), "dp", 0, 0, tiled=True
    ).reshape(D, 4 * COLS)

    normed = call(
        norm_kernel,
        (1,),
        0,
        [whole((MB, 1, QUARTER, D)), whole((1, D)), whole((1, D))],
        [whole((QUARTER, D))] * MB,
        [struct((QUARTER, D), BF)] * MB,
        [],
        cost(MB * QUARTER * D * 10, MB * QUARTER * D * 4),
    )(inputs, gain1, bias1)
    tokens = []
    for m in range(MB):
        far = swap(normed[m], 2)
        tokens.append((normed[m], swap(normed[m], 1), far, swap(far, 1)))

    shard = jnp.concatenate([up_weight, down_weight.T, output_weight.T], axis=1)
    packed = 2 * D + COLS
    w_all = lax.all_gather(shard, ("dp", "tensor"), axis=0, tiled=False)
    w_all = w_all.reshape(n_dp, 4, rows, packed)
    if rows % 16:
        w_all = jnp.swapaxes(w_all, 0, 1).reshape(1, 4, D, packed)
    groups, rows_in = w_all.shape[0], w_all.shape[2]
    far = swap(up_bias, 2)
    near = swap(jnp.stack([up_bias, far]), 1)
    up_bias_all = jnp.stack([up_bias, near[0], far, near[1]])[ids]

    steps = jnp.arange(D // 2, dtype=F32)
    freq = jnp.exp(steps * (-2.0 * math.log(10000.0) / D))
    angle = freq[:, None] * jnp.arange(DEPTH, dtype=F32)[None, :]
    sines, cosines = jnp.sin(angle), jnp.cos(angle)
    sincos = jnp.concatenate([sines, cosines], axis=0)
    table = jnp.concatenate([cosines, sines], axis=0).astype(BF).T

    head_block = [
        pl.BlockSpec((1, SAVED, QB), lambda h, *_: (h, 0, 0)),
        pl.BlockSpec((1, 8, TREE), lambda h, *_: (h, 0, 0)),
        whole((3, TREE, COLS)),
        whole((2, COLS, TREE)),
    ]
    saved_shapes = [
        struct((2, SAVED, QB), BF),
        struct((2, 8, TREE), F32),
        struct((3, TREE, COLS), BF),
        struct((2, COLS, TREE), BF),
    ]
    forward = []
    for m in range(MB):
        forward.append(
            call(
                functools.partial(forward_kernel, m),
                (2,),
                2,
                [whole((QUARTER, D))] * 4
                + [whole((D, D)), whole((2, COLS)), whole((D, DEPTH)), whole((DEPTH, D))],
                [whole((QUARTER, COLS))] * 4 + head_block,
                [struct((QUARTER, COLS), BF)] * 4 + saved_shapes,
                [
                    pltpu.VMEM((TREE, D + COLS), BF),
                    pltpu.VMEM((COLS, TREE), BF),
                    pltpu.VMEM((COLS, TREE), BF),
                    pltpu.VMEM((D, TREE), F32),
                    pltpu.VMEM((D + COLS, QB), BF),
                    pltpu.VMEM((1024, QB), F32),
                    pltpu.VMEM((COLS, TREE), F32),
                ],
                cost(7e9, 12e6, 2e6),
            )(ids, hosts, *tokens[m], w_heads, head_bias, sincos, table)
        )

    def spread(blocks):
        return (blocks[0], *(swap(blocks[k], k) for k in (1, 2, 3)))

    outs = jnp.zeros((MB, 1, QUARTER, D), F32)
    hid = jnp.zeros((PADDED, FF), BF)
    pg = jnp.zeros((PADDED, FF), BF)
    n2 = jnp.zeros((PADDED, D), BF)
    mix = jnp.zeros((PADDED, D), BF)
    att = jnp.zeros((PADDED, D), BF)
    middle = []
    for m in range(MB):
        blocks = spread(forward[m][:4])
        third = pl.BlockSpec((1, 1, QUARTER, D), lambda t, *_: (m, 0, 0, 0))
        wide = pl.BlockSpec((QUARTER, D), lambda t, *_: (m, t))
        narrow = pl.BlockSpec((QUARTER, D), lambda t, *_: (m, 0))
        anywhere = pl.BlockSpec(memory_space=pl.ANY)
        res = call(
            middle_kernel,
            (4,),
            1,
            [whole((QUARTER, COLS))] * 4
            + [
                third,
                third,
                pl.BlockSpec((groups, 1, rows_in, 2 * D), lambda t, *_: (0, t, 0, 0)),
                pl.BlockSpec((groups, 4, rows_in, COLS), lambda t, *_: (0, 0, 0, 2 * D // COLS)),
                whole((1, D)),
                whole((1, D)),
                whole((4, D)),
                whole((1, D)),
            ]
            + [anywhere] * 6,
            [third, wide, wide, narrow, narrow, narrow, whole((QUARTER, D))]
            + [whole((QUARTER, COLS))] * 4
            + [whole((8, D)), whole((4, D))],
            [
                struct((MB, 1, QUARTER, D), F32),
                struct((PADDED, FF), BF),
                struct((PADDED, FF), BF),
                struct((PADDED, D), BF),
                struct((PADDED, D), BF),
                struct((PADDED, D), BF),
                struct((QUARTER, D), F32),
            ]
            + [struct((QUARTER, COLS), BF)] * 4
            + [struct((8, D), F32), struct((4, D), F32)],
            [
                pltpu.VMEM((QUARTER, D), F32),
                pltpu.VMEM((QUARTER, D), F32),
                pltpu.VMEM((QUARTER, 1), F32),
                pltpu.VMEM((QUARTER, D), BF),
                pltpu.VMEM((QUARTER, D), F32),
                pltpu.VMEM((QUARTER, D), F32),
            ],
            cost(4e9, 12e6, 1.3e6),
            {13 + n: n for n in range(6)},
        )(
            ids, *blocks, inputs, cotangent, w_all, w_all, gain2, bias2, up_bias_all,
            down_bias.reshape(1, D), outs, hid, pg, n2, mix, att,
        )
        outs, hid, pg, n2, mix, att = res[:6]
        middle.append(res)

    cot_rows = jnp.pad(cotangent.reshape(MB * QUARTER, D), ((0, PADDED - MB * QUARTER), (0, 0)))
    order = (1, 3, 0, 2)

    def turn(step):
        return jnp.where(step < 2, 2 * step + 1, 2 * step - 4)

    keep, send = call(
        weights_kernel,
        (4,),
        1,
        [whole((PADDED, D))] * 3
        + [pl.BlockSpec((PADDED, D), lambda s, ids: (0, ids[turn(s)]))] * 2
        + [pl.BlockSpec((PADDED, COLS), lambda s, ids: (0, ids[turn(s)]))],
        [
            pl.BlockSpec((1, D, packed), lambda s, ids: (jnp.maximum(s - 2, 0), 0, 0)),
            pl.BlockSpec((1, D, packed), lambda s, ids: (jnp.minimum(s, 1), 0, 0)),
        ],
        [struct((2, D, packed), BF)] * 2,
        [pltpu.VMEM((D, PADDED), BF)] * 3,
        cost(5e9, 17e6),
    )(ids, n2, cot_rows, mix, hid, pg, att)
    del order
    other = swap(send, 1)
    mine = keep[0].astype(F32) + other[0].astype(F32)
    away = (keep[1].astype(F32) + other[1].astype(F32)).astype(BF)
    mine = (mine + swap(away, 2).astype(F32)).astype(BF)
    parts = lax.all_to_all(mine.reshape(n_dp, rows, packed), "dp", 0, 0, tiled=True)
    g_ff = jnp.sum(parts.astype(F32), axis=0)

    acc_w = jnp.zeros((3 * COLS, D), F32)
    acc_r = jnp.zeros((D, COLS), F32)
    acc_s = jnp.zeros((8, D), F32)
    in_grad = jnp.zeros((MB, 1, QUARTER, D), F32)
    for m in range(MB):
        blocks = spread(middle[m][7:11])
        keep, send, acc_w, acc_r, acc_s = call(
            functools.partial(backward_kernel, m),
            (2,),
            2,
            [whole((QUARTER, COLS))] * 4
            + [whole((QUARTER, D))] * 4
            + [whole((D, D)), whole((D, DEPTH))]
            + head_block
            + [whole((3 * COLS, D)), whole((D, COLS)), whole((8, D))],
            [
                whole((2, QUARTER, D)),
                whole((2, QUARTER, D)),
                whole((3 * COLS, D)),
                whole((D, COLS)),
                whole((8, D)),
            ],
            [
                struct((2, QUARTER, D), BF),
                struct((2, QUARTER, D), BF),
                struct((3 * COLS, D), F32),
                struct((D, COLS), F32),
                struct((8, D), F32),
            ],
            [
                pltpu.VMEM((TREE, COLS), BF),
                pltpu.VMEM((COLS, TREE), BF),
                pltpu.VMEM((D + COLS, TREE), BF),
                pltpu.VMEM((D, TREE), F32),
                pltpu.VMEM((1024, QB), BF),
                pltpu.VMEM((TREE, COLS), F32),
                pltpu.VMEM((TREE, COLS), F32),
                pltpu.VMEM((COLS, TREE), BF),
                pltpu.VMEM((COLS, QB), F32),
                pltpu.VMEM((COLS, QB), F32),
                pltpu.VMEM((TREE, 3 * COLS), BF),
                pltpu.VMEM((TREE, D), BF),
            ],
            cost(12e9, 16e6),
        )(ids, hosts, *blocks, *tokens[m], w_heads, sincos, *forward[m][4:], acc_w, acc_r, acc_s)
        other = swap(send, 1)
        away = (keep[1].astype(F32) + other[1].astype(F32)).astype(BF)
        far = swap(away, 2)
        first = pl.BlockSpec((1, QUARTER, D), lambda i: (0, 0, 0))
        third = pl.BlockSpec((1, 1, QUARTER, D), lambda i: (m, 0, 0, 0))
        in_grad = call(
            tail_kernel,
            (1,),
            0,
            [third, whole((1, D)), whole((QUARTER, D)), first, first, whole((QUARTER, D))]
            + [pl.BlockSpec(memory_space=pl.ANY)],
            third,
            struct((MB, 1, QUARTER, D), F32),
            [],
            cost(QUARTER * D * 20, QUARTER * D * 14),
            {6: 0},
        )(inputs, gain1, middle[m][6], keep, other, far, in_grad)

    g = jnp.concatenate([acc_w.astype(BF).T, acc_r.astype(BF)], axis=1)
    parts = lax.all_to_all(g.reshape(n_dp, rows, 4 * COLS), "dp", 0, 0, tiled=True)
    g_heads = jnp.sum(parts.astype(F32), axis=0)

    n_all = n_dp * 4
    smalls = middle[0][11] + middle[1][11] + middle[2][11]
    ups = middle[0][12] + middle[1][12] + middle[2][12]
    heads = lax.dynamic_update_slice(
        jnp.zeros((2, D), F32), acc_s[2:4, 0:COLS], (jnp.int32(0), me * COLS)
    )
    vectors = jnp.concatenate([acc_s[0:2], smalls[0:3], heads], axis=0)
    vectors = vectors.reshape(7, n_all, D // n_all).transpose(1, 0, 2).reshape(n_all, -1)
    vectors = jnp.concatenate([vectors, ups.reshape(n_all, FF // n_all)], axis=1)
    summed = jnp.sum(
        lax.all_to_all(vectors[:, None], ("dp", "tensor"), 0, 0, tiled=True), axis=(0, 1)
    )
    each = D // n_all
    piece = summed[: 7 * each].reshape(7, each)
    at = (lax.axis_index("dp") * 4 + me) * each
    gain_here = lax.dynamic_slice(attention_norm_gain, (at,), (each,))
    bias_here = lax.dynamic_slice(attention_norm_bias, (at,), (each,))

    return (
        outs,
        in_grad,
        (piece[0] - bias_here * piece[1]) / gain_here,
        piece[1],
        g_heads[:, 0:COLS],
        g_heads[:, COLS : 2 * COLS],
        g_heads[:, 2 * COLS : 3 * COLS],
        g_heads[:, 3 * COLS :],
        piece[5:7],
        g_ff[:, 2 * D :].T,
        piece[2],
        piece[3],
        g_ff[:, 0:D],
        summed[7 * each :],
        g_ff[:, D : 2 * D].T,
        piece[4],
    )


def solution(mesh):
    placed = (
        P(None, "dp", "tensor", None),
        P(),
        P(),
        P("dp", "tensor"),
        P("dp", "tensor"),
        P("dp", "tensor"),
        P("dp", "tensor"),
        P(None, "tensor"),
        P("tensor", "dp"),
        P(),
        P(),
        P("dp", "tensor"),
        P("tensor"),
        P("tensor", "dp"),
        P(),
        P(None, "dp", None),
        P(None, "dp", None),
        P(None, "dp", "tensor", None),
    )
    return jax.shard_map(
        body,
        mesh=mesh,
        in_specs=placed,
        out_specs=(
            P(None, "dp", "tensor", None),
            P(None, "dp", "tensor", None),
            P(("dp", "tensor")),
            P(("dp", "tensor")),
            P("dp", "tensor"),
            P("dp", "tensor"),
            P("dp", "tensor"),
            P("dp", "tensor"),
            P(None, ("dp", "tensor")),
            P("tensor", "dp"),
            P(("dp", "tensor")),
            P(("dp", "tensor")),
            P("dp", "tensor"),
            P(("dp", "tensor")),
            P("tensor", "dp"),
            P(("dp", "tensor")),
        ),
        check_vma=False,
    )
```

```python
import functools
import math

import jax
import jax.numpy as jnp
from jax import lax
from jax.experimental import pallas as pl
from jax.experimental.pallas import tpu as pltpu
from jax.sharding import PartitionSpec as P

D = 512
HD = 64
FF = 2048
TRUNK = 512
SEG = 64
BRANCHES = 4
LEAVES = 8
MB = 3
TREE = 1280
DEPTH = 640
COLS = 128
QUARTER = 320
PACKED = 2 * D + COLS
QB = 256
EPS = 1e-05
BF = jnp.bfloat16
F32 = jnp.float32

CHUNKS = (
    ((0, "causal"),),
    ((0, None), (256, "causal")),
    ((0, None), (256, None), (512, "segment")),
    ((0, None), (256, None), (512, "host"), (768, "segment")),
    ((0, None), (256, None), (512, "host"), (1024, "segment")),
)
OFFSETS = (0, 256, 768, 1536, 2560)
SAVED = 3584


def nn(a, b):
    return lax.dot_general(a, b, (((1,), (0,)), ((), ())), preferred_element_type=F32)


def nt(a, b):
    return lax.dot_general(a, b, (((1,), (1,)), ((), ())), preferred_element_type=F32)


def key_runs(block):
    runs = []
    for n, (start, _) in enumerate(CHUNKS[block]):
        if runs and runs[-1][0] + runs[-1][1] == start:
            runs[-1][1] += 256
        else:
            runs.append([start, 256, n * 256])
    return runs


def chunk_mask(kind, block, parents, micro):
    key = lax.broadcasted_iota(jnp.int32, (256, QB), 0)
    query = lax.broadcasted_iota(jnp.int32, (256, QB), 1)
    if kind == "causal":
        return key <= query
    if kind == "segment":
        return (key <= query) & (key // SEG == query // SEG)
    lane = lax.broadcasted_iota(jnp.int32, (1, QB), 1) // SEG
    first = (block - 3) * 4
    host = jnp.zeros((1, QB), jnp.int32)
    for n in range(4):
        host = jnp.where(lane == n, parents[micro, first + n], host)
    return (key // SEG + 1) == host


def raised(parents, micro, leaf):
    return (parents[micro, leaf] > 0).astype(jnp.int32)


def last_columns(near, out_ref, parents, micro):
    last = near[...]
    turned = pltpu.roll(last, SEG, 1)
    lane = lax.broadcasted_iota(jnp.int32, (1, 128), 1)
    low = jnp.where(lane < SEG, last, turned)
    out_ref[:, TRUNK : TRUNK + 128] = low
    out_ref[:, TRUNK + 128 : TRUNK + 256] = low
    for pair in range(LEAVES // 2):
        left = raised(parents, micro, 2 * pair)
        right = raised(parents, micro, 2 * pair + 1)
        straight = jnp.where(lane < SEG, 1 - left, right)
        at = TRUNK + 256 + pair * 128
        out_ref[:, at : at + 128] = jnp.where(straight > 0, last, turned)


def norm_kernel(x_ref, gain_ref, bias_ref, first, rest):
    for n in range(MB):
        x = x_ref[n, 0].astype(F32)
        centered = x - jnp.mean(x, axis=-1, keepdims=True)
        spread = jnp.mean(centered * centered, axis=-1, keepdims=True)
        y = (centered * lax.rsqrt(spread + EPS) * gain_ref[...] + bias_ref[...]).astype(BF)
        if n == 0:
            first[...] = y
        else:
            rest[n - 1] = y


def table_kernel(fine, coarse, sincos, table):
    sf, cf = fine[0:256, :], fine[256:512, :]
    for n in range(DEPTH // 128):
        sc, cc = coarse[0:256, n : n + 1], coarse[256:512, n : n + 1]
        cols = slice(n * 128, (n + 1) * 128)
        sines = sc * cf + cc * sf
        cosines = cc * cf - sc * sf
        sincos[0:256, cols] = sines
        sincos[256:512, cols] = cosines
        table[cols, 0:256] = jnp.transpose(cosines.astype(BF))
        table[cols, 256:512] = jnp.transpose(sines.astype(BF))


def copies(sems, pairs):
    made = []
    for n, (source, target) in enumerate(pairs):
        made.append(pltpu.make_async_copy(source, target, sems.at[n]))
        made[-1].start()
    return made


def wait(made):
    for copy in made:
        copy.wait()


def weight_rows(ids, blocks, target):
    rows = blocks[0].shape[0]
    count = len(blocks)
    pairs = []
    for n, block in enumerate(blocks):
        place = (ids[4] ^ n) if count > 1 else 0
        at = pl.multiple_of(place * rows, rows) if count > 1 else 0
        pairs.append((block, target.at[pl.ds(at, rows), :]))
    return pairs


def token_rows(ids, n):
    return pl.ds(pl.multiple_of(ids[n] * QUARTER, SEG), QUARTER)


def forward_kernel(micro, blocks, aliased, ids, hosts, *refs):
    x = refs[0:4]
    wb = refs[4 : 4 + blocks]
    hb, sincos, table = refs[4 + blocks : 7 + blocks]
    refs = refs[7 + blocks + aliased :]
    att, (probs, inverse, natural, turned) = refs[0:4], refs[4:8]
    xs, w, near, kcat, vt, ct, sct, qts, scores, att_t, ps, inv, nat, trn, att_n, s_in, s_tab, s_out = refs[8:]

    x = [v if len(v.shape) == 2 else v.at[micro - 1] for v in x]
    tokens = copies(s_in, [(x[n], xs.at[n]) for n in range(4)] + weight_rows(ids, wb, w))
    pairs = [(table.at[0 : TRUNK + SEG, :], kcat.at[0 : TRUNK + SEG, 0:D])]
    for n in range(1, BRANCHES):
        at = TRUNK + n * SEG
        pairs.append((table.at[TRUNK : TRUNK + SEG, :], kcat.at[at : at + SEG, 0:D]))
    for n in range(LEAVES):
        at = TRUNK + (BRANCHES + n) * SEG
        row = pl.multiple_of(TRUNK + SEG * raised(hosts, micro, n), SEG)
        pairs.append((table.at[pl.ds(row, SEG), :], kcat.at[at : at + SEG, 0:D]))
    pairs.append((sincos.at[:, 0:TRUNK], sct.at[:, 0:TRUNK]))
    pairs.append((sincos.at[:, TRUNK:DEPTH], near))
    tables = copies(s_tab, pairs)
    wait(tokens)
    for n in range(4):
        y = nn(xs[n], w[:, 0 : 3 * COLS])
        rows = token_rows(ids, n)
        q = y[:, 0:COLS]
        nat[0, rows, :] = (q + hb[0:1, :]).astype(BF)
        nat[1, rows, :] = (q + hb[1:2, :]).astype(BF)
        kcat[rows, D : D + COLS] = y[:, COLS : 2 * COLS].astype(BF)
        nat[2, rows, :] = y[:, 2 * COLS : 3 * COLS].astype(BF)
    wait(tables)
    sent = copies(s_out, [(nat, natural)])
    last_columns(near, sct, hosts, micro)
    ct[...] = jnp.transpose(nat[0])
    trn[0] = jnp.transpose(kcat[:, D : D + COLS])
    vt[...] = jnp.transpose(nat[2])
    factor = math.log2(math.e) / math.sqrt(HD)

    def one_head(head, _):
        mine = lax.broadcasted_iota(jnp.int32, (1, COLS), 1) // HD == head
        mine_t = lax.broadcasted_iota(jnp.int32, (COLS, 1), 0) // HD == head

        def rotate(block):
            cols = slice(block * QB, (block + 1) * QB)
            qt = qts.at[block]
            position = jnp.where(mine, nat[1, cols, :], 0)
            relative = nt(w[:, 3 * COLS : 4 * COLS], position)
            rs, rc = relative[0:256], relative[256:512]
            sines, cosines = sct[0:256, cols], sct[256:512, cols]
            qt[0:256, :] = (rs * sines + rc * cosines).astype(BF)
            qt[256:512, :] = (rc * sines - rs * cosines).astype(BF)
            qt[512:640, :] = jnp.where(mine_t, ct[:, cols], 0)

        def score(block, n):
            start, kind = CHUNKS[block][n]
            s = nn(kcat[start : start + 256, :], qts[block])
            if kind is not None:
                s = jnp.where(chunk_mask(kind, block, hosts, micro), s, -1e30)
            scores[block % 2, n * 256 : (n + 1) * 256, :] = s
            return jnp.max(s, axis=0, keepdims=True)

        def grow(block, n, peak):
            e = jnp.exp2((scores[block % 2, n * 256 : (n + 1) * 256, :] - peak) * factor)
            row = OFFSETS[block] + n * 256
            ps[head, row : row + 256, :] = e.astype(BF)
            return jnp.sum(e, axis=0, keepdims=True)

        def finish(block, total):
            cols = slice(block * QB, (block + 1) * QB)
            out = None
            for start, keys, row in key_runs(block):
                row = OFFSETS[block] + row
                term = nn(vt[:, start : start + keys], ps[head, row : row + keys, :])
                out = term if out is None else out + term
            over = 1.0 / total
            inv[head, :, cols] = jnp.broadcast_to(over, (8, QB))
            att_t[:, cols] = jnp.where(mine_t, out * over, att_t[:, cols])

        order = (4, 3, 2, 1, 0)
        rotate(order[0])
        peak = None
        for n in range(len(CHUNKS[order[0]])):
            high = score(order[0], n)
            peak = high if peak is None else jnp.maximum(peak, high)
        rotate(order[1])
        for at, block in enumerate(order):
            after = order[at + 1] if at < 4 else None
            count = len(CHUNKS[block])
            ahead = len(CHUNKS[after]) if after is not None else 0
            total, high = None, None
            for n in range(max(count, ahead)):
                if n < ahead:
                    top = score(after, n)
                    high = top if high is None else jnp.maximum(high, top)
                if n < count:
                    part = grow(block, n, peak)
                    total = part if total is None else total + part
            if at < 3:
                rotate(order[at + 2])
            finish(block, total)
            peak = high
        return 0

    lax.fori_loop(0, 2, one_head, 0)
    full = att_t[...].astype(BF)
    trn[1] = full
    att_n[...] = jnp.transpose(full)
    targets = [a if len(a.shape) == 2 else a.at[micro - 1] for a in att]
    wait(sent)
    wait(
        copies(
            s_out,
            [(att_n.at[token_rows(ids, n), :], targets[n]) for n in range(4)]
            + [(ps, probs), (inv, inverse), (trn, turned)],
        )
    )


def middle_kernel(ids, *refs):
    a, refs = refs[0:8], refs[8:]
    (
        x, cot, w, gain, bias, down_bias,
        out, hid, pg, n2_out, mix_out, att_out, mgrad,
    ) = refs[:13]
    g, (small, ubg, a_s, mid, n2, ffn, n2g, sems) = refs[13:21], refs[21:]
    m = pl.program_id(0)
    groups, rows = w.shape[0], w.shape[2]

    def part(t, first, last):
        return w[:, t, :, first:last].reshape(D, last - first)

    @pl.when(m == 0)
    def _():
        wait(
            copies(
                sems,
                [(a[n], a_s.at[0, n]) for n in range(4)]
                + [(a[4 + n].at[k], a_s.at[1 + k, n]) for n in range(4) for k in range(MB - 1)],
            )
        )

    total = x[0, 0].astype(F32)
    later = jnp.maximum(m - 1, 0)
    for n in range(4):
        block = a_s[m, n]
        total = total + nt(block, part(ids[n], 2 * D, 2 * D + COLS))
        att_out[:, pl.ds(pl.multiple_of(ids[n] * COLS, COLS), COLS)] = block
    centered = total - jnp.mean(total, axis=-1, keepdims=True)
    spread = jnp.mean(centered * centered, axis=-1, keepdims=True)
    inv = lax.rsqrt(spread + EPS)
    mid[...] = total
    n2[...] = (centered * inv * gain[...] + bias[...]).astype(BF)
    n2_out[...] = n2[...]

    @pl.when(m == 0)
    def _():
        small[...] = jnp.zeros_like(small)
        ubg[...] = jnp.zeros_like(ubg)

    ahead = None
    for t in range(5):
        if t < 4:
            up, down = part(t, 0, D), part(t, D, 2 * D)
            extra = jnp.transpose(part(t, 2 * D + COLS, 2 * D + 2 * COLS))
            up_bias = extra[0:1, :].astype(F32) + extra[1:2, :].astype(F32)
            now = (nn(n2[...], up) + up_bias, nn(cot[0, 0], down))
        if t > 0:
            pre, hg = ahead
            cols = slice((t - 1) * D, t * D)
            cdf = 0.5 * (1.0 + lax.erf(pre * 0.7071067811865476))
            hid[:, cols] = (pre * cdf).astype(BF)
            slope = cdf + pre * jnp.exp(-0.5 * pre * pre) * 0.3989422804014327
            p = (hg * slope).astype(BF)
            pg[:, cols] = p
            ubg[t - 1 : t, :] += jnp.sum(p.astype(F32), axis=0, keepdims=True)
            up, down = part(t - 1, 0, D), part(t - 1, D, 2 * D)
            f, b = nt(hid[:, cols], down), nt(pg[:, cols], up)
            if t == 1:
                ffn[...] = f
                n2g[...] = b
            else:
                ffn[...] += f
                n2g[...] += b
        if t < 4:
            ahead = now

    out[0, 0] = mid[...] + ffn[...] + down_bias[...]
    gr = n2g[...]
    total = mid[...]
    centered = total - jnp.mean(total, axis=-1, keepdims=True)
    inv = lax.rsqrt(jnp.mean(centered * centered, axis=-1, keepdims=True) + EPS)
    xh = centered * inv
    c = cot[0, 0].astype(F32)
    small[0:1, :] += jnp.sum(gr * xh, axis=0, keepdims=True)
    small[1:2, :] += jnp.sum(gr, axis=0, keepdims=True)
    small[2:3, :] += jnp.sum(c, axis=0, keepdims=True)
    e = gr * gain[...]
    mg = c + inv * (
        e - jnp.mean(e, axis=-1, keepdims=True) - xh * jnp.mean(e * xh, axis=-1, keepdims=True)
    )
    mgrad[0] = mg
    mixed = mg.astype(BF)
    mix_out[...] = mixed
    for n in range(4):
        block = nn(mixed, part(ids[n], 2 * D, 2 * D + COLS)).astype(BF)

        @pl.when(m == 0)
        def _():
            g[n][...] = block

        @pl.when(m > 0)
        def _():
            g[4 + n][later] = block


def weights_kernel(ids, n2, cot, mix, hid, pg, att, send, keep, n2t, cott, mixt):
    step = pl.program_id(0)

    @pl.when(step == 0)
    def _():
        n2t[...] = jnp.transpose(n2[...])
        cott[...] = jnp.transpose(cot[...].reshape(MB * QUARTER, D))
        mixt[...] = jnp.transpose(mix[...])

    def write(ref):
        ref[0, :, 0:D] = nn(n2t[...], pg[...]).astype(BF)
        ref[0, :, D : 2 * D] = nn(cott[...], hid[...]).astype(BF)
        ref[0, :, 2 * D :] = nn(mixt[...], att[...]).astype(BF)

    @pl.when(step < 2)
    def _():
        write(send)

    @pl.when(step >= 2)
    def _():
        write(keep)


def backward_kernel(micro, blocks, ids, hosts, *refs):
    d, x, wb = refs[0:4], refs[4:8], refs[8 : 8 + blocks]
    sincos, probs, inverse, natural, turned = refs[8 + blocks : 13 + blocks]
    refs = refs[13 + blocks :]
    acc, acc_s = refs[0:2] if micro else (None, None)
    refs = refs[2 if micro else 0 :]
    keep, send, out_s = refs[0:3]
    last = micro == MB - 1
    out_g = refs[3]
    (
        do, xs, w, near, ps, inv, nat, trn, dot, kcat_t, sct, ds, dqs, dk, dv, dq_t, hc, hp,
        dall, xall, gw, dns, s_in, s_probs, s_x, s_out,
    ) = refs[4:]

    grads = [v if len(v.shape) == 2 else v.at[micro - 1] for v in d]
    x = [v if len(v.shape) == 2 else v.at[micro - 1] for v in x]
    first = copies(
        s_in,
        [(grads[n], do.at[token_rows(ids, n), :]) for n in range(4)]
        + [(inverse, inv), (natural, nat), (turned, trn)]
        + weight_rows(ids, wb, w)
        + [(sincos.at[:, 0:TRUNK], sct.at[:, 0:TRUNK]), (sincos.at[:, TRUNK:DEPTH], near)],
    )
    order = (4, 3, 2, 1, 0)
    chunks = [(0, block) for block in order] + [(1, block) for block in order]
    loads = []
    for n, (head, block) in enumerate(chunks):
        rows = pl.ds(OFFSETS[block], 256 * len(CHUNKS[block]))
        loads.append(
            pltpu.make_async_copy(probs.at[head, rows, :], ps.at[head, rows, :], s_probs.at[n])
        )
        loads[-1].start()
    tokens = copies(
        s_x,
        [(x[n], xall.at[token_rows(ids, n), :]) for n in range(4)] + ([(acc, gw)] if micro else []),
    )
    dk[...] = jnp.zeros_like(dk)
    dv[...] = jnp.zeros_like(dv)
    hc[...] = jnp.zeros_like(hc)
    hp[...] = jnp.zeros_like(hp)
    wait(first)
    dot[...] = jnp.transpose(do[...])
    last_columns(near, sct, hosts, micro)
    kcat_t[0:256, :] = sct[256:512, :].astype(BF)
    kcat_t[256:512, :] = sct[0:256, :].astype(BF)
    kcat_t[512:640, :] = trn[0]
    wait(tokens)
    if not micro:
        gw[...] = jnp.zeros_like(gw)
    factor = 1.0 / math.sqrt(HD)

    def one_head(head, _):
        mine = lax.broadcasted_iota(jnp.int32, (1, COLS), 1) // HD == head
        mine_t = lax.broadcasted_iota(jnp.int32, (COLS, 1), 0) // HD == head

        def begin(block):
            cols = slice(block * QB, (block + 1) * QB)
            over = inv[head, 0:1, cols]
            grad = jnp.where(mine_t, dot[:, cols].astype(F32), 0.0) * over
            delta = jnp.sum(grad * trn[1, :, cols].astype(F32), axis=0, keepdims=True)
            grad_t = grad.astype(BF)
            content = jnp.where(mine, nat[0, cols, :], 0)
            return grad_t, jnp.transpose(grad_t), delta, content

        def chunk(block, n, state):
            grad_t, grad_n, delta, content = state
            row = OFFSETS[block] + n * 256
            keys = slice(CHUNKS[block][n][0], CHUNKS[block][n][0] + 256)
            p = ps[head, row : row + 256, :]
            dp = nn(nat[2, keys, :], grad_t)
            s = (p.astype(F32) * (dp - delta)).astype(BF)
            ds[block % 2, n * 256 : (n + 1) * 256, :] = s
            dv[keys, :] += nn(p, grad_n)
            dk[keys, :] += nn(s, content)

        def back(block):
            dq = None
            for start, keys, row in key_runs(block):
                term = nn(kcat_t[:, start : start + keys], ds[block % 2, row : row + keys, :])
                dq = term if dq is None else dq + term
            dqs[block % 2] = dq * factor

        def turn(block):
            cols = slice(block * QB, (block + 1) * QB)
            s1, s2 = dqs[block % 2, 0:256, :], dqs[block % 2, 256:512, :]
            sines, cosines = sct[0:256, cols], sct[256:512, cols]
            relative = jnp.concatenate(
                [(s1 * sines - s2 * cosines).astype(BF), (s1 * cosines + s2 * sines).astype(BF)],
                axis=0,
            )
            pgrad = lax.dot_general(
                w[:, 3 * COLS : 4 * COLS],
                relative,
                (((0,), (0,)), ((), ())),
                preferred_element_type=F32,
            )
            position = jnp.where(mine, nat[1, cols, :], 0)
            gw[:, 3 * COLS :] += nn(relative, position)
            pgrad = jnp.where(mine_t, pgrad, 0.0)
            cgrad = jnp.where(mine_t, dqs[block % 2, 512:640, :], 0.0)
            hp[...] += pgrad
            hc[...] += cgrad
            dq_t[:, cols] = jnp.where(mine_t, (pgrad + cgrad).astype(BF), dq_t[:, cols])

        for at, block in enumerate(order):
            pltpu.make_async_copy(
                probs.at[head, pl.ds(OFFSETS[block], 256 * len(CHUNKS[block])), :],
                ps.at[head, pl.ds(OFFSETS[block], 256 * len(CHUNKS[block])), :],
                s_probs.at[head * 5 + at],
            ).wait()
            state = begin(block)
            for n in range(len(CHUNKS[block])):
                chunk(block, n, state)
                if n == 0 and at > 0:
                    turn(order[at - 1])
            back(block)
        turn(order[-1])
        return 0

    lax.fori_loop(0, 2, one_head, 0)
    dall[:, 0:COLS] = jnp.transpose(dq_t[...])
    dall[:, COLS : 2 * COLS] = (dk[...] * factor).astype(BF)
    dall[:, 2 * COLS :] = dv[...].astype(BF)
    before = acc_s[...] if micro else jnp.zeros((8, D), F32)
    gain_sum = before[0:1, :]
    shift_sum = before[1:2, :]
    sent = []
    for n, target in ((1, send.at[0]), (3, send.at[1]), (0, keep.at[0]), (2, keep.at[1])):
        rows = token_rows(ids, n)
        g = nt(dall[rows, :], w[:, 0 : 3 * COLS])
        dns[n] = g.astype(BF)
        sent.append(pltpu.make_async_copy(dns.at[n], target, s_out.at[n]))
        sent[-1].start()
        gain_sum = gain_sum + jnp.sum(g * xall[rows, :].astype(F32), axis=0, keepdims=True)
        shift_sum = shift_sum + jnp.sum(g, axis=0, keepdims=True)
    gw[:, 0 : 3 * COLS] += lax.dot_general(
        xall[...], dall[...], (((0,), (0,)), ((), ())), preferred_element_type=F32
    )
    out_s[...] = jnp.zeros_like(out_s)
    out_s[0:1, :] = gain_sum
    out_s[1:2, :] = shift_sum
    for n, h in enumerate((hc, hp)):
        v = jnp.transpose(h[:, 0:128] + h[:, 128:256])
        v = jnp.sum(v, axis=0, keepdims=True)
        out_s[2 + n : 3 + n, 0:COLS] = before[2 + n : 3 + n, 0:COLS] + v
    if last:
        xs[...] = gw[...].astype(BF)
    sent.append(pltpu.make_async_copy(xs if last else gw, out_g, s_out.at[4]))
    sent[-1].start()
    wait(sent)


def tail_kernel(micro, gain, x, mgrad, own, near, far, *refs):
    out, xs, ms, gs, result, sems = refs[-6:]
    made = copies(
        sems,
        [
            (x.at[micro, 0], xs),
            (mgrad.at[micro], ms),
            (own.at[0], gs.at[0]),
            (near.at[0], gs.at[1]),
            (far, gs.at[2]),
        ],
    )
    wait(made)
    g = gs[0].astype(F32) + gs[1].astype(F32) + gs[2].astype(F32)
    xf = xs[...].astype(F32)
    centered = xf - jnp.mean(xf, axis=-1, keepdims=True)
    spread = jnp.mean(centered * centered, axis=-1, keepdims=True)
    inv = lax.rsqrt(spread + EPS)
    xh = centered * inv
    e = g * gain[...]
    result[...] = ms[...] + inv * (
        e - jnp.mean(e, axis=-1, keepdims=True) - xh * jnp.mean(e * xh, axis=-1, keepdims=True)
    )
    wait(copies(sems, [(result, out.at[micro, 0])]))


def whole(shape):
    return pl.BlockSpec(shape, lambda i, *_: (0,) * len(shape))


def cost(flops, nbytes, trans=0):
    return pl.CostEstimate(flops=int(flops), bytes_accessed=int(nbytes), transcendentals=int(trans))


def struct(shape, dtype):
    return jax.ShapeDtypeStruct(shape, dtype)


def call(
    kernel, prefetch, in_specs, out_specs, out_shape, scratch, estimate, *, grid=(), alias=None,
    after=(),
):
    first, last = prefetch + len(in_specs), prefetch + len(in_specs) + len(after)

    def run(*refs):
        kernel(*refs[:first], *refs[last:])

    made = pl.pallas_call(
        run,
        out_shape=out_shape,
        grid_spec=pltpu.PrefetchScalarGridSpec(
            num_scalar_prefetch=prefetch,
            grid=grid,
            in_specs=list(in_specs) + [pl.BlockSpec(memory_space=pl.ANY)] * len(after),
            out_specs=out_specs,
            scratch_shapes=scratch,
        ),
        input_output_aliases=alias or {},
        cost_estimate=estimate,
        compiler_params=pltpu.CompilerParams(
            dimension_semantics=("arbitrary",) * len(grid), vmem_limit_bytes=56 << 20
        ),
    )
    return lambda *operands: made(*operands, *after)


ANY = pl.BlockSpec(memory_space=pl.ANY)


def dma(count):
    return pltpu.SemaphoreType.DMA((count,))


SAVED_SHAPES = [
    ((2, SAVED, QB), BF),
    ((2, 8, TREE), F32),
    ((3, TREE, COLS), BF),
    ((2, COLS, TREE), BF),
]


def of_tree(array, m):
    return array[min(m, 1)]


def attention_forward(m, ids, hosts, tokens, w_heads, head_bias, sincos, table, att, after=()):
    shape = (QUARTER, COLS) if m == 0 else (MB - 1, QUARTER, COLS)
    count = len(w_heads)
    return call(
        functools.partial(forward_kernel, m, count, len(att)),
        2,
        [ANY] * (4 + count)
        + [pl.BlockSpec(memory_space=pltpu.VMEM), ANY, ANY]
        + [ANY] * len(att),
        [ANY] * 8,
        [struct(shape, BF)] * 4 + [struct(*v) for v in SAVED_SHAPES],
        [
            pltpu.VMEM((4, QUARTER, D), BF),
            pltpu.VMEM((D, D), BF),
            pltpu.VMEM((D, 128), F32),
            pltpu.VMEM((TREE, D + COLS), BF),
            pltpu.VMEM((COLS, TREE), BF),
            pltpu.VMEM((COLS, TREE), BF),
            pltpu.VMEM((D, TREE), F32),
            pltpu.VMEM((5, D + COLS, QB), BF),
            pltpu.VMEM((2, 1024, QB), F32),
            pltpu.VMEM((COLS, TREE), F32),
            *[pltpu.VMEM(*v) for v in SAVED_SHAPES],
            pltpu.VMEM((TREE, COLS), BF),
            dma(4 + count),
            dma(BRANCHES + LEAVES + 2),
            dma(7),
        ],
        cost(15e9, 12e6, 2e6),
        alias={9 + count + n: n for n in range(len(att))},
        after=after,
    )(ids, hosts, *tokens, *w_heads, head_bias, sincos, table, *att)


def middle_part(ids, blocks, inputs, cotangent, w_all, gain, bias, down_bias):
    third = pl.BlockSpec((1, 1, QUARTER, D), lambda m, *_: (m, 0, 0, 0))
    wide = pl.BlockSpec((QUARTER, FF), lambda m, *_: (m, 0))
    narrow = pl.BlockSpec((QUARTER, D), lambda m, *_: (m, 0))
    small = [(QUARTER, COLS)] * 4 + [(MB - 1, QUARTER, COLS)] * 4
    return call(
        middle_kernel,
        1,
        [ANY] * 8
        + [
            third,
            third,
            pl.BlockSpec(w_all.shape, lambda m, *_: (0,) * 4, pipeline_mode=pl.Buffered(1)),
            whole((1, D)),
            whole((1, D)),
            whole((1, D)),
        ],
        [third, wide, wide, narrow, narrow, narrow]
        + [pl.BlockSpec((1, QUARTER, D), lambda m, *_: (m, 0, 0))]
        + [whole(v) for v in small]
        + [whole((8, D)), whole((4, D))],
        [
            struct((MB, 1, QUARTER, D), F32),
            struct((MB * QUARTER, FF), BF),
            struct((MB * QUARTER, FF), BF),
            struct((MB * QUARTER, D), BF),
            struct((MB * QUARTER, D), BF),
            struct((MB * QUARTER, D), BF),
            struct((MB, QUARTER, D), F32),
        ]
        + [struct(v, BF) for v in small]
        + [struct((8, D), F32), struct((4, D), F32)],
        [
            pltpu.VMEM((MB, 4, QUARTER, COLS), BF),
            pltpu.VMEM((QUARTER, D), F32),
            pltpu.VMEM((QUARTER, D), BF),
            pltpu.VMEM((QUARTER, D), F32),
            pltpu.VMEM((QUARTER, D), F32),
            dma(4 * MB),
        ],
        cost(24e9, 36e6, 4e6),
        grid=(MB,),
    )(ids, *blocks, inputs, cotangent, w_all, gain, bias, down_bias.reshape(1, D))


def weight_products(ids, n2, cot, mix, hid, pg, att):
    tall = MB * QUARTER

    def turn(s, ids):
        return (0, ids[jnp.where(s < 2, 2 * s + 1, 2 * s - 4)])

    return call(
        weights_kernel,
        1,
        [whole((tall, D)), whole(cot.shape), whole((tall, D))]
        + [pl.BlockSpec((tall, D), turn)] * 2
        + [pl.BlockSpec((tall, COLS), turn)],
        [
            pl.BlockSpec((1, D, PACKED), lambda s, ids: (jnp.minimum(s, 1), 0, 0)),
            pl.BlockSpec((1, D, PACKED), lambda s, ids: (jnp.maximum(s - 2, 0), 0, 0)),
        ],
        [struct((2, D, PACKED), BF)] * 2,
        [pltpu.VMEM((D, tall), BF)] * 3,
        cost(12e9, 17e6),
        grid=(4,),
    )(ids, n2, cot, mix, hid, pg, att)


def attention_backward(m, ids, hosts, blocks, tokens, w_heads, sincos, saved, sums, after=()):
    count = len(w_heads)
    last = m == MB - 1
    outs = [struct((D, D), BF if last else F32)]
    return call(
        functools.partial(backward_kernel, m, count),
        2,
        [ANY] * (13 + count) + ([ANY, whole((8, D))] if sums else []),
        [ANY, ANY, whole((8, D))] + [ANY] * len(outs),
        [struct((2, QUARTER, D), BF)] * 2 + [struct((8, D), F32)] + outs,
        [
            pltpu.VMEM((TREE, COLS), BF),
            pltpu.VMEM((D, D), BF),
            pltpu.VMEM((D, D), BF),
            pltpu.VMEM((D, 128), F32),
            *[pltpu.VMEM(*v) for v in SAVED_SHAPES],
            pltpu.VMEM((COLS, TREE), BF),
            pltpu.VMEM((D + COLS, TREE), BF),
            pltpu.VMEM((D, TREE), F32),
            pltpu.VMEM((2, 1024, QB), BF),
            pltpu.VMEM((2, D + COLS, QB), F32),
            pltpu.VMEM((TREE, COLS), F32),
            pltpu.VMEM((TREE, COLS), F32),
            pltpu.VMEM((COLS, TREE), BF),
            pltpu.VMEM((COLS, QB), F32),
            pltpu.VMEM((COLS, QB), F32),
            pltpu.VMEM((TREE, 3 * COLS), BF),
            pltpu.VMEM((TREE, D), BF),
            pltpu.VMEM((D, D), F32),
            pltpu.VMEM((4, QUARTER, D), BF),
            dma(9 + count),
            dma(10),
            dma(5),
            dma(5),
        ],
        cost(20e9, 16e6),
        after=after,
    )(ids, hosts, *blocks, *tokens, *w_heads, sincos, *saved, *sums)


def input_gradient(m, gain, inputs, mgrad, keep, other, far, in_grad, after=()):
    return call(
        functools.partial(tail_kernel, m),
        0,
        [pl.BlockSpec(memory_space=pltpu.VMEM)] + [ANY] * (5 + len(in_grad)),
        [ANY],
        [struct((MB, 1, QUARTER, D), F32)],
        [
            pltpu.VMEM((QUARTER, D), BF),
            pltpu.VMEM((QUARTER, D), F32),
            pltpu.VMEM((3, QUARTER, D), BF),
            pltpu.VMEM((QUARTER, D), F32),
            dma(5),
        ],
        cost(QUARTER * D * 20, QUARTER * D * 14),
        alias={6: 0} if in_grad else {},
        after=after,
    )(gain, inputs, mgrad, keep, other, far, *in_grad)


def swap(value, bits):
    return lax.ppermute(value, "tensor", [(n, n ^ bits) for n in range(4)])


def dp_swap(value, bits):
    return lax.ppermute(value, "dp", [(n, n ^ bits) for n in range(lax.axis_size("dp"))])


def gathered(shard):
    n_dp = lax.axis_size("dp")
    both = jnp.broadcast_to(shard[None], (n_dp, *shard.shape))
    return lax.all_to_all(both, "dp", 0, 0, tiled=True).reshape(-1, shard.shape[1])


def ordered(value, *others):
    return lax.optimization_barrier((value, *others))[0]


def summed_everywhere(value):
    for bit in (1, 2):
        value = value + swap(value, bit)
    bit = 1
    while bit < lax.axis_size("dp"):
        value = value + dp_swap(value, bit)
        bit *= 2
    return value


def body(
    inputs,
    attention_norm_gain,
    attention_norm_bias,
    query_weight,
    key_weight,
    value_weight,
    relative_weight,
    head_bias,
    output_weight,
    feedforward_norm_gain,
    feedforward_norm_bias,
    up_weight,
    up_bias,
    down_weight,
    down_bias,
    parents,
    positions,
    cotangent,
):
    del positions
    n_dp = lax.axis_size("dp")
    rows = query_weight.shape[0]
    me = lax.axis_index("tensor").astype(jnp.int32)
    place = lax.axis_index("dp").astype(jnp.int32)
    ids = jnp.where(jnp.arange(8) < 4, me ^ jnp.arange(8, dtype=jnp.int32), place)
    hosts = parents.reshape(MB, LEAVES)
    gain1 = attention_norm_gain.reshape(1, D)

    shard = jnp.concatenate([query_weight, key_weight, value_weight, relative_weight], axis=1)
    w_heads = (gathered(shard),)

    normed = call(
        norm_kernel,
        0,
        [whole((MB, 1, QUARTER, D)), whole((1, D)), whole((1, D))],
        [whole((QUARTER, D)), whole((MB - 1, QUARTER, D))],
        [struct((QUARTER, D), BF), struct((MB - 1, QUARTER, D), BF)],
        [],
        cost(MB * QUARTER * D * 10, MB * QUARTER * D * 4),
        grid=(1,),
    )(inputs, gain1, attention_norm_bias.reshape(1, D))
    first_far, rest_far = (swap(v, 2) for v in normed)
    first_tokens = (normed[0], swap(normed[0], 1), first_far, swap(first_far, 1))

    here = lax.dynamic_slice(up_bias, (place * rows,), (rows,))
    high = here.astype(BF)
    low = (here - high.astype(F32)).astype(BF)
    shard = jnp.concatenate(
        [
            up_weight,
            down_weight.T,
            output_weight.T,
            jnp.pad(jnp.stack([high, low], axis=1), ((0, 0), (0, COLS - 2))),
        ],
        axis=1,
    )
    w_all = lax.all_gather(shard, ("dp", "tensor"), axis=0, tiled=False)
    w_all = w_all.reshape(n_dp, 4, rows, PACKED + COLS)
    if rows % 16:
        w_all = jnp.swapaxes(w_all, 0, 1).reshape(1, 4, D, PACKED + COLS)

    freq = jnp.exp(jnp.arange(D // 2, dtype=F32) * (-2.0 * math.log(10000.0) / D))[:, None]
    fine = freq * jnp.arange(128, dtype=F32)
    coarse = freq * (128.0 * jnp.arange(8, dtype=F32))
    sincos, table = call(
        table_kernel,
        0,
        [whole((D, 128)), whole((D, 8))],
        [whole((D, DEPTH)), whole((DEPTH, D))],
        [struct((D, DEPTH), F32), struct((DEPTH, D), BF)],
        [],
        cost(D * DEPTH * 20, D * DEPTH * 6),
        grid=(1,),
    )(
        jnp.concatenate([jnp.sin(fine), jnp.cos(fine)]),
        jnp.concatenate([jnp.sin(coarse), jnp.cos(coarse)]),
    )

    forward = []
    att = ()
    tokens = (first_tokens,)
    for m in range(MB):
        if m == 1:
            rest_far = ordered(rest_far, forward[0][0])
            tokens += ((normed[1], swap(normed[1], 1), rest_far, swap(rest_far, 1)),)
        forward.append(
            attention_forward(
                m, ids, hosts, of_tree(tokens, m), w_heads, head_bias, sincos, table, att
            )
        )
        if m > 0:
            att = forward[m][:4]

    def spread(blocks):
        return [blocks[0], *(swap(blocks[k], k) for k in (1, 2, 3))]

    middle = middle_part(
        ids, spread(forward[0][:4]) + spread(att), inputs, cotangent, w_all,
        feedforward_norm_gain.reshape(1, D), feedforward_norm_bias.reshape(1, D), down_bias,
    )
    out, hid, pg, n2, mix, attended, mgrad = middle[:7]
    grads = (spread(middle[7:11]), spread(middle[11:15]))
    smalls, ups = middle[15:]

    send, keep = weight_products(ids, n2, cotangent, mix, hid, pg, attended)
    other = swap(send, 1)
    half = n_dp // 2
    cut = 640
    low_bit = place & 1

    def pick(value, axis, index):
        return lax.dynamic_index_in_dim(value, index, axis, keepdims=False)

    def plus(a, b):
        return (a.astype(F32) + b.astype(F32)).astype(BF)

    both = plus(keep, other)
    first = both[..., :cut]
    second = both[..., cut:].reshape(2, half, 2, rows, PACKED - cut)
    first_away, second_away = first[1], pick(second, 2, 1 - low_bit)
    stage1 = (first_away, second_away)
    first = plus(first[0], swap(first_away, 2)).reshape(half, 2, rows, cut)
    second = plus(pick(second, 2, low_bit), dp_swap(second_away, 1))
    first_away, second_away = pick(first, 1, 1 - low_bit), second[1]
    stage2 = (first_away, second_away)
    first = plus(pick(first, 1, low_bit), dp_swap(first_away, 1))
    second = plus(second[0], swap(second_away, 2))
    third = jnp.concatenate([first, second], axis=-1)

    sums = ()
    in_grad = ()
    after = [(), stage1, stage2]
    kept = []
    for m in range(MB):
        keep, send, *sums = attention_backward(
            m, ids, hosts, of_tree(grads, m), of_tree(tokens, m), w_heads, sincos,
            forward[m][4:], tuple(sums)[::-1], after[m],
        )
        other = swap(send, 1)
        away = plus(keep[1], other[1])
        if m == 0:
            after[2] += (away,)
        kept.append((keep, other, swap(away, 2)))
    acc_s, g_heads = sums
    for m in range(MB):
        wait_for = (away,) if m < MB - 1 else ()
        in_grad = input_gradient(m, gain1, inputs, mgrad, *kept[m], in_grad, wait_for)

    g_heads = ordered(g_heads, third).reshape(n_dp, rows, D)
    g_heads = jnp.sum(lax.all_to_all(g_heads, "dp", 0, 0, tiled=True).astype(F32), axis=0)
    g_ff = pick(third, 0, place >> 1).astype(F32)
    others = [dp_swap(pick(third, 0, (place >> 1) ^ k), 2 * k) for k in range(1, half)]
    others = ordered(others, g_heads)
    for v in others:
        g_ff = g_ff + v.astype(F32)

    n_all = n_dp * 4
    heads = lax.dynamic_update_slice(
        jnp.zeros((2, D), F32), acc_s[2:4, 0:COLS], (jnp.int32(0), me * COLS)
    )
    vectors = jnp.concatenate([acc_s[0:2], smalls[0:3], heads, ups], axis=0)
    vectors = summed_everywhere(ordered(vectors, away))
    each = D // n_all
    at = (place * 4 + me) * each
    piece = lax.dynamic_slice(vectors, (0, at), (7, each))
    ups = lax.dynamic_slice(vectors[7:].reshape(FF), (4 * at,), (4 * each,))
    gain_here = lax.dynamic_slice(attention_norm_gain, (at,), (each,))
    bias_here = lax.dynamic_slice(attention_norm_bias, (at,), (each,))

    return (
        out,
        in_grad[0],
        (piece[0] - bias_here * piece[1]) / gain_here,
        piece[1],
        g_heads[:, 0:COLS],
        g_heads[:, COLS : 2 * COLS],
        g_heads[:, 2 * COLS : 3 * COLS],
        g_heads[:, 3 * COLS :],
        piece[5:7],
        g_ff[:, 2 * D :].T,
        piece[2],
        piece[3],
        g_ff[:, 0:D],
        ups,
        g_ff[:, D : 2 * D].T,
        piece[4],
    )


def solution(mesh):
    placed = (
        P(None, "dp", "tensor", None),
        P(),
        P(),
        P("dp", "tensor"),
        P("dp", "tensor"),
        P("dp", "tensor"),
        P("dp", "tensor"),
        P(None, "tensor"),
        P("tensor", "dp"),
        P(),
        P(),
        P("dp", "tensor"),
        P("tensor"),
        P("tensor", "dp"),
        P(),
        P(None, "dp", None),
        P(None, "dp", None),
        P(None, "dp", "tensor", None),
    )
    return jax.shard_map(
        body,
        mesh=mesh,
        in_specs=placed,
        out_specs=(
            P(None, "dp", "tensor", None),
            P(None, "dp", "tensor", None),
            P(("dp", "tensor")),
            P(("dp", "tensor")),
            P("dp", "tensor"),
            P("dp", "tensor"),
            P("dp", "tensor"),
            P("dp", "tensor"),
            P(None, ("dp", "tensor")),
            P("tensor", "dp"),
            P(("dp", "tensor")),
            P(("dp", "tensor")),
            P("dp", "tensor"),
            P(("dp", "tensor")),
            P("tensor", "dp"),
            P(("dp", "tensor")),
        ),
        check_vma=False,
    )
```

```python
import functools
import math

import jax
import jax.numpy as jnp
from jax import lax
from jax.experimental import pallas as pl
from jax.experimental.pallas import tpu as pltpu
from jax.sharding import PartitionSpec as P

D = 512
HD = 64
FF = 2048
TRUNK = 512
SEG = 64
BRANCHES = 4
LEAVES = 8
MB = 3
TREE = 1280
DEPTH = 640
COLS = 128
QUARTER = 320
PACKED = 2 * D + COLS
QB = 256
EPS = 1e-05
BF = jnp.bfloat16
F32 = jnp.float32

CHUNKS = (
    ((0, "causal"),),
    ((0, None), (256, "causal")),
    ((0, None), (256, None), (512, "segment")),
    ((0, None), (256, None), (512, "host"), (768, "segment")),
    ((0, None), (256, None), (512, "host"), (1024, "segment")),
)
OFFSETS = (0, 256, 768, 1536, 2560)
SAVED = 3584


def nn(a, b):
    return lax.dot_general(a, b, (((1,), (0,)), ((), ())), preferred_element_type=F32)


def nt(a, b):
    return lax.dot_general(a, b, (((1,), (1,)), ((), ())), preferred_element_type=F32)


def key_runs(block):
    runs = []
    for n, (start, _) in enumerate(CHUNKS[block]):
        if runs and runs[-1][0] + runs[-1][1] == start:
            runs[-1][1] += 256
        else:
            runs.append([start, 256, n * 256])
    return runs


def chunk_mask(kind, block, parents, micro):
    key = lax.broadcasted_iota(jnp.int32, (256, QB), 0)
    query = lax.broadcasted_iota(jnp.int32, (256, QB), 1)
    if kind == "causal":
        return key <= query
    if kind == "segment":
        return (key <= query) & (key // SEG == query // SEG)
    lane = lax.broadcasted_iota(jnp.int32, (1, QB), 1) // SEG
    first = (block - 3) * 4
    host = jnp.zeros((1, QB), jnp.int32)
    for n in range(4):
        host = jnp.where(lane == n, parents[micro, first + n], host)
    return (key // SEG + 1) == host


def raised(parents, micro, leaf):
    return (parents[micro, leaf] > 0).astype(jnp.int32)


def last_columns(near, out_ref, parents, micro):
    last = near[...]
    turned = pltpu.roll(last, SEG, 1)
    lane = lax.broadcasted_iota(jnp.int32, (1, 128), 1)
    low = jnp.where(lane < SEG, last, turned)
    out_ref[:, TRUNK : TRUNK + 128] = low
    out_ref[:, TRUNK + 128 : TRUNK + 256] = low
    for pair in range(LEAVES // 2):
        left = raised(parents, micro, 2 * pair)
        right = raised(parents, micro, 2 * pair + 1)
        straight = jnp.where(lane < SEG, 1 - left, right)
        at = TRUNK + 256 + pair * 128
        out_ref[:, at : at + 128] = jnp.where(straight > 0, last, turned)


def prepare_kernel(
    where, x_ref, gain_ref, bias_ref, q, k, v, r, up, down_t, out_t, up_bias, first, rest, heads, ff
):
    for n in range(MB):
        x = x_ref[n, 0].astype(F32)
        centered = x - jnp.mean(x, axis=-1, keepdims=True)
        spread = jnp.mean(centered * centered, axis=-1, keepdims=True)
        y = (centered * lax.rsqrt(spread + EPS) * gain_ref[...] + bias_ref[...]).astype(BF)
        if n == 0:
            first[...] = y
        else:
            rest[n - 1] = y
    for n in range(heads.shape[0]):
        for at, part in enumerate((q, k, v, r)):
            heads[n, :, at * COLS : (at + 1) * COLS] = part[...]
    rows = up.shape[0]
    ff[:, 0:D] = up[...]
    ff[:, D : 2 * D] = down_t[...]
    ff[:, 2 * D : PACKED] = out_t[...]
    at = where[4] * rows
    line = pltpu.roll(jnp.broadcast_to(up_bias[...], (8, D)), jnp.where(at > 0, D - at, 0), 1)
    column = jnp.transpose(jnp.broadcast_to(line[0:1, 0:128], (128, 128)))[0:rows]
    high = column.astype(BF).astype(F32)
    lane = lax.broadcasted_iota(jnp.int32, (rows, COLS), 1)
    ff[:, PACKED:] = jnp.where(lane == 0, high, column - high).astype(BF)


def table_kernel(fine, coarse, sincos, table):
    sf, cf = fine[0:256, :], fine[256:512, :]
    for n in range(DEPTH // 128):
        sc, cc = coarse[0:256, n : n + 1], coarse[256:512, n : n + 1]
        cols = slice(n * 128, (n + 1) * 128)
        sines = sc * cf + cc * sf
        cosines = cc * cf - sc * sf
        sincos[0:256, cols] = sines
        sincos[256:512, cols] = cosines
        table[cols, 0:256] = jnp.transpose(cosines.astype(BF))
        table[cols, 256:512] = jnp.transpose(sines.astype(BF))


def copies(sems, pairs):
    made = []
    for n, (source, target) in enumerate(pairs):
        made.append(pltpu.make_async_copy(source, target, sems.at[n]))
        made[-1].start()
    return made


def wait(made):
    for copy in made:
        copy.wait()


def weight_rows(ids, blocks, target):
    rows = blocks[0].shape[0]
    count = len(blocks)
    pairs = []
    for n, block in enumerate(blocks):
        place = (ids[4] ^ n) if count > 1 else 0
        at = pl.multiple_of(place * rows, rows) if count > 1 else 0
        pairs.append((block, target.at[pl.ds(at, rows), :]))
    return pairs


def token_rows(ids, n):
    return pl.ds(pl.multiple_of(ids[n] * QUARTER, SEG), QUARTER)


def forward_kernel(micro, blocks, ids, hosts, *refs):
    x = refs[0:4]
    wb = refs[4 : 4 + blocks]
    hb, sincos, table = refs[4 + blocks : 7 + blocks]
    refs = refs[7 + blocks :]
    att, (probs, inverse, natural, turned) = refs[0:4], refs[4:8]
    xs, w, near, kcat, vt, ct, sct, qts, scores, att_t, ps, inv, nat, trn, att_n, s_in, s_tab, s_out, s_probs = refs[8:]

    x = [v if len(v.shape) == 2 else v.at[micro - 1] for v in x]
    tokens = copies(s_in, [(x[n], xs.at[n]) for n in range(4)] + weight_rows(ids, wb, w))
    pairs = [(table.at[0 : TRUNK + SEG, :], kcat.at[0 : TRUNK + SEG, 0:D])]
    for n in range(1, BRANCHES):
        at = TRUNK + n * SEG
        pairs.append((table.at[TRUNK : TRUNK + SEG, :], kcat.at[at : at + SEG, 0:D]))
    for n in range(LEAVES):
        at = TRUNK + (BRANCHES + n) * SEG
        row = pl.multiple_of(TRUNK + SEG * raised(hosts, micro, n), SEG)
        pairs.append((table.at[pl.ds(row, SEG), :], kcat.at[at : at + SEG, 0:D]))
    pairs.append((sincos.at[:, 0:TRUNK], sct.at[:, 0:TRUNK]))
    pairs.append((sincos.at[:, TRUNK:DEPTH], near))
    wait(tokens[4:])
    for n in range(4):
        tokens[n].wait()
        if n == 1:
            tables = copies(s_tab, pairs)
        y = nn(xs[n], w[:, 0 : 3 * COLS])
        rows = token_rows(ids, n)
        q = y[:, 0:COLS]
        nat[0, rows, :] = (q + hb[0:1, :]).astype(BF)
        nat[1, rows, :] = (q + hb[1:2, :]).astype(BF)
        kcat[rows, D : D + COLS] = y[:, COLS : 2 * COLS].astype(BF)
        nat[2, rows, :] = y[:, 2 * COLS : 3 * COLS].astype(BF)
    ct[...] = jnp.transpose(nat[0])
    trn[0] = jnp.transpose(kcat[:, D : D + COLS])
    vt[...] = jnp.transpose(nat[2])
    sent = copies(s_out, [(nat, natural), (trn.at[0], turned.at[0])])
    wait(tables)
    last_columns(near, sct, hosts, micro)
    factor = math.log2(math.e) / math.sqrt(HD)

    order = (4, 3, 2, 1, 0)

    def saved(head, at):
        rows = pl.ds(OFFSETS[order[at]], 256 * len(CHUNKS[order[at]]))
        return pltpu.make_async_copy(
            ps.at[head, rows, :], probs.at[head, rows, :], s_probs.at[head * 5 + at]
        )

    def one_head(head, _):
        mine = lax.broadcasted_iota(jnp.int32, (1, COLS), 1) // HD == head
        mine_t = lax.broadcasted_iota(jnp.int32, (COLS, 1), 0) // HD == head

        def rotate(block):
            cols = slice(block * QB, (block + 1) * QB)
            qt = qts.at[block]
            position = jnp.where(mine, nat[1, cols, :], 0)
            relative = nt(w[:, 3 * COLS : 4 * COLS], position)
            rs, rc = relative[0:256], relative[256:512]
            sines, cosines = sct[0:256, cols], sct[256:512, cols]
            qt[0:256, :] = (rs * sines + rc * cosines).astype(BF)
            qt[256:512, :] = (rc * sines - rs * cosines).astype(BF)
            qt[512:640, :] = jnp.where(mine_t, ct[:, cols], 0)

        def score(block, n):
            start, kind = CHUNKS[block][n]
            s = nn(kcat[start : start + 256, :], qts[block])
            if kind is not None:
                s = jnp.where(chunk_mask(kind, block, hosts, micro), s, -1e30)
            scores[block % 2, n * 256 : (n + 1) * 256, :] = s
            return jnp.max(s, axis=0, keepdims=True)

        def grow(block, n, peak):
            e = jnp.exp2((scores[block % 2, n * 256 : (n + 1) * 256, :] - peak) * factor)
            row = OFFSETS[block] + n * 256
            ps[head, row : row + 256, :] = e.astype(BF)
            return jnp.sum(e, axis=0, keepdims=True)

        def finish(block, total):
            cols = slice(block * QB, (block + 1) * QB)
            out = None
            for start, keys, row in key_runs(block):
                row = OFFSETS[block] + row
                term = nn(vt[:, start : start + keys], ps[head, row : row + keys, :])
                out = term if out is None else out + term
            over = 1.0 / total
            inv[head, :, cols] = jnp.broadcast_to(over, (8, QB))
            att_t[:, cols] = jnp.where(mine_t, out * over, att_t[:, cols])

        rotate(order[0])
        peak = None
        for n in range(len(CHUNKS[order[0]])):
            high = score(order[0], n)
            peak = high if peak is None else jnp.maximum(peak, high)
        rotate(order[1])
        for at, block in enumerate(order):
            after = order[at + 1] if at < 4 else None
            count = len(CHUNKS[block])
            ahead = len(CHUNKS[after]) if after is not None else 0
            total, high = None, None
            for n in range(max(count, ahead)):
                if n < ahead:
                    top = score(after, n)
                    high = top if high is None else jnp.maximum(high, top)
                if n < count:
                    part = grow(block, n, peak)
                    total = part if total is None else total + part
            if at < 3:
                rotate(order[at + 2])
            finish(block, total)
            saved(head, at).start()
            peak = high
        return 0

    lax.fori_loop(0, 2, one_head, 0)
    wait(sent)
    full = att_t[...].astype(BF)
    trn[1] = full
    att_n[...] = jnp.transpose(full)
    sent = copies(
        s_out,
        [(att_n.at[token_rows(ids, n), :], att[n]) for n in range(4)]
        + [(inv, inverse), (trn.at[1], turned.at[1])],
    )
    for head in range(2):
        for at in range(5):
            saved(head, at).wait()
    wait(sent)


def middle_kernel(ids, *refs):
    a, refs = refs[0 : 4 * MB], refs[4 * MB :]
    (
        x, cot, w, gain, bias, down_bias,
        out, hid, pg, n2_out, mix_out, att_out, mgrad,
    ) = refs[:13]
    g, (small, a_s, mid, n2, ffn, n2g, sems) = refs[13:21], refs[21:]
    m = pl.program_id(0)
    groups, rows = w.shape[0], w.shape[2]

    def part(t, first, last):
        return w[:, t, :, first:last].reshape(D, last - first)

    @pl.when(m == 0)
    def _():
        wait(
            copies(
                sems,
                [(a[4 * k + n], a_s.at[k, n]) for k in range(MB) for n in range(4)],
            )
        )

    total = x[0, 0].astype(F32)
    later = jnp.maximum(m - 1, 0)
    for n in range(4):
        block = a_s[m, n]
        total = total + nt(block, part(ids[n], 2 * D, 2 * D + COLS))
        att_out[:, pl.ds(pl.multiple_of(ids[n] * COLS, COLS), COLS)] = block
    centered = total - jnp.mean(total, axis=-1, keepdims=True)
    spread = jnp.mean(centered * centered, axis=-1, keepdims=True)
    inv = lax.rsqrt(spread + EPS)
    mid[...] = total
    n2[...] = (centered * inv * gain[...] + bias[...]).astype(BF)
    n2_out[...] = n2[...]

    @pl.when(m == 0)
    def _():
        small[...] = jnp.zeros_like(small)

    ahead = None
    for t in range(5):
        if t < 4:
            up, down = part(t, 0, D), part(t, D, 2 * D)
            extra = jnp.transpose(part(t, 2 * D + COLS, 2 * D + 2 * COLS))
            up_bias = extra[0:1, :].astype(F32) + extra[1:2, :].astype(F32)
            now = (nn(n2[...], up) + up_bias, nn(cot[0, 0], down))
        if t > 0:
            pre, hg = ahead
            cols = slice((t - 1) * D, t * D)
            cdf = 0.5 * (1.0 + lax.erf(pre * 0.7071067811865476))
            hid[:, cols] = (pre * cdf).astype(BF)
            slope = cdf + pre * jnp.exp(-0.5 * pre * pre) * 0.3989422804014327
            p = (hg * slope).astype(BF)
            pg[:, cols] = p
            small[7 + t : 8 + t, :] += jnp.sum(p.astype(F32), axis=0, keepdims=True)
            up, down = part(t - 1, 0, D), part(t - 1, D, 2 * D)
            f, b = nt(hid[:, cols], down), nt(pg[:, cols], up)
            if t == 1:
                ffn[...] = f
                n2g[...] = b
            else:
                ffn[...] += f
                n2g[...] += b
        if t < 4:
            ahead = now

    out[0, 0] = mid[...] + ffn[...] + down_bias[...]
    gr = n2g[...]
    total = mid[...]
    centered = total - jnp.mean(total, axis=-1, keepdims=True)
    inv = lax.rsqrt(jnp.mean(centered * centered, axis=-1, keepdims=True) + EPS)
    xh = centered * inv
    c = cot[0, 0].astype(F32)
    small[4:5, :] += jnp.sum(gr * xh, axis=0, keepdims=True)
    small[5:6, :] += jnp.sum(gr, axis=0, keepdims=True)
    small[6:7, :] += jnp.sum(c, axis=0, keepdims=True)
    e = gr * gain[...]
    mg = c + inv * (
        e - jnp.mean(e, axis=-1, keepdims=True) - xh * jnp.mean(e * xh, axis=-1, keepdims=True)
    )
    mgrad[0] = mg
    mixed = mg.astype(BF)
    mix_out[...] = mixed
    for n in range(4):
        block = nn(mixed, part(ids[n], 2 * D, 2 * D + COLS)).astype(BF)

        @pl.when(m == 0)
        def _():
            g[n][...] = block

        @pl.when(m > 0)
        def _():
            g[4 + n][later] = block


def weights_kernel(ids, n2, cot, mix, hid, pg, att, send, keep, n2t, cott, mixt):
    step = pl.program_id(0)

    @pl.when(step == 0)
    def _():
        n2t[...] = jnp.transpose(n2[...])
        cott[...] = jnp.transpose(cot[...].reshape(MB * QUARTER, D))
        mixt[...] = jnp.transpose(mix[...])

    def write(ref):
        ref[0, :, 0:D] = nn(n2t[...], pg[...]).astype(BF)
        ref[0, :, D : 2 * D] = nn(cott[...], hid[...]).astype(BF)
        ref[0, :, 2 * D :] = nn(mixt[...], att[...]).astype(BF)

    @pl.when(step < 2)
    def _():
        write(send)

    @pl.when(step >= 2)
    def _():
        write(keep)


def backward_kernel(micro, blocks, ids, hosts, *refs):
    d, x, wb = refs[0:4], refs[4:8], refs[8 : 8 + blocks]
    sincos, probs, inverse, natural, turned = refs[8 + blocks : 13 + blocks]
    refs = refs[13 + blocks :]
    last = micro == MB - 1
    before, acc = refs[0], refs[1] if micro else None
    refs = refs[2 if micro else 1 :]
    if last:
        dall_out, out_s, out_g = refs[0:3]
        refs = refs[3:]
    else:
        keep, send, out_s, out_g = refs[0:4]
        refs = refs[4:]
    (
        do, w, near, ps, inv, nat, trn, dot, kcat_t, sct, ds, dqs, dk, dv, dq_t, hc, hp,
        dall, wrt, rel, cg, grel, xall, gw, result, dps, s_in, s_probs, s_x, s_out,
    ) = refs

    grads = [v if len(v.shape) == 2 else v.at[micro - 1] for v in d]
    x = [v if len(v.shape) == 2 else v.at[micro - 1] for v in x]
    first = copies(
        s_in,
        [(grads[n], do.at[token_rows(ids, n), :]) for n in range(4)]
        + [(turned, trn), (inverse, inv), (sincos.at[:, TRUNK:DEPTH], near)]
        + [(sincos.at[:, 0:TRUNK], sct.at[:, 0:TRUNK]), (natural, nat)]
        + weight_rows(ids, wb, w),
    )
    order = (4, 3, 2, 1, 0)
    dk[...] = jnp.zeros_like(dk)
    dv[...] = jnp.zeros_like(dv)
    hc[...] = jnp.zeros_like(hc)
    hp[...] = jnp.zeros_like(hp)
    wait(first[:6])
    chunks = [(0, block) for block in order] + [(1, block) for block in order]
    for n, (head, block) in enumerate(chunks):
        rows = pl.ds(OFFSETS[block], 256 * len(CHUNKS[block]))
        pltpu.make_async_copy(
            probs.at[head, rows, :], ps.at[head, rows, :], s_probs.at[n]
        ).start()
    tokens = copies(s_x, token_pairs(ids, x, xall) + ([(acc, gw)] if micro else []))
    dot[...] = jnp.transpose(do[...])
    kcat_t[512:640, :] = trn[0]
    wait(first[6:8])
    last_columns(near, sct, hosts, micro)
    kcat_t[0:256, :] = sct[256:512, :].astype(BF)
    kcat_t[256:512, :] = sct[0:256, :].astype(BF)
    wait(first[8:])
    wrt[...] = jnp.transpose(w[:, 3 * COLS : 4 * COLS])
    factor = 1.0 / math.sqrt(HD)

    def one_head(head, _):
        mine = lax.broadcasted_iota(jnp.int32, (1, COLS), 1) // HD == head
        mine_t = lax.broadcasted_iota(jnp.int32, (COLS, 1), 0) // HD == head

        def begin(block):
            cols = slice(block * QB, (block + 1) * QB)
            over = inv[head, 0:1, cols]
            grad = jnp.where(mine_t, dot[:, cols].astype(F32), 0.0) * (over * factor)
            delta = jnp.sum(grad * trn[1, :, cols].astype(F32), axis=0, keepdims=True)
            grad_t = grad.astype(BF)
            content = jnp.where(mine, nat[0, cols, :], 0)
            return grad_t, jnp.transpose(grad_t), delta, content

        def gain(block, n, state, slot):
            start = CHUNKS[block][n][0]
            dps[slot] = nn(nat[2, start : start + 256, :], state[0]) - state[2]

        def weigh(block, n, slot):
            row = OFFSETS[block] + n * 256
            p = ps[head, row : row + 256, :].astype(F32)
            ds[block, n * 256 : (n + 1) * 256, :] = (p * dps[slot]).astype(BF)

        def spend(block, n, state):
            row = OFFSETS[block] + n * 256
            keys = slice(CHUNKS[block][n][0], CHUNKS[block][n][0] + 256)
            dv[keys, :] += nn(ps[head, row : row + 256, :], state[1])
            dk[keys, :] += nn(ds[block, n * 256 : (n + 1) * 256, :], state[3])

        def back(block, first, last):
            dq = None
            for start, keys, row in key_runs(block):
                term = nn(
                    kcat_t[first:last, start : start + keys], ds[block, row : row + keys, :]
                )
                dq = term if dq is None else dq + term
            if first < D:
                dqs[block, first:last, :] = dq
            else:
                cg[:, block * QB : (block + 1) * QB] = dq

        def turn(block, first, last):
            cols = slice(block * QB, (block + 1) * QB)
            s1, s2 = dqs[block, first:last, :], dqs[block, 256 + first : 256 + last, :]
            sines, cosines = sct[first:last, cols], sct[256 + first : 256 + last, cols]
            rel[first:last, cols] = (s1 * sines - s2 * cosines).astype(BF)
            rel[256 + first : 256 + last, cols] = (s1 * cosines + s2 * sines).astype(BF)

        items = [(block, n) for block in order for n in range(len(CHUNKS[block]))]
        states = {}
        todo = []
        for i in range(len(items) + 2):
            for task in todo[:2]:
                task()
            todo = todo[2:]
            if i < len(items):
                block, n = items[i]
                if n == 0:
                    at = order.index(block)
                    rows = pl.ds(OFFSETS[block], 256 * len(CHUNKS[block]))
                    pltpu.make_async_copy(
                        probs.at[head, rows, :], ps.at[head, rows, :], s_probs.at[head * 5 + at]
                    ).wait()
                    states[block] = begin(block)
                gain(block, n, states[block], i % 3)
            if 0 <= i - 1 < len(items):
                weigh(*items[i - 1], (i - 1) % 3)
            if i >= 2:
                block, n = items[i - 2]
                spend(block, n, states[block])
                if n + 1 == len(CHUNKS[block]):
                    for cut in (0, 128):
                        todo.append(functools.partial(back, block, cut, cut + 128))
                        todo.append(functools.partial(back, block, 256 + cut, 384 + cut))
                    todo.append(functools.partial(back, block, D, D + COLS))
                    for cut in (0, 128):
                        todo.append(functools.partial(turn, block, cut, cut + 128))
        for task in todo:
            task()
        position = jnp.where(mine, nat[1], 0)
        grel[...] = grel[...] + nn(rel[...], position)
        pgrad = jnp.where(mine_t, nn(wrt[...], rel[...]), 0.0)
        cgrad = jnp.where(mine_t, cg[...], 0.0)
        for n in range(TREE // 128):
            hp[...] += pgrad[:, n * 128 : (n + 1) * 128]
            hc[...] += cgrad[:, n * 128 : (n + 1) * 128]
        dq_t[...] = jnp.where(mine_t, (pgrad + cgrad).astype(BF), dq_t[...])
        return 0

    grel[...] = jnp.zeros_like(grel)
    lax.fori_loop(0, 2, one_head, 0)
    dall[:, 0:COLS] = jnp.transpose(dq_t[...])
    dall[:, COLS : 2 * COLS] = dk[...].astype(BF)
    dall[:, 2 * COLS :] = (dv[...] * math.sqrt(HD)).astype(BF)
    wait(tokens)
    sent = []
    if last:
        sent += copies(s_in, [(dall, dall_out)])
    if not micro:
        gw[...] = jnp.zeros_like(gw)
    new = lax.dot_general(
        xall[...], dall[...], (((0,), (0,)), ((), ())), preferred_element_type=F32
    )
    gw[:, 0 : 3 * COLS] += new
    gw[:, 3 * COLS :] += grel[...]
    if last:
        result[...] = gw[...].astype(BF)
    sent += copies(s_x, [(result if last else gw, out_g)])
    if not last:
        sent += token_grads(ids, dall, w, result, keep, send, s_out)

    columns = jnp.sum(dall[...].astype(F32), axis=0, keepdims=True)
    scaled, plain = None, None
    for n in range(3):
        cols = slice(n * COLS, (n + 1) * COLS)
        weight = w[:, cols].astype(F32)
        one, two = new[:, cols] * weight, columns[:, cols] * weight
        scaled = one if scaled is None else scaled + one
        plain = two if plain is None else plain + two
    out_s[...] = before[...]
    for n, v in enumerate((scaled, plain)):
        v = jnp.sum(jnp.transpose(v), axis=0, keepdims=True)
        out_s[n : n + 1, :] = before[n : n + 1, :] + v
    lanes = pl.ds(pl.multiple_of(ids[0] * COLS, COLS), COLS)
    for n, h in enumerate((hc, hp)):
        v = jnp.sum(jnp.transpose(h[...]), axis=0, keepdims=True)
        out_s[2 + n : 3 + n, lanes] = before[2 + n : 3 + n, lanes] + v
    wait(sent)


def token_pairs(ids, x, target):
    return [(x[n], target.at[token_rows(ids, n), :]) for n in range(4)]


def token_grads(ids, dall, w, dns, keep, send, sems):
    sent = []
    for n, target in ((1, send.at[0]), (3, send.at[1]), (0, keep.at[0]), (2, keep.at[1])):
        dns[n] = nt(dall[token_rows(ids, n), :], w[:, 0 : 3 * COLS]).astype(BF)
        sent.append(pltpu.make_async_copy(dns.at[n], target, sems.at[n]))
        sent[-1].start()
    return sent


def token_grads_kernel(blocks, ids, *refs):
    dall_in, wb = refs[0], refs[1 : 1 + blocks]
    keep, send, dall, w, dns, s_in, s_out = refs[1 + blocks :]
    wait(copies(s_in, weight_rows(ids, wb, w) + [(dall_in, dall)]))
    wait(token_grads(ids, dall, w, dns, keep, send, s_out))


def tail_kernel(gain, x, mgrad, *refs):
    parts, (out, xs, ms, gs, result, sems) = refs[:-6], refs[-6:]
    made = []
    for m in range(MB):
        own, near, far = parts[3 * m : 3 * m + 3]
        made.append(
            copies(
                sems.at[m],
                [
                    (x.at[m, 0], xs.at[m]),
                    (mgrad.at[m], ms.at[m]),
                    (own.at[0], gs.at[m, 0]),
                    (near.at[0], gs.at[m, 1]),
                    (far, gs.at[m, 2]),
                ],
            )
        )
    sent = []
    for m in range(MB):
        wait(made[m])
        g = gs[m, 0].astype(F32) + gs[m, 1].astype(F32) + gs[m, 2].astype(F32)
        xf = xs[m].astype(F32)
        centered = xf - jnp.mean(xf, axis=-1, keepdims=True)
        spread = jnp.mean(centered * centered, axis=-1, keepdims=True)
        inv = lax.rsqrt(spread + EPS)
        xh = centered * inv
        e = g * gain[...]
        result[m] = ms[m] + inv * (
            e
            - jnp.mean(e, axis=-1, keepdims=True)
            - xh * jnp.mean(e * xh, axis=-1, keepdims=True)
        )
        sent += copies(sems.at[MB + m], [(result.at[m], out.at[m, 0])])
    wait(sent)


def final_kernel(where, parts, vectors, gain, bias, *refs):
    ff, (gq, gk, gv, gr, up, down, out, mg, ms, heads, fg, fs, upb, downb) = refs[:-14], refs[-14:]
    total = parts[0].astype(F32)
    for n in range(1, parts.shape[0]):
        total = total + parts[n].astype(F32)
    for n, ref in enumerate((gq, gk, gv, gr)):
        ref[...] = total[:, n * COLS : (n + 1) * COLS]
    total = ff[0][...].astype(F32)
    for v in ff[1:]:
        total = total + v[...].astype(F32)
    up[...] = total[:, 0:D]
    down[...] = total[:, D : 2 * D]
    out[...] = total[:, 2 * D :]
    each = mg.shape[1]

    at = where[0] * each
    rows = pltpu.roll(vectors[0:8, :], jnp.where(at > 0, D - at, 0), 1)
    scale = pltpu.roll(jnp.broadcast_to(gain[...], (8, D)), jnp.where(at > 0, D - at, 0), 1)
    shift = pltpu.roll(jnp.broadcast_to(bias[...], (8, D)), jnp.where(at > 0, D - at, 0), 1)
    first = (rows[0:1] - shift[0:1] * rows[1:2]) / scale[0:1]
    mg[...] = first[:, 0:each]
    ms[...] = rows[1:2, 0:each]
    heads[...] = rows[2:4, 0:each]
    fg[...] = rows[4:5, 0:each]
    fs[...] = rows[5:6, 0:each]
    downb[...] = rows[6:7, 0:each]
    start = where[0] * (4 * each)
    line = jnp.broadcast_to(vectors[pl.ds(8 + start // D, 1), :], (8, D))
    at = start % D
    upb[...] = pltpu.roll(line, jnp.where(at > 0, D - at, 0), 1)[0:1, 0 : 4 * each]


def whole(shape):
    return pl.BlockSpec(shape, lambda i, *_: (0,) * len(shape))


def cost(flops, nbytes, trans=0):
    return pl.CostEstimate(flops=int(flops), bytes_accessed=int(nbytes), transcendentals=int(trans))


def struct(shape, dtype):
    return jax.ShapeDtypeStruct(shape, dtype)


def call(
    kernel, prefetch, in_specs, out_specs, out_shape, scratch, estimate, *, grid=(), alias=None,
    after=(),
):
    first, last = prefetch + len(in_specs), prefetch + len(in_specs) + len(after)

    def run(*refs):
        kernel(*refs[:first], *refs[last:])

    made = pl.pallas_call(
        run,
        out_shape=out_shape,
        grid_spec=pltpu.PrefetchScalarGridSpec(
            num_scalar_prefetch=prefetch,
            grid=grid,
            in_specs=list(in_specs) + [pl.BlockSpec(memory_space=pl.ANY)] * len(after),
            out_specs=out_specs,
            scratch_shapes=scratch,
        ),
        input_output_aliases=alias or {},
        cost_estimate=estimate,
        compiler_params=pltpu.CompilerParams(
            dimension_semantics=("arbitrary",) * len(grid), vmem_limit_bytes=56 << 20
        ),
    )
    return lambda *operands: made(*operands, *after)


ANY = pl.BlockSpec(memory_space=pl.ANY)


def dma(count):
    return pltpu.SemaphoreType.DMA((count,))


SAVED_SHAPES = [
    ((2, SAVED, QB), BF),
    ((2, 8, TREE), F32),
    ((3, TREE, COLS), BF),
    ((2, COLS, TREE), BF),
]


def of_tree(array, m):
    return array[min(m, 1)]


def attention_forward(m, ids, hosts, tokens, w_heads, head_bias, sincos, table, after=()):
    count = len(w_heads)
    return call(
        functools.partial(forward_kernel, m, count),
        2,
        [ANY] * (4 + count)
        + [pl.BlockSpec(memory_space=pltpu.VMEM), ANY, ANY],
        [ANY] * 8,
        [struct((QUARTER, COLS), BF)] * 4 + [struct(*v) for v in SAVED_SHAPES],
        [
            pltpu.VMEM((4, QUARTER, D), BF),
            pltpu.VMEM((D, D), BF),
            pltpu.VMEM((D, 128), F32),
            pltpu.VMEM((TREE, D + COLS), BF),
            pltpu.VMEM((COLS, TREE), BF),
            pltpu.VMEM((COLS, TREE), BF),
            pltpu.VMEM((D, TREE), F32),
            pltpu.VMEM((5, D + COLS, QB), BF),
            pltpu.VMEM((2, 1024, QB), F32),
            pltpu.VMEM((COLS, TREE), F32),
            *[pltpu.VMEM(*v) for v in SAVED_SHAPES],
            pltpu.VMEM((TREE, COLS), BF),
            dma(4 + count),
            dma(BRANCHES + LEAVES + 2),
            dma(6),
            dma(10),
        ],
        cost(15e9, 12e6, 2e6),
        after=after,
    )(ids, hosts, *tokens, *w_heads, head_bias, sincos, table)


def middle_part(ids, blocks, inputs, cotangent, w_all, gain, bias, down_bias):
    third = pl.BlockSpec((1, 1, QUARTER, D), lambda m, *_: (m, 0, 0, 0))
    wide = pl.BlockSpec((QUARTER, FF), lambda m, *_: (m, 0))
    narrow = pl.BlockSpec((QUARTER, D), lambda m, *_: (m, 0))
    small = [(QUARTER, COLS)] * 4 + [(MB - 1, QUARTER, COLS)] * 4
    return call(
        middle_kernel,
        1,
        [ANY] * (4 * MB)
        + [
            third,
            third,
            pl.BlockSpec(w_all.shape, lambda m, *_: (0,) * 4, pipeline_mode=pl.Buffered(1)),
            whole((1, D)),
            whole((1, D)),
            whole((1, D)),
        ],
        [third, wide, wide, narrow, narrow, narrow]
        + [pl.BlockSpec((1, QUARTER, D), lambda m, *_: (m, 0, 0))]
        + [whole(v) for v in small]
        + [whole((16, D))],
        [
            struct((MB, 1, QUARTER, D), F32),
            struct((MB * QUARTER, FF), BF),
            struct((MB * QUARTER, FF), BF),
            struct((MB * QUARTER, D), BF),
            struct((MB * QUARTER, D), BF),
            struct((MB * QUARTER, D), BF),
            struct((MB, QUARTER, D), F32),
        ]
        + [struct(v, BF) for v in small]
        + [struct((16, D), F32)],
        [
            pltpu.VMEM((MB, 4, QUARTER, COLS), BF),
            pltpu.VMEM((QUARTER, D), F32),
            pltpu.VMEM((QUARTER, D), BF),
            pltpu.VMEM((QUARTER, D), F32),
            pltpu.VMEM((QUARTER, D), F32),
            dma(4 * MB),
        ],
        cost(24e9, 36e6, 4e6),
        grid=(MB,),
    )(ids, *blocks, inputs, cotangent, w_all, gain, bias, down_bias.reshape(1, D))


def weight_products(ids, n2, cot, mix, hid, pg, att):
    tall = MB * QUARTER

    def turn(s, ids):
        return (0, ids[jnp.where(s < 2, 2 * s + 1, 2 * s - 4)])

    return call(
        weights_kernel,
        1,
        [whole((tall, D)), whole(cot.shape), whole((tall, D))]
        + [pl.BlockSpec((tall, D), turn)] * 2
        + [pl.BlockSpec((tall, COLS), turn)],
        [
            pl.BlockSpec((1, D, PACKED), lambda s, ids: (jnp.minimum(s, 1), 0, 0)),
            pl.BlockSpec((1, D, PACKED), lambda s, ids: (jnp.maximum(s - 2, 0), 0, 0)),
        ],
        [struct((2, D, PACKED), BF)] * 2,
        [pltpu.VMEM((D, tall), BF)] * 3,
        cost(12e9, 17e6),
        grid=(4,),
    )(ids, n2, cot, mix, hid, pg, att)


def attention_backward(m, ids, hosts, blocks, tokens, w_heads, sincos, saved, sums, after=()):
    count = len(w_heads)
    last = m == MB - 1
    vmem = pl.BlockSpec(memory_space=pltpu.VMEM)
    if last:
        first = [struct((TREE, 3 * COLS), BF)]
    else:
        first = [struct((2, QUARTER, D), BF)] * 2
    return call(
        functools.partial(backward_kernel, m, count),
        2,
        [ANY] * (13 + count) + [vmem, ANY][: len(sums)],
        [ANY] * len(first) + [vmem, ANY],
        first + [struct((16, D), F32), struct((D, D), BF if last else F32)],
        [
            pltpu.VMEM((TREE, COLS), BF),
            pltpu.VMEM((D, D), BF),
            pltpu.VMEM((D, 128), F32),
            *[pltpu.VMEM(*v) for v in SAVED_SHAPES],
            pltpu.VMEM((COLS, TREE), BF),
            pltpu.VMEM((D + COLS, TREE), BF),
            pltpu.VMEM((D, TREE), F32),
            pltpu.VMEM((5, 1024, QB), BF),
            pltpu.VMEM((5, D, QB), F32),
            pltpu.VMEM((TREE, COLS), F32),
            pltpu.VMEM((TREE, COLS), F32),
            pltpu.VMEM((COLS, TREE), BF),
            pltpu.VMEM((COLS, 128), F32),
            pltpu.VMEM((COLS, 128), F32),
            pltpu.VMEM((TREE, 3 * COLS), BF),
            pltpu.VMEM((COLS, D), BF),
            pltpu.VMEM((D, TREE), BF),
            pltpu.VMEM((COLS, TREE), F32),
            pltpu.VMEM((D, COLS), F32),
            pltpu.VMEM((TREE, D), BF),
            pltpu.VMEM((D, D), F32),
            pltpu.VMEM((D, D) if last else (4, QUARTER, D), BF),
            pltpu.VMEM((3, 256, QB), F32),
            dma(9 + count),
            dma(10),
            dma(5),
            dma(4),
        ],
        cost(20e9, 16e6),
        after=after,
    )(ids, hosts, *blocks, *tokens, *w_heads, sincos, *saved, *sums)


def token_gradients(ids, dall, w_heads, after=()):
    count = len(w_heads)
    return call(
        functools.partial(token_grads_kernel, count),
        1,
        [ANY] * (1 + count),
        [ANY, ANY],
        [struct((2, QUARTER, D), BF)] * 2,
        [
            pltpu.VMEM((TREE, 3 * COLS), BF),
            pltpu.VMEM((D, D), BF),
            pltpu.VMEM((4, QUARTER, D), BF),
            dma(1 + count),
            dma(4),
        ],
        cost(4e9, 8e6),
        after=after,
    )(ids, dall, *w_heads)


def input_gradient(gain, inputs, mgrad, kept, after=()):
    return call(
        tail_kernel,
        0,
        [pl.BlockSpec(memory_space=pltpu.VMEM)] + [ANY] * (2 + 3 * MB),
        ANY,
        struct((MB, 1, QUARTER, D), F32),
        [
            pltpu.VMEM((MB, QUARTER, D), BF),
            pltpu.VMEM((MB, QUARTER, D), F32),
            pltpu.VMEM((MB, 3, QUARTER, D), BF),
            pltpu.VMEM((MB, QUARTER, D), F32),
            pltpu.SemaphoreType.DMA((2 * MB, 5)),
        ],
        cost(MB * QUARTER * D * 20, MB * QUARTER * D * 14),
        after=after,
    )(gain, inputs, mgrad, *kept)


def final_sums(where, parts, vectors, gain, bias, ff, after=()):
    rows = ff[0].shape[0]
    each = D * rows // (4 * D)
    vmem = pl.BlockSpec(memory_space=pltpu.VMEM)
    shapes = (
        [(rows, COLS)] * 4
        + [(rows, D), (rows, D), (rows, COLS), (1, each), (1, each), (2, each)]
        + [(1, each), (1, each), (1, 4 * each), (1, each)]
    )
    return call(
        final_kernel,
        1,
        [vmem] * (4 + len(ff)),
        [vmem] * len(shapes),
        [struct(v, F32) for v in shapes],
        [],
        cost(1e6, 4e6),
        after=after,
    )(where, parts, vectors, gain, bias, *ff)


def swap(value, bits):
    return lax.ppermute(value, "tensor", [(n, n ^ bits) for n in range(4)])


def dp_swap(value, bits):
    return lax.ppermute(value, "dp", [(n, n ^ bits) for n in range(lax.axis_size("dp"))])


def ordered(value, *others):
    return lax.optimization_barrier((value, *others))[0]


def body(
    inputs,
    attention_norm_gain,
    attention_norm_bias,
    query_weight,
    key_weight,
    value_weight,
    relative_weight,
    head_bias,
    output_weight,
    feedforward_norm_gain,
    feedforward_norm_bias,
    up_weight,
    up_bias,
    down_weight,
    down_bias,
    parents,
    positions,
    cotangent,
):
    del positions
    n_dp = lax.axis_size("dp")
    rows = query_weight.shape[0]
    me = lax.axis_index("tensor").astype(jnp.int32)
    place = lax.axis_index("dp").astype(jnp.int32)
    ids = jnp.where(jnp.arange(8) < 4, me ^ jnp.arange(8, dtype=jnp.int32), place)
    hosts = parents.reshape(MB, LEAVES)
    gain1 = attention_norm_gain.reshape(1, D)

    vmem = pl.BlockSpec(memory_space=pltpu.VMEM)
    *normed, shards, shard = call(
        prepare_kernel,
        1,
        [vmem] * 11,
        [vmem] * 4,
        [
            struct((QUARTER, D), BF),
            struct((MB - 1, QUARTER, D), BF),
            struct((n_dp, rows, 4 * COLS), BF),
            struct((rows, PACKED + COLS), BF),
        ],
        [],
        cost(MB * QUARTER * D * 10, MB * QUARTER * D * 4),
    )(
        ids, inputs, gain1, attention_norm_bias.reshape(1, D), query_weight, key_weight,
        value_weight, relative_weight, up_weight, down_weight.T, output_weight.T,
        up_bias.reshape(1, D),
    )
    w_heads = (lax.all_to_all(shards, "dp", 0, 0, tiled=True).reshape(D, 4 * COLS),)
    first_far = swap(normed[0], 2)
    rest_far = swap(ordered(normed[1], first_far), 2)
    first_tokens = (normed[0], swap(normed[0], 1), first_far, swap(first_far, 1))

    w_all = lax.all_gather(shard, ("dp", "tensor"), axis=0, tiled=False)
    w_all = w_all.reshape(n_dp, 4, rows, PACKED + COLS)
    if rows % 16:
        w_all = jnp.swapaxes(w_all, 0, 1).reshape(1, 4, D, PACKED + COLS)

    freq = jnp.exp(jnp.arange(D // 2, dtype=F32) * (-2.0 * math.log(10000.0) / D))[:, None]
    fine = freq * jnp.arange(128, dtype=F32)
    coarse = freq * (128.0 * jnp.arange(8, dtype=F32))
    sincos, table = call(
        table_kernel,
        0,
        [whole((D, 128)), whole((D, 8))],
        [whole((D, DEPTH)), whole((DEPTH, D))],
        [struct((D, DEPTH), F32), struct((DEPTH, D), BF)],
        [],
        cost(D * DEPTH * 20, D * DEPTH * 6),
        grid=(1,),
    )(
        jnp.concatenate([jnp.sin(fine), jnp.cos(fine)]),
        jnp.concatenate([jnp.sin(coarse), jnp.cos(coarse)]),
    )

    forward = []
    tokens = (first_tokens,)
    for m in range(MB):
        if m == 1:
            rest_far = ordered(rest_far, forward[0][0])
            tokens += ((normed[1], swap(normed[1], 1), rest_far, swap(rest_far, 1)),)
        forward.append(
            attention_forward(
                m, ids, hosts, of_tree(tokens, m), w_heads, head_bias, sincos, table
            )
        )

    def spread(blocks):
        return [blocks[0], *(swap(blocks[k], k) for k in (1, 2, 3))]

    middle = middle_part(
        ids, sum((spread(v[:4]) for v in forward), []), inputs, cotangent, w_all,
        feedforward_norm_gain.reshape(1, D), feedforward_norm_bias.reshape(1, D), down_bias,
    )
    out, hid, pg, n2, mix, attended, mgrad = middle[:7]
    grads = (spread(middle[7:11]), spread(middle[11:15]))
    (smalls,) = middle[15:]

    send, keep = weight_products(ids, n2, cotangent, mix, hid, pg, attended)
    other = swap(send, 1)
    half = n_dp // 2
    cut = 640
    low_bit = place & 1

    def pick(value, axis, index):
        return lax.dynamic_index_in_dim(value, index, axis, keepdims=False)

    def plus(a, b):
        return (a.astype(F32) + b.astype(F32)).astype(BF)

    both = plus(keep, other)
    first = both[..., :cut]
    second = both[..., cut:].reshape(2, half, 2, rows, PACKED - cut)
    first_away, second_away = first[1], pick(second, 2, 1 - low_bit)
    stage1 = (first_away, second_away)
    first = plus(first[0], swap(first_away, 2)).reshape(half, 2, rows, cut)
    second = plus(pick(second, 2, low_bit), dp_swap(second_away, 1))
    first_away, second_away = pick(first, 1, 1 - low_bit), second[1]
    stage2 = (first_away, second_away)
    first = plus(pick(first, 1, low_bit), dp_swap(first_away, 1))
    second = plus(second[0], swap(second_away, 2))
    third = jnp.concatenate([first, second], axis=-1)

    others = [dp_swap(pick(third, 0, (place >> 1) ^ k), 2 * k) for k in range(1, half)]
    sums = (smalls,)
    after = [stage1, stage2, (third,)]
    kept = []
    for m in range(MB):
        res = attention_backward(
            m, ids, hosts, of_tree(grads, m), of_tree(tokens, m), w_heads, sincos,
            forward[m][4:], tuple(sums), after[m],
        )
        sums = res[-2:]
        if m == MB - 1:
            keep, send = token_gradients(ids, res[0], w_heads, (*others, kept[3 * m - 1]))
        else:
            keep, send = res[:2]
        other = swap(send, 1)
        if m == MB - 1:
            vectors = sums[0]
            for bit in (1, 2):
                vectors = vectors + swap(vectors, bit)
            other = ordered(other, vectors)
        away = plus(keep[1], other[1])
        if m + 1 < MB:
            after[m + 1] += (away,)
        kept += [keep, other, swap(away, 2)]
    in_grad = input_gradient(gain1, inputs, mgrad, kept)

    g_heads = sums[1].reshape(n_dp, rows, D)
    parts = lax.all_to_all(g_heads, "dp", 0, 0, tiled=True)
    bit = 1
    while bit < n_dp:
        vectors = vectors + dp_swap(vectors, bit)
        bit *= 2
    where = (place * 4 + me).reshape(1)
    gq, gk, gv, gr, up, down, o, mg, ms, heads, fg, fs, upb, downb = final_sums(
        where, parts, vectors, gain1, attention_norm_bias.reshape(1, D),
        [pick(third, 0, place >> 1), *others], (in_grad,),
    )
    return (
        out, in_grad, mg[0], ms[0], gq, gk, gv, gr, heads, o.T, fg[0], fs[0], up, upb[0], down.T,
        downb[0],
    )


def solution(mesh):
    placed = (
        P(None, "dp", "tensor", None),
        P(),
        P(),
        P("dp", "tensor"),
        P("dp", "tensor"),
        P("dp", "tensor"),
        P("dp", "tensor"),
        P(None, "tensor"),
        P("tensor", "dp"),
        P(),
        P(),
        P("dp", "tensor"),
        P("tensor"),
        P("tensor", "dp"),
        P(),
        P(None, "dp", None),
        P(None, "dp", None),
        P(None, "dp", "tensor", None),
    )
    return jax.shard_map(
        body,
        mesh=mesh,
        in_specs=placed,
        out_specs=(
            P(None, "dp", "tensor", None),
            P(None, "dp", "tensor", None),
            P(("dp", "tensor")),
            P(("dp", "tensor")),
            P("dp", "tensor"),
            P("dp", "tensor"),
            P("dp", "tensor"),
            P("dp", "tensor"),
            P(None, ("dp", "tensor")),
            P("tensor", "dp"),
            P(("dp", "tensor")),
            P(("dp", "tensor")),
            P("dp", "tensor"),
            P(("dp", "tensor")),
            P("tensor", "dp"),
            P(("dp", "tensor")),
        ),
        check_vma=False,
    )
```

```python
import functools
import math

import jax
import jax.numpy as jnp
from jax import lax
from jax.experimental import pallas as pl
from jax.experimental.pallas import tpu as pltpu
from jax.sharding import PartitionSpec as P

D = 512
HD = 64
FF = 2048
TRUNK = 512
SEG = 64
BRANCHES = 4
LEAVES = 8
MB = 3
TREE = 1280
DEPTH = 640
COLS = 128
QUARTER = 320
PACKED = 2 * D + COLS
QB = 256
EPS = 1e-05
BF = jnp.bfloat16
F32 = jnp.float32

CHUNKS = (
    ((0, "causal"),),
    ((0, None), (256, "causal")),
    ((0, None), (256, None), (512, "segment")),
    ((0, None), (256, None), (512, "host"), (768, "segment")),
    ((0, None), (256, None), (512, "host"), (1024, "segment")),
)
OFFSETS = (0, 256, 768, 1536, 2560)
SAVED = 3584


def nn(a, b):
    return lax.dot_general(a, b, (((1,), (0,)), ((), ())), preferred_element_type=F32)


def nt(a, b):
    return lax.dot_general(a, b, (((1,), (1,)), ((), ())), preferred_element_type=F32)


def key_runs(block):
    runs = []
    for n, (start, _) in enumerate(CHUNKS[block]):
        if runs and runs[-1][0] + runs[-1][1] == start:
            runs[-1][1] += 256
        else:
            runs.append([start, 256, n * 256])
    return runs


def chunk_mask(kind, block, parents, micro):
    key = lax.broadcasted_iota(jnp.int32, (256, QB), 0)
    query = lax.broadcasted_iota(jnp.int32, (256, QB), 1)
    if kind == "causal":
        return key <= query
    if kind == "segment":
        return (key <= query) & (key // SEG == query // SEG)
    lane = lax.broadcasted_iota(jnp.int32, (1, QB), 1) // SEG
    first = (block - 3) * 4
    host = jnp.zeros((1, QB), jnp.int32)
    for n in range(4):
        host = jnp.where(lane == n, parents[micro, first + n], host)
    return (key // SEG + 1) == host


def raised(parents, micro, leaf):
    return (parents[micro, leaf] > 0).astype(jnp.int32)


def last_columns(near, out_ref, parents, micro):
    last = near[...]
    turned = pltpu.roll(last, SEG, 1)
    lane = lax.broadcasted_iota(jnp.int32, (1, 128), 1)
    low = jnp.where(lane < SEG, last, turned)
    out_ref[:, TRUNK : TRUNK + 128] = low
    out_ref[:, TRUNK + 128 : TRUNK + 256] = low
    for pair in range(LEAVES // 2):
        left = raised(parents, micro, 2 * pair)
        right = raised(parents, micro, 2 * pair + 1)
        straight = jnp.where(lane < SEG, 1 - left, right)
        at = TRUNK + 256 + pair * 128
        out_ref[:, at : at + 128] = jnp.where(straight > 0, last, turned)


def prepare_kernel(
    where, x_ref, gain_ref, bias_ref, q, k, v, r, up, down_t, out_t, up_bias, first, rest, heads, ff
):
    for n in range(MB):
        x = x_ref[n, 0].astype(F32)
        centered = x - jnp.mean(x, axis=-1, keepdims=True)
        spread = jnp.mean(centered * centered, axis=-1, keepdims=True)
        y = (centered * lax.rsqrt(spread + EPS) * gain_ref[...] + bias_ref[...]).astype(BF)
        if n == 0:
            first[...] = y
        else:
            rest[n - 1] = y
    for n in range(heads.shape[0]):
        for at, part in enumerate((q, k, v, r)):
            heads[n, :, at * COLS : (at + 1) * COLS] = part[...]
    rows = up.shape[0]
    ff[:, 0:D] = up[...]
    ff[:, D : 2 * D] = down_t[...]
    ff[:, 2 * D : PACKED] = out_t[...]
    at = where[4] * rows
    line = pltpu.roll(jnp.broadcast_to(up_bias[...], (8, D)), jnp.where(at > 0, D - at, 0), 1)
    column = jnp.transpose(jnp.broadcast_to(line[0:1, 0:128], (128, 128)))[0:rows]
    high = column.astype(BF).astype(F32)
    lane = lax.broadcasted_iota(jnp.int32, (rows, COLS), 1)
    ff[:, PACKED:] = jnp.where(lane == 0, high, column - high).astype(BF)


def table_kernel(fine, coarse, sincos, table):
    sf, cf = fine[0:256, :], fine[256:512, :]
    for n in range(DEPTH // 128):
        sc, cc = coarse[0:256, n : n + 1], coarse[256:512, n : n + 1]
        cols = slice(n * 128, (n + 1) * 128)
        sines = sc * cf + cc * sf
        cosines = cc * cf - sc * sf
        sincos[0:256, cols] = sines
        sincos[256:512, cols] = cosines
        table[cols, 0:256] = jnp.transpose(cosines.astype(BF))
        table[cols, 256:512] = jnp.transpose(sines.astype(BF))


def copies(sems, pairs):
    made = []
    for n, (source, target) in enumerate(pairs):
        made.append(pltpu.make_async_copy(source, target, sems.at[n]))
        made[-1].start()
    return made


def wait(made):
    for copy in made:
        copy.wait()


def weight_rows(ids, blocks, target):
    rows = blocks[0].shape[0]
    count = len(blocks)
    pairs = []
    for n, block in enumerate(blocks):
        place = (ids[4] ^ n) if count > 1 else 0
        at = pl.multiple_of(place * rows, rows) if count > 1 else 0
        pairs.append((block, target.at[pl.ds(at, rows), :]))
    return pairs


def token_rows(ids, n):
    return pl.ds(pl.multiple_of(ids[n] * QUARTER, SEG), QUARTER)


def forward_kernel(micro, blocks, ids, hosts, *refs):
    x = refs[0:4]
    wb = refs[4 : 4 + blocks]
    hb, sincos, table = refs[4 + blocks : 7 + blocks]
    refs = refs[7 + blocks :]
    att, (probs, inverse, natural, turned) = refs[0:4], refs[4:8]
    xs, w, near, kcat, vt, ct, sct, qts, scores, att_t, ps, inv, nat, trn, att_n, s_in, s_tab, s_out, s_probs = refs[8:]

    x = [v if len(v.shape) == 2 else v.at[micro - 1] for v in x]
    tokens = copies(s_in, [(x[n], xs.at[n]) for n in range(4)] + weight_rows(ids, wb, w))
    pairs = [(table.at[0 : TRUNK + SEG, :], kcat.at[0 : TRUNK + SEG, 0:D])]
    for n in range(1, BRANCHES):
        at = TRUNK + n * SEG
        pairs.append((table.at[TRUNK : TRUNK + SEG, :], kcat.at[at : at + SEG, 0:D]))
    for n in range(LEAVES):
        at = TRUNK + (BRANCHES + n) * SEG
        row = pl.multiple_of(TRUNK + SEG * raised(hosts, micro, n), SEG)
        pairs.append((table.at[pl.ds(row, SEG), :], kcat.at[at : at + SEG, 0:D]))
    pairs.append((sincos.at[:, 0:TRUNK], sct.at[:, 0:TRUNK]))
    pairs.append((sincos.at[:, TRUNK:DEPTH], near))
    wait(tokens[4:])
    for n in range(4):
        tokens[n].wait()
        if n == 1:
            tables = copies(s_tab, pairs)
        y = nn(xs[n], w[:, 0 : 3 * COLS])
        rows = token_rows(ids, n)
        q = y[:, 0:COLS]
        nat[0, rows, :] = (q + hb[0:1, :]).astype(BF)
        nat[1, rows, :] = (q + hb[1:2, :]).astype(BF)
        kcat[rows, D : D + COLS] = y[:, COLS : 2 * COLS].astype(BF)
        nat[2, rows, :] = y[:, 2 * COLS : 3 * COLS].astype(BF)
    ct[...] = jnp.transpose(nat[0])
    trn[0] = jnp.transpose(kcat[:, D : D + COLS])
    vt[...] = jnp.transpose(nat[2])
    sent = copies(s_out, [(nat, natural), (trn.at[0], turned.at[0])])
    wait(tables)
    last_columns(near, sct, hosts, micro)
    factor = math.log2(math.e) / math.sqrt(HD)

    order = (4, 3, 2, 1, 0)

    def saved(head, at):
        rows = pl.ds(OFFSETS[order[at]], 256 * len(CHUNKS[order[at]]))
        return pltpu.make_async_copy(
            ps.at[head, rows, :], probs.at[head, rows, :], s_probs.at[head * 5 + at]
        )

    def one_head(head, _):
        mine = lax.broadcasted_iota(jnp.int32, (1, COLS), 1) // HD == head
        mine_t = lax.broadcasted_iota(jnp.int32, (COLS, 1), 0) // HD == head

        def rotate(block):
            cols = slice(block * QB, (block + 1) * QB)
            qt = qts.at[block]
            position = jnp.where(mine, nat[1, cols, :], 0)
            relative = nt(w[:, 3 * COLS : 4 * COLS], position)
            rs, rc = relative[0:256], relative[256:512]
            sines, cosines = sct[0:256, cols], sct[256:512, cols]
            qt[0:256, :] = (rs * sines + rc * cosines).astype(BF)
            qt[256:512, :] = (rc * sines - rs * cosines).astype(BF)
            qt[512:640, :] = jnp.where(mine_t, ct[:, cols], 0)

        def score(block, n):
            start, kind = CHUNKS[block][n]
            s = nn(kcat[start : start + 256, :], qts[block])
            if kind is not None:
                s = jnp.where(chunk_mask(kind, block, hosts, micro), s, -1e30)
            scores[block % 2, n * 256 : (n + 1) * 256, :] = s
            return jnp.max(s, axis=0, keepdims=True)

        def grow(block, n, peak):
            e = jnp.exp2((scores[block % 2, n * 256 : (n + 1) * 256, :] - peak) * factor)
            row = OFFSETS[block] + n * 256
            ps[head, row : row + 256, :] = e.astype(BF)
            return jnp.sum(e, axis=0, keepdims=True)

        def finish(block, total):
            cols = slice(block * QB, (block + 1) * QB)
            out = None
            for start, keys, row in key_runs(block):
                row = OFFSETS[block] + row
                term = nn(vt[:, start : start + keys], ps[head, row : row + keys, :])
                out = term if out is None else out + term
            over = 1.0 / total
            inv[head, :, cols] = jnp.broadcast_to(over, (8, QB))
            att_t[:, cols] = jnp.where(mine_t, out * over, att_t[:, cols])

        rotate(order[0])
        peak = None
        for n in range(len(CHUNKS[order[0]])):
            high = score(order[0], n)
            peak = high if peak is None else jnp.maximum(peak, high)
        rotate(order[1])
        for at, block in enumerate(order):
            after = order[at + 1] if at < 4 else None
            count = len(CHUNKS[block])
            ahead = len(CHUNKS[after]) if after is not None else 0
            total, high = None, None
            for n in range(max(count, ahead)):
                if n < ahead:
                    top = score(after, n)
                    high = top if high is None else jnp.maximum(high, top)
                if n < count:
                    part = grow(block, n, peak)
                    total = part if total is None else total + part
            if at < 3:
                rotate(order[at + 2])
            finish(block, total)
            saved(head, at).start()
            peak = high
        return 0

    lax.fori_loop(0, 2, one_head, 0)
    wait(sent)
    full = att_t[...].astype(BF)
    trn[1] = full
    att_n[...] = jnp.transpose(full)
    sent = copies(
        s_out,
        [(att_n.at[token_rows(ids, n), :], att[n]) for n in range(4)]
        + [(inv, inverse), (trn.at[1], turned.at[1])],
    )
    for head in range(2):
        for at in range(5):
            saved(head, at).wait()
    wait(sent)


def middle_kernel(ids, *refs):
    a, refs = refs[0 : 4 * MB], refs[4 * MB :]
    x, cot, w_ref, gain, bias, down_bias, out, mgrad, send, keep = refs[:10]
    g = refs[10:18]
    (
        small, a_s, w, hid_all, pg_all, n2_all, mix_all, cot_all, att_all, n2t, cott, mixt,
        mid, xhat, inverse, ffn, n2g, pres, hgs, sems,
    ) = refs[18:]
    m = pl.program_id(0)

    @pl.when(m < MB)
    def _():
        tree_rows(
            m, ids, a, x, cot, w_ref, gain, bias, down_bias, out, mgrad, g, small, a_s, w,
            hid_all, pg_all, n2_all, mix_all, cot_all, att_all, mid, xhat, inverse, ffn, n2g,
            pres, hgs, sems,
        )

    @pl.when(m == MB)
    def _():
        n2t[...] = jnp.transpose(n2_all[...])
        cott[...] = jnp.transpose(cot_all[...])
        mixt[...] = jnp.transpose(mix_all[...])

    @pl.when(m >= MB)
    def _():
        step = m - MB
        part = ids[jnp.where(step < 2, 2 * step + 1, 2 * step - 4)]
        wide = pl.ds(pl.multiple_of(part * D, D), D)
        slim = pl.ds(pl.multiple_of(part * COLS, COLS), COLS)
        value = jnp.concatenate(
            [
                nn(n2t[...], pg_all[:, wide]).astype(BF),
                nn(cott[...], hid_all[:, wide]).astype(BF),
                nn(mixt[...], att_all[:, slim]).astype(BF),
            ],
            axis=1,
        )

        @pl.when(step < 2)
        def _():
            send[0] = value

        @pl.when(step >= 2)
        def _():
            keep[0] = value


def tree_rows(
    m, ids, a, x, cot, w_ref, gain, bias, down_bias, out, mgrad, g, small, a_s, w,
    hid_all, pg_all, n2_all, mix_all, cot_all, att_all, mid, xhat, inverse, ffn, n2g,
    pres, hgs, sems,
):
    groups, rows = w.shape[0], w.shape[2]
    here = pl.ds(pl.multiple_of(m * QUARTER, SEG), QUARTER)
    hid, pg, n2 = hid_all.at[here, :], pg_all.at[here, :], n2_all.at[here, :]

    def part(t, first, last):
        return w[:, t, :, first:last].reshape(D, last - first)

    def loads(first, last):
        pairs = [(a[4 * k + n], a_s.at[k, n]) for k in range(MB) for n in range(4)]
        pairs.append((w_ref.at[:, :, :, 2 * D :], w.at[:, :, :, 2 * D :]))
        pairs += [(w_ref.at[:, t, :, 0 : 2 * D], w.at[:, t, :, 0 : 2 * D]) for t in range(4)]
        pairs = list(enumerate(pairs))[first:last]
        return [pltpu.make_async_copy(p, q, sems.at[n]) for n, (p, q) in pairs]

    @pl.when(m == 0)
    def _():
        made = loads(0, 4 * MB + 5)
        for copy in made:
            copy.start()
        wait(made[: 4 * MB + 1])

    cot_all[here, :] = cot[0, 0]
    total = x[0, 0].astype(F32)
    later = jnp.maximum(m - 1, 0)
    for n in range(4):
        block = a_s[m, n]
        total = total + nt(block, part(ids[n], 2 * D, 2 * D + COLS))
        att_all[here, pl.ds(pl.multiple_of(ids[n] * COLS, COLS), COLS)] = block
    centered = total - jnp.mean(total, axis=-1, keepdims=True)
    spread = jnp.mean(centered * centered, axis=-1, keepdims=True)
    inv = lax.rsqrt(spread + EPS)
    mid[...] = total
    inverse[...] = inv
    xhat[...] = centered * inv
    n2[...] = (centered * inv * gain[...] + bias[...]).astype(BF)

    @pl.when(m == 0)
    def _():
        small[...] = jnp.zeros_like(small)
        wait(loads(4 * MB + 1, 4 * MB + 5))

    width = 256
    steps = FF // width
    biases = []
    for t in range(4):
        extra = jnp.transpose(part(t, PACKED, PACKED + COLS))
        biases.append(extra[0:1, :].astype(F32) + extra[1:2, :].astype(F32))

    def weights(n):
        t, at = n * width // D, n * width % D
        return part(t, at, at + width), part(t, D + at, D + at + width)

    def start(n):
        up, down = weights(n)
        t, at = n * width // D, n * width % D
        pres[n % 3] = nn(n2[...], up) + biases[t][:, at : at + width]
        hgs[n % 3] = nn(cot[0, 0], down)

    def shape(n):
        cols = slice(n * width, (n + 1) * width)
        pre = pres[n % 3]
        cdf = 0.5 * (1.0 + lax.erf(pre * 0.7071067811865476))
        hid[:, cols] = (pre * cdf).astype(BF)
        slope = cdf + pre * jnp.exp(-0.5 * pre * pre) * 0.3989422804014327
        p = hgs[n % 3] * slope
        pg[:, cols] = p.astype(BF)
        t, at = n * width // D, n * width % D
        small[8 + t : 9 + t, at : at + width] += jnp.sum(
            pg[:, cols].astype(F32), axis=0, keepdims=True
        )

    def gather(n):
        cols = slice(n * width, (n + 1) * width)
        up, down = weights(n)
        f, b = nt(hid[:, cols], down), nt(pg[:, cols], up)
        if n == 0:
            ffn[...] = f
            n2g[...] = b
        else:
            ffn[...] += f
            n2g[...] += b

    for n in range(steps + 2):
        if n < steps:
            start(n)
        if 0 <= n - 1 < steps:
            shape(n - 1)
        if n >= 2:
            gather(n - 2)

    out[0, 0] = mid[...] + ffn[...] + down_bias[...]
    gr = n2g[...]
    inv = inverse[...]
    xh = xhat[...]
    c = cot[0, 0].astype(F32)
    small[4:5, :] += jnp.sum(gr * xh, axis=0, keepdims=True)
    small[5:6, :] += jnp.sum(gr, axis=0, keepdims=True)
    small[6:7, :] += jnp.sum(c, axis=0, keepdims=True)
    e = gr * gain[...]
    mg = c + inv * (
        e - jnp.mean(e, axis=-1, keepdims=True) - xh * jnp.mean(e * xh, axis=-1, keepdims=True)
    )
    mgrad[0] = mg
    mixed = mg.astype(BF)
    mix_all[here, :] = mixed
    for n in range(4):
        block = nn(mixed, part(ids[n], 2 * D, 2 * D + COLS)).astype(BF)

        @pl.when(m == 0)
        def _():
            g[n][...] = block

        @pl.when(m > 0)
        def _():
            g[4 + n][later] = block


def backward_kernel(micro, blocks, ids, hosts, *refs):
    d, x, wb = refs[0:4], refs[4:8], refs[8 : 8 + blocks]
    sincos, probs, inverse, natural, turned = refs[8 + blocks : 13 + blocks]
    refs = refs[13 + blocks :]
    last = micro == MB - 1
    before, acc = refs[0], refs[1] if micro else None
    refs = refs[2 if micro else 1 :]
    if last:
        dall_out, out_s, out_g = refs[0:3]
        refs = refs[3:]
    else:
        keep, send, out_s, out_g = refs[0:4]
        refs = refs[4:]
    (
        do, w, near, ps, inv, nat, trn, dot, kcat_t, sct, ds, dqs, dk, dv, dq_t, hc, hp,
        dall, wrt, rel, cg, grel, xall, gw, result, dps, s_in, s_probs, s_x, s_out,
    ) = refs

    grads = [v if len(v.shape) == 2 else v.at[micro - 1] for v in d]
    x = [v if len(v.shape) == 2 else v.at[micro - 1] for v in x]
    first = copies(
        s_in,
        [(grads[n], do.at[token_rows(ids, n), :]) for n in range(4)]
        + [(turned, trn), (inverse, inv), (sincos.at[:, TRUNK:DEPTH], near)]
        + [(sincos.at[:, 0:TRUNK], sct.at[:, 0:TRUNK]), (natural, nat)]
        + weight_rows(ids, wb, w),
    )
    order = (4, 3, 2, 1, 0)
    dk[...] = jnp.zeros_like(dk)
    dv[...] = jnp.zeros_like(dv)
    hc[...] = jnp.zeros_like(hc)
    hp[...] = jnp.zeros_like(hp)
    wait(first[:6])
    chunks = [(0, block) for block in order] + [(1, block) for block in order]
    for n, (head, block) in enumerate(chunks):
        rows = pl.ds(OFFSETS[block], 256 * len(CHUNKS[block]))
        pltpu.make_async_copy(
            probs.at[head, rows, :], ps.at[head, rows, :], s_probs.at[n]
        ).start()
    tokens = copies(s_x, token_pairs(ids, x, xall) + ([(acc, gw)] if micro else []))
    dot[...] = jnp.transpose(do[...])
    kcat_t[512:640, :] = trn[0]
    wait(first[6:8])
    last_columns(near, sct, hosts, micro)
    kcat_t[0:256, :] = sct[256:512, :].astype(BF)
    kcat_t[256:512, :] = sct[0:256, :].astype(BF)
    wait(first[8:])
    wrt[...] = jnp.transpose(w[:, 3 * COLS : 4 * COLS])
    factor = 1.0 / math.sqrt(HD)

    def one_head(head, _):
        mine = lax.broadcasted_iota(jnp.int32, (1, COLS), 1) // HD == head
        mine_t = lax.broadcasted_iota(jnp.int32, (COLS, 1), 0) // HD == head

        def begin(block):
            cols = slice(block * QB, (block + 1) * QB)
            over = inv[head, 0:1, cols]
            grad = jnp.where(mine_t, dot[:, cols].astype(F32), 0.0) * (over * factor)
            delta = jnp.sum(grad * trn[1, :, cols].astype(F32), axis=0, keepdims=True)
            grad_t = grad.astype(BF)
            content = jnp.where(mine, nat[0, cols, :], 0)
            return grad_t, jnp.transpose(grad_t), delta, content

        def gain(block, n, state, slot):
            start = CHUNKS[block][n][0]
            dps[slot] = nn(nat[2, start : start + 256, :], state[0]) - state[2]

        def weigh(block, n, slot):
            row = OFFSETS[block] + n * 256
            p = ps[head, row : row + 256, :].astype(F32)
            ds[block, n * 256 : (n + 1) * 256, :] = (p * dps[slot]).astype(BF)

        def spend(block, n, state):
            row = OFFSETS[block] + n * 256
            keys = slice(CHUNKS[block][n][0], CHUNKS[block][n][0] + 256)
            dv[keys, :] += nn(ps[head, row : row + 256, :], state[1])
            dk[keys, :] += nn(ds[block, n * 256 : (n + 1) * 256, :], state[3])

        def back(block, first, last):
            dq = None
            for start, keys, row in key_runs(block):
                term = nn(
                    kcat_t[first:last, start : start + keys], ds[block, row : row + keys, :]
                )
                dq = term if dq is None else dq + term
            if first < D:
                dqs[block, first:last, :] = dq
            else:
                cg[:, block * QB : (block + 1) * QB] = dq

        def turn(block, first, last):
            cols = slice(block * QB, (block + 1) * QB)
            s1, s2 = dqs[block, first:last, :], dqs[block, 256 + first : 256 + last, :]
            sines, cosines = sct[first:last, cols], sct[256 + first : 256 + last, cols]
            rel[first:last, cols] = (s1 * sines - s2 * cosines).astype(BF)
            rel[256 + first : 256 + last, cols] = (s1 * cosines + s2 * sines).astype(BF)

        items = [(block, n) for block in order for n in range(len(CHUNKS[block]))]
        states = {}
        todo = []
        for i in range(len(items) + 2):
            for task in todo[:2]:
                task()
            todo = todo[2:]
            if i < len(items):
                block, n = items[i]
                if n == 0:
                    at = order.index(block)
                    rows = pl.ds(OFFSETS[block], 256 * len(CHUNKS[block]))
                    pltpu.make_async_copy(
                        probs.at[head, rows, :], ps.at[head, rows, :], s_probs.at[head * 5 + at]
                    ).wait()
                    states[block] = begin(block)
                gain(block, n, states[block], i % 3)
            if 0 <= i - 1 < len(items):
                weigh(*items[i - 1], (i - 1) % 3)
            if i >= 2:
                block, n = items[i - 2]
                spend(block, n, states[block])
                if n + 1 == len(CHUNKS[block]):
                    for cut in (0, 128):
                        todo.append(functools.partial(back, block, cut, cut + 128))
                        todo.append(functools.partial(back, block, 256 + cut, 384 + cut))
                    todo.append(functools.partial(back, block, D, D + COLS))
                    for cut in (0, 128):
                        todo.append(functools.partial(turn, block, cut, cut + 128))
        for task in todo:
            task()
        position = jnp.where(mine, nat[1], 0)
        grel[...] = grel[...] + nn(rel[...], position)
        pgrad = jnp.where(mine_t, nn(wrt[...], rel[...]), 0.0)
        cgrad = jnp.where(mine_t, cg[...], 0.0)
        for n in range(TREE // 128):
            hp[...] += pgrad[:, n * 128 : (n + 1) * 128]
            hc[...] += cgrad[:, n * 128 : (n + 1) * 128]
        dq_t[...] = jnp.where(mine_t, (pgrad + cgrad).astype(BF), dq_t[...])
        return 0

    grel[...] = jnp.zeros_like(grel)
    lax.fori_loop(0, 2, one_head, 0)
    dall[:, 0:COLS] = jnp.transpose(dq_t[...])
    dall[:, COLS : 2 * COLS] = dk[...].astype(BF)
    dall[:, 2 * COLS :] = (dv[...] * math.sqrt(HD)).astype(BF)
    wait(tokens)
    sent = []
    if last:
        sent += copies(s_in, [(dall, dall_out)])
    if not micro:
        gw[...] = jnp.zeros_like(gw)
    new = lax.dot_general(
        xall[...], dall[...], (((0,), (0,)), ((), ())), preferred_element_type=F32
    )
    gw[:, 0 : 3 * COLS] += new
    gw[:, 3 * COLS :] += grel[...]
    if last:
        result[...] = gw[...].astype(BF)
    sent += copies(s_x, [(result if last else gw, out_g)])
    if not last:
        sent += token_grads(ids, dall, w, result, keep, send, s_out)

    columns = jnp.sum(dall[...].astype(F32), axis=0, keepdims=True)
    scaled, plain = None, None
    for n in range(3):
        cols = slice(n * COLS, (n + 1) * COLS)
        weight = w[:, cols].astype(F32)
        one, two = new[:, cols] * weight, columns[:, cols] * weight
        scaled = one if scaled is None else scaled + one
        plain = two if plain is None else plain + two
    out_s[...] = before[...]
    for n, v in enumerate((scaled, plain)):
        v = jnp.sum(jnp.transpose(v), axis=0, keepdims=True)
        out_s[n : n + 1, :] = before[n : n + 1, :] + v
    lanes = pl.ds(pl.multiple_of(ids[0] * COLS, COLS), COLS)
    for n, h in enumerate((hc, hp)):
        v = jnp.sum(jnp.transpose(h[...]), axis=0, keepdims=True)
        out_s[2 + n : 3 + n, lanes] = before[2 + n : 3 + n, lanes] + v
    wait(sent)


def token_pairs(ids, x, target):
    return [(x[n], target.at[token_rows(ids, n), :]) for n in range(4)]


def token_grads(ids, dall, w, dns, keep, send, sems):
    sent = []
    for n, target in ((1, send.at[0]), (3, send.at[1]), (0, keep.at[0]), (2, keep.at[1])):
        dns[n] = nt(dall[token_rows(ids, n), :], w[:, 0 : 3 * COLS]).astype(BF)
        sent.append(pltpu.make_async_copy(dns.at[n], target, sems.at[n]))
        sent[-1].start()
    return sent


def token_grads_kernel(blocks, ids, *refs):
    dall_in, wb = refs[0], refs[1 : 1 + blocks]
    keep, send, dall, w, dns, s_in, s_out = refs[1 + blocks :]
    wait(copies(s_in, weight_rows(ids, wb, w) + [(dall_in, dall)]))
    wait(token_grads(ids, dall, w, dns, keep, send, s_out))


def tail_kernel(gain, x, mgrad, *refs):
    parts, (out, xs, ms, gs, result, sems) = refs[:-6], refs[-6:]
    made = []
    for m in range(MB):
        own, near, far = parts[3 * m : 3 * m + 3]
        made.append(
            copies(
                sems.at[m],
                [
                    (x.at[m, 0], xs.at[m]),
                    (mgrad.at[m], ms.at[m]),
                    (own.at[0], gs.at[m, 0]),
                    (near.at[0], gs.at[m, 1]),
                    (far, gs.at[m, 2]),
                ],
            )
        )
    sent = []
    for m in range(MB):
        wait(made[m])
        g = gs[m, 0].astype(F32) + gs[m, 1].astype(F32) + gs[m, 2].astype(F32)
        xf = xs[m].astype(F32)
        centered = xf - jnp.mean(xf, axis=-1, keepdims=True)
        spread = jnp.mean(centered * centered, axis=-1, keepdims=True)
        inv = lax.rsqrt(spread + EPS)
        xh = centered * inv
        e = g * gain[...]
        result[m] = ms[m] + inv * (
            e
            - jnp.mean(e, axis=-1, keepdims=True)
            - xh * jnp.mean(e * xh, axis=-1, keepdims=True)
        )
        sent += copies(sems.at[MB + m], [(result.at[m], out.at[m, 0])])
    wait(sent)


def final_kernel(where, parts, vectors, gain, bias, *refs):
    ff, (gq, gk, gv, gr, up, down, out, mg, ms, heads, fg, fs, upb, downb) = refs[:-14], refs[-14:]
    total = parts[0].astype(F32)
    for n in range(1, parts.shape[0]):
        total = total + parts[n].astype(F32)
    for n, ref in enumerate((gq, gk, gv, gr)):
        ref[...] = total[:, n * COLS : (n + 1) * COLS]
    total = ff[0][...].astype(F32)
    for v in ff[1:]:
        total = total + v[...].astype(F32)
    up[...] = total[:, 0:D]
    down[...] = total[:, D : 2 * D]
    out[...] = total[:, 2 * D :]
    each = mg.shape[1]

    at = where[0] * each
    rows = pltpu.roll(vectors[0:8, :], jnp.where(at > 0, D - at, 0), 1)
    scale = pltpu.roll(jnp.broadcast_to(gain[...], (8, D)), jnp.where(at > 0, D - at, 0), 1)
    shift = pltpu.roll(jnp.broadcast_to(bias[...], (8, D)), jnp.where(at > 0, D - at, 0), 1)
    first = (rows[0:1] - shift[0:1] * rows[1:2]) / scale[0:1]
    mg[...] = first[:, 0:each]
    ms[...] = rows[1:2, 0:each]
    heads[...] = rows[2:4, 0:each]
    fg[...] = rows[4:5, 0:each]
    fs[...] = rows[5:6, 0:each]
    downb[...] = rows[6:7, 0:each]
    start = where[0] * (4 * each)
    line = jnp.broadcast_to(vectors[pl.ds(8 + start // D, 1), :], (8, D))
    at = start % D
    upb[...] = pltpu.roll(line, jnp.where(at > 0, D - at, 0), 1)[0:1, 0 : 4 * each]


def whole(shape):
    return pl.BlockSpec(shape, lambda i, *_: (0,) * len(shape))


def cost(flops, nbytes, trans=0):
    return pl.CostEstimate(flops=int(flops), bytes_accessed=int(nbytes), transcendentals=int(trans))


def struct(shape, dtype):
    return jax.ShapeDtypeStruct(shape, dtype)


def call(
    kernel, prefetch, in_specs, out_specs, out_shape, scratch, estimate, *, grid=(), alias=None,
    after=(),
):
    first, last = prefetch + len(in_specs), prefetch + len(in_specs) + len(after)

    def run(*refs):
        kernel(*refs[:first], *refs[last:])

    made = pl.pallas_call(
        run,
        out_shape=out_shape,
        grid_spec=pltpu.PrefetchScalarGridSpec(
            num_scalar_prefetch=prefetch,
            grid=grid,
            in_specs=list(in_specs) + [pl.BlockSpec(memory_space=pl.ANY)] * len(after),
            out_specs=out_specs,
            scratch_shapes=scratch,
        ),
        input_output_aliases=alias or {},
        cost_estimate=estimate,
        compiler_params=pltpu.CompilerParams(
            dimension_semantics=("arbitrary",) * len(grid), vmem_limit_bytes=56 << 20
        ),
    )
    return lambda *operands: made(*operands, *after)


ANY = pl.BlockSpec(memory_space=pl.ANY)


def dma(count):
    return pltpu.SemaphoreType.DMA((count,))


SAVED_SHAPES = [
    ((2, SAVED, QB), BF),
    ((2, 8, TREE), F32),
    ((3, TREE, COLS), BF),
    ((2, COLS, TREE), BF),
]


def of_tree(array, m):
    return array[min(m, 1)]


def attention_forward(m, ids, hosts, tokens, w_heads, head_bias, sincos, table, after=()):
    count = len(w_heads)
    return call(
        functools.partial(forward_kernel, m, count),
        2,
        [ANY] * (4 + count)
        + [pl.BlockSpec(memory_space=pltpu.VMEM), ANY, ANY],
        [ANY] * 8,
        [struct((QUARTER, COLS), BF)] * 4 + [struct(*v) for v in SAVED_SHAPES],
        [
            pltpu.VMEM((4, QUARTER, D), BF),
            pltpu.VMEM((D, D), BF),
            pltpu.VMEM((D, 128), F32),
            pltpu.VMEM((TREE, D + COLS), BF),
            pltpu.VMEM((COLS, TREE), BF),
            pltpu.VMEM((COLS, TREE), BF),
            pltpu.VMEM((D, TREE), F32),
            pltpu.VMEM((5, D + COLS, QB), BF),
            pltpu.VMEM((2, 1024, QB), F32),
            pltpu.VMEM((COLS, TREE), F32),
            *[pltpu.VMEM(*v) for v in SAVED_SHAPES],
            pltpu.VMEM((TREE, COLS), BF),
            dma(4 + count),
            dma(BRANCHES + LEAVES + 2),
            dma(6),
            dma(10),
        ],
        cost(15e9, 12e6, 2e6),
        after=after,
    )(ids, hosts, *tokens, *w_heads, head_bias, sincos, table)


def middle_part(ids, blocks, inputs, cotangent, w_all, gain, bias, down_bias):
    tall = MB * QUARTER
    third = pl.BlockSpec(
        (1, 1, QUARTER, D), lambda m, *_: (jnp.minimum(m, MB - 1), 0, 0, 0)
    )
    small = [(QUARTER, COLS)] * 4 + [(MB - 1, QUARTER, COLS)] * 4
    return call(
        middle_kernel,
        1,
        [ANY] * (4 * MB) + [third, third, ANY, whole((1, D)), whole((1, D)), whole((1, D))],
        [
            third,
            pl.BlockSpec((1, QUARTER, D), lambda m, *_: (jnp.minimum(m, MB - 1), 0, 0)),
            pl.BlockSpec((1, D, PACKED), lambda m, *_: (jnp.clip(m - MB, 0, 1), 0, 0)),
            pl.BlockSpec((1, D, PACKED), lambda m, *_: (jnp.clip(m - MB - 2, 0, 1), 0, 0)),
        ]
        + [whole(v) for v in small]
        + [whole((16, D))],
        [
            struct((MB, 1, QUARTER, D), F32),
            struct((MB, QUARTER, D), F32),
            struct((2, D, PACKED), BF),
            struct((2, D, PACKED), BF),
        ]
        + [struct(v, BF) for v in small]
        + [struct((16, D), F32)],
        [
            pltpu.VMEM((MB, 4, QUARTER, COLS), BF),
            pltpu.VMEM(w_all.shape, BF),
            pltpu.VMEM((tall, FF), BF),
            pltpu.VMEM((tall, FF), BF),
            pltpu.VMEM((tall, D), BF),
            pltpu.VMEM((tall, D), BF),
            pltpu.VMEM((tall, D), BF),
            pltpu.VMEM((tall, D), BF),
            pltpu.VMEM((D, tall), BF),
            pltpu.VMEM((D, tall), BF),
            pltpu.VMEM((D, tall), BF),
            pltpu.VMEM((QUARTER, D), F32),
            pltpu.VMEM((QUARTER, D), F32),
            pltpu.VMEM((QUARTER, 1), F32),
            pltpu.VMEM((QUARTER, D), F32),
            pltpu.VMEM((QUARTER, D), F32),
            pltpu.VMEM((3, QUARTER, 256), F32),
            pltpu.VMEM((3, QUARTER, 256), F32),
            dma(4 * MB + 5),
        ],
        cost(36e9, 36e6, 4e6),
        grid=(MB + 4,),
    )(ids, *blocks, inputs, cotangent, w_all, gain, bias, down_bias.reshape(1, D))


def attention_backward(m, ids, hosts, blocks, tokens, w_heads, sincos, saved, sums, after=()):
    count = len(w_heads)
    last = m == MB - 1
    vmem = pl.BlockSpec(memory_space=pltpu.VMEM)
    if last:
        first = [struct((TREE, 3 * COLS), BF)]
    else:
        first = [struct((2, QUARTER, D), BF)] * 2
    return call(
        functools.partial(backward_kernel, m, count),
        2,
        [ANY] * (13 + count) + [vmem, ANY][: len(sums)],
        [ANY] * len(first) + [vmem, ANY],
        first + [struct((16, D), F32), struct((D, D), BF if last else F32)],
        [
            pltpu.VMEM((TREE, COLS), BF),
            pltpu.VMEM((D, D), BF),
            pltpu.VMEM((D, 128), F32),
            *[pltpu.VMEM(*v) for v in SAVED_SHAPES],
            pltpu.VMEM((COLS, TREE), BF),
            pltpu.VMEM((D + COLS, TREE), BF),
            pltpu.VMEM((D, TREE), F32),
            pltpu.VMEM((5, 1024, QB), BF),
            pltpu.VMEM((5, D, QB), F32),
            pltpu.VMEM((TREE, COLS), F32),
            pltpu.VMEM((TREE, COLS), F32),
            pltpu.VMEM((COLS, TREE), BF),
            pltpu.VMEM((COLS, 128), F32),
            pltpu.VMEM((COLS, 128), F32),
            pltpu.VMEM((TREE, 3 * COLS), BF),
            pltpu.VMEM((COLS, D), BF),
            pltpu.VMEM((D, TREE), BF),
            pltpu.VMEM((COLS, TREE), F32),
            pltpu.VMEM((D, COLS), F32),
            pltpu.VMEM((TREE, D), BF),
            pltpu.VMEM((D, D), F32),
            pltpu.VMEM((D, D) if last else (4, QUARTER, D), BF),
            pltpu.VMEM((3, 256, QB), F32),
            dma(9 + count),
            dma(10),
            dma(5),
            dma(4),
        ],
        cost(20e9, 16e6),
        after=after,
    )(ids, hosts, *blocks, *tokens, *w_heads, sincos, *saved, *sums)


def token_gradients(ids, dall, w_heads, after=()):
    count = len(w_heads)
    return call(
        functools.partial(token_grads_kernel, count),
        1,
        [ANY] * (1 + count),
        [ANY, ANY],
        [struct((2, QUARTER, D), BF)] * 2,
        [
            pltpu.VMEM((TREE, 3 * COLS), BF),
            pltpu.VMEM((D, D), BF),
            pltpu.VMEM((4, QUARTER, D), BF),
            dma(1 + count),
            dma(4),
        ],
        cost(4e9, 8e6),
        after=after,
    )(ids, dall, *w_heads)


def input_gradient(gain, inputs, mgrad, kept, after=()):
    return call(
        tail_kernel,
        0,
        [pl.BlockSpec(memory_space=pltpu.VMEM)] + [ANY] * (2 + 3 * MB),
        ANY,
        struct((MB, 1, QUARTER, D), F32),
        [
            pltpu.VMEM((MB, QUARTER, D), BF),
            pltpu.VMEM((MB, QUARTER, D), F32),
            pltpu.VMEM((MB, 3, QUARTER, D), BF),
            pltpu.VMEM((MB, QUARTER, D), F32),
            pltpu.SemaphoreType.DMA((2 * MB, 5)),
        ],
        cost(MB * QUARTER * D * 20, MB * QUARTER * D * 14),
        after=after,
    )(gain, inputs, mgrad, *kept)


def final_sums(where, parts, vectors, gain, bias, ff, after=()):
    rows = ff[0].shape[0]
    each = D * rows // (4 * D)
    vmem = pl.BlockSpec(memory_space=pltpu.VMEM)
    shapes = (
        [(rows, COLS)] * 4
        + [(rows, D), (rows, D), (rows, COLS), (1, each), (1, each), (2, each)]
        + [(1, each), (1, each), (1, 4 * each), (1, each)]
    )
    return call(
        final_kernel,
        1,
        [vmem] * (4 + len(ff)),
        [vmem] * len(shapes),
        [struct(v, F32) for v in shapes],
        [],
        cost(1e6, 4e6),
        after=after,
    )(where, parts, vectors, gain, bias, *ff)


def swap(value, bits):
    return lax.ppermute(value, "tensor", [(n, n ^ bits) for n in range(4)])


def dp_swap(value, bits):
    return lax.ppermute(value, "dp", [(n, n ^ bits) for n in range(lax.axis_size("dp"))])


def ordered(value, *others):
    return lax.optimization_barrier((value, *others))[0]


def body(
    inputs,
    attention_norm_gain,
    attention_norm_bias,
    query_weight,
    key_weight,
    value_weight,
    relative_weight,
    head_bias,
    output_weight,
    feedforward_norm_gain,
    feedforward_norm_bias,
    up_weight,
    up_bias,
    down_weight,
    down_bias,
    parents,
    positions,
    cotangent,
):
    del positions
    n_dp = lax.axis_size("dp")
    rows = query_weight.shape[0]
    me = lax.axis_index("tensor").astype(jnp.int32)
    place = lax.axis_index("dp").astype(jnp.int32)
    ids = jnp.where(jnp.arange(8) < 4, me ^ jnp.arange(8, dtype=jnp.int32), place)
    hosts = parents.reshape(MB, LEAVES)
    gain1 = attention_norm_gain.reshape(1, D)

    vmem = pl.BlockSpec(memory_space=pltpu.VMEM)
    *normed, shards, shard = call(
        prepare_kernel,
        1,
        [vmem] * 11,
        [vmem] * 4,
        [
            struct((QUARTER, D), BF),
            struct((MB - 1, QUARTER, D), BF),
            struct((n_dp, rows, 4 * COLS), BF),
            struct((rows, PACKED + COLS), BF),
        ],
        [],
        cost(MB * QUARTER * D * 10, MB * QUARTER * D * 4),
    )(
        ids, inputs, gain1, attention_norm_bias.reshape(1, D), query_weight, key_weight,
        value_weight, relative_weight, up_weight, down_weight.T, output_weight.T,
        up_bias.reshape(1, D),
    )
    w_heads = (lax.all_to_all(shards, "dp", 0, 0, tiled=True).reshape(D, 4 * COLS),)
    first_far = swap(normed[0], 2)
    rest_far = swap(ordered(normed[1], first_far), 2)
    first_tokens = (normed[0], swap(normed[0], 1), first_far, swap(first_far, 1))

    w_all = lax.all_gather(shard, ("dp", "tensor"), axis=0, tiled=False)
    w_all = w_all.reshape(n_dp, 4, rows, PACKED + COLS)
    if rows % 16:
        w_all = jnp.swapaxes(w_all, 0, 1).reshape(1, 4, D, PACKED + COLS)

    freq = jnp.exp(jnp.arange(D // 2, dtype=F32) * (-2.0 * math.log(10000.0) / D))[:, None]
    fine = freq * jnp.arange(128, dtype=F32)
    coarse = freq * (128.0 * jnp.arange(8, dtype=F32))
    sincos, table = call(
        table_kernel,
        0,
        [whole((D, 128)), whole((D, 8))],
        [whole((D, DEPTH)), whole((DEPTH, D))],
        [struct((D, DEPTH), F32), struct((DEPTH, D), BF)],
        [],
        cost(D * DEPTH * 20, D * DEPTH * 6),
        grid=(1,),
    )(
        jnp.concatenate([jnp.sin(fine), jnp.cos(fine)]),
        jnp.concatenate([jnp.sin(coarse), jnp.cos(coarse)]),
    )

    forward = []
    tokens = (first_tokens,)
    for m in range(MB):
        if m == 1:
            rest_far = ordered(rest_far, forward[0][0])
            tokens += ((normed[1], swap(normed[1], 1), rest_far, swap(rest_far, 1)),)
        forward.append(
            attention_forward(
                m, ids, hosts, of_tree(tokens, m), w_heads, head_bias, sincos, table
            )
        )

    def spread(blocks):
        return [blocks[0], *(swap(blocks[k], k) for k in (1, 2, 3))]

    middle = middle_part(
        ids, sum((spread(v[:4]) for v in forward), []), inputs, cotangent, w_all,
        feedforward_norm_gain.reshape(1, D), feedforward_norm_bias.reshape(1, D), down_bias,
    )
    out, mgrad, send, keep = middle[:4]
    grads = (spread(middle[4:8]), spread(middle[8:12]))
    smalls = middle[12]

    other = swap(send, 1)
    half = n_dp // 2
    cut = 640
    low_bit = place & 1

    def pick(value, axis, index):
        return lax.dynamic_index_in_dim(value, index, axis, keepdims=False)

    def plus(a, b):
        return (a.astype(F32) + b.astype(F32)).astype(BF)

    both = plus(keep, other)
    first = both[..., :cut]
    second = both[..., cut:].reshape(2, half, 2, rows, PACKED - cut)
    first_away, second_away = first[1], pick(second, 2, 1 - low_bit)
    stage1 = (first_away, second_away)
    first = plus(first[0], swap(first_away, 2)).reshape(half, 2, rows, cut)
    second = plus(pick(second, 2, low_bit), dp_swap(second_away, 1))
    first_away, second_away = pick(first, 1, 1 - low_bit), second[1]
    stage2 = (first_away, second_away)
    first = plus(pick(first, 1, low_bit), dp_swap(first_away, 1))
    second = plus(second[0], swap(second_away, 2))
    third = jnp.concatenate([first, second], axis=-1)

    others = [dp_swap(pick(third, 0, (place >> 1) ^ k), 2 * k) for k in range(1, half)]
    sums = (smalls,)
    after = [stage1, stage2, (third,)]
    kept = []
    for m in range(MB):
        res = attention_backward(
            m, ids, hosts, of_tree(grads, m), of_tree(tokens, m), w_heads, sincos,
            forward[m][4:], tuple(sums), after[m],
        )
        sums = res[-2:]
        if m == MB - 1:
            keep, send = token_gradients(ids, res[0], w_heads, (*others, kept[3 * m - 1]))
        else:
            keep, send = res[:2]
        other = swap(send, 1)
        if m == MB - 1:
            vectors = sums[0]
            for bit in (1, 2):
                vectors = vectors + swap(vectors, bit)
            other = ordered(other, vectors)
        away = plus(keep[1], other[1])
        if m + 1 < MB:
            after[m + 1] += (away,)
        kept += [keep, other, swap(away, 2)]
    in_grad = input_gradient(gain1, inputs, mgrad, kept)

    g_heads = sums[1].reshape(n_dp, rows, D)
    parts = lax.all_to_all(g_heads, "dp", 0, 0, tiled=True)
    bit = 1
    while bit < n_dp:
        vectors = vectors + dp_swap(vectors, bit)
        bit *= 2
    where = (place * 4 + me).reshape(1)
    gq, gk, gv, gr, up, down, o, mg, ms, heads, fg, fs, upb, downb = final_sums(
        where, parts, vectors, gain1, attention_norm_bias.reshape(1, D),
        [pick(third, 0, place >> 1), *others], (in_grad,),
    )
    return (
        out, in_grad, mg[0], ms[0], gq, gk, gv, gr, heads, o.T, fg[0], fs[0], up, upb[0], down.T,
        downb[0],
    )


def solution(mesh):
    placed = (
        P(None, "dp", "tensor", None),
        P(),
        P(),
        P("dp", "tensor"),
        P("dp", "tensor"),
        P("dp", "tensor"),
        P("dp", "tensor"),
        P(None, "tensor"),
        P("tensor", "dp"),
        P(),
        P(),
        P("dp", "tensor"),
        P("tensor"),
        P("tensor", "dp"),
        P(),
        P(None, "dp", None),
        P(None, "dp", None),
        P(None, "dp", "tensor", None),
    )
    return jax.shard_map(
        body,
        mesh=mesh,
        in_specs=placed,
        out_specs=(
            P(None, "dp", "tensor", None),
            P(None, "dp", "tensor", None),
            P(("dp", "tensor")),
            P(("dp", "tensor")),
            P("dp", "tensor"),
            P("dp", "tensor"),
            P("dp", "tensor"),
            P("dp", "tensor"),
            P(None, ("dp", "tensor")),
            P("tensor", "dp"),
            P(("dp", "tensor")),
            P(("dp", "tensor")),
            P("dp", "tensor"),
            P(("dp", "tensor")),
            P("tensor", "dp"),
            P(("dp", "tensor")),
        ),
        check_vma=False,
    )
```

```python
import functools
import math

import jax
import jax.numpy as jnp
import numpy as np
from jax import lax
from jax.experimental import pallas as pl
from jax.experimental.pallas import tpu as pltpu
from jax.sharding import PartitionSpec as P

D = 512
HD = 64
FF = 2048
TRUNK = 512
SEG = 64
BRANCHES = 4
LEAVES = 8
MB = 3
TREE = 1280
DEPTH = 640
COLS = 128
QUARTER = 320
PACKED = 2 * D + COLS
QB = 256
EPS = 1e-05
BF = jnp.bfloat16
F32 = jnp.float32

CHUNKS = (
    ((0, "causal"),),
    ((0, None), (256, "causal")),
    ((0, None), (256, None), (512, "segment")),
    ((0, None), (256, None), (512, "host"), (768, "segment")),
    ((0, None), (256, None), (512, "host"), (1024, "segment")),
)
OFFSETS = (0, 256, 768, 1536, 2560)
SAVED = 3584


def nn(a, b):
    return lax.dot_general(a, b, (((1,), (0,)), ((), ())), preferred_element_type=F32)


def nt(a, b):
    return lax.dot_general(a, b, (((1,), (1,)), ((), ())), preferred_element_type=F32)


def key_runs(block):
    runs = []
    for n, (start, _) in enumerate(CHUNKS[block]):
        if runs and runs[-1][0] + runs[-1][1] == start:
            runs[-1][1] += 256
        else:
            runs.append([start, 256, n * 256])
    return runs


def chunk_mask(kind, block, parents, micro):
    key = lax.broadcasted_iota(jnp.int32, (256, QB), 0)
    query = lax.broadcasted_iota(jnp.int32, (256, QB), 1)
    if kind == "causal":
        return key <= query
    if kind == "segment":
        return (key <= query) & (key // SEG == query // SEG)
    lane = lax.broadcasted_iota(jnp.int32, (1, QB), 1) // SEG
    first = (block - 3) * 4
    host = jnp.zeros((1, QB), jnp.int32)
    for n in range(4):
        host = jnp.where(lane == n, parents[micro, first + n], host)
    return (key // SEG + 1) == host


def raised(parents, micro, leaf):
    return (parents[micro, leaf] > 0).astype(jnp.int32)


def last_columns(near, out_ref, parents, micro):
    last = near[...]
    turned = pltpu.roll(last, SEG, 1)
    lane = lax.broadcasted_iota(jnp.int32, (1, 128), 1)
    low = jnp.where(lane < SEG, last, turned)
    out_ref[:, TRUNK : TRUNK + 128] = low
    out_ref[:, TRUNK + 128 : TRUNK + 256] = low
    for pair in range(LEAVES // 2):
        left = raised(parents, micro, 2 * pair)
        right = raised(parents, micro, 2 * pair + 1)
        straight = jnp.where(lane < SEG, 1 - left, right)
        at = TRUNK + 256 + pair * 128
        out_ref[:, at : at + 128] = jnp.where(straight > 0, last, turned)


def norm_kernel(x_ref, gain_ref, bias_ref, fine, coarse, first, rest, sincos, table):
    for n in range(MB):
        x = x_ref[n, 0].astype(F32)
        centered = x - jnp.mean(x, axis=-1, keepdims=True)
        spread = jnp.mean(centered * centered, axis=-1, keepdims=True)
        y = (centered * lax.rsqrt(spread + EPS) * gain_ref[...] + bias_ref[...]).astype(BF)
        if n == 0:
            first[...] = y
        else:
            rest[n - 1] = y
    position_tables(fine, coarse, sincos, table)


def prepare_kernel(where, q, k, v, r, up, down_t, out_t, up_bias, heads, ff):
    for n in range(heads.shape[0]):
        for at, part in enumerate((q, k, v, r)):
            heads[n, :, at * COLS : (at + 1) * COLS] = part[...]
    rows = up.shape[0]
    ff[:, 0:D] = up[...]
    ff[:, D : 2 * D] = down_t[...]
    ff[:, 2 * D : PACKED] = out_t[...]
    at = where[4] * rows
    line = pltpu.roll(jnp.broadcast_to(up_bias[...], (8, D)), jnp.where(at > 0, D - at, 0), 1)
    column = jnp.transpose(jnp.broadcast_to(line[0:1, 0:128], (128, 128)))[0:rows]
    high = column.astype(BF).astype(F32)
    lane = lax.broadcasted_iota(jnp.int32, (rows, COLS), 1)
    ff[:, PACKED:] = jnp.where(lane == 0, high, column - high).astype(BF)


def position_tables(fine, coarse, sincos, table):
    sf, cf = fine[0:256, :], fine[256:512, :]
    for n in range(DEPTH // 128):
        sc, cc = coarse[0:256, n : n + 1], coarse[256:512, n : n + 1]
        cols = slice(n * 128, (n + 1) * 128)
        sines = sc * cf + cc * sf
        cosines = cc * cf - sc * sf
        sincos[0:256, cols] = sines
        sincos[256:512, cols] = cosines
        table[cols, 0:256] = jnp.transpose(cosines.astype(BF))
        table[cols, 256:512] = jnp.transpose(sines.astype(BF))


def copies(sems, pairs):
    made = []
    for n, (source, target) in enumerate(pairs):
        made.append(pltpu.make_async_copy(source, target, sems.at[n]))
        made[-1].start()
    return made


def wait(made):
    for copy in made:
        copy.wait()


def weight_rows(ids, blocks, target):
    rows = blocks[0].shape[0]
    count = len(blocks)
    pairs = []
    for n, block in enumerate(blocks):
        place = (ids[4] ^ n) if count > 1 else 0
        at = pl.multiple_of(place * rows, rows) if count > 1 else 0
        pairs.append((block, target.at[pl.ds(at, rows), :]))
    return pairs


def token_rows(ids, n):
    return pl.ds(pl.multiple_of(ids[n] * QUARTER, SEG), QUARTER)


def forward_kernel(micro, blocks, ids, hosts, *refs):
    x = refs[0:4]
    wb = refs[4 : 4 + blocks]
    hb, sincos, table = refs[4 + blocks : 7 + blocks]
    refs = refs[7 + blocks :]
    att, (probs, inverse, natural, turned) = refs[0:4], refs[4:8]
    xs, w, near, kcat, vt, ct, sct, qts, scores, att_t, ps, inv, nat, trn, att_n, s_in, s_tab, s_out, s_probs = refs[8:]

    x = [v if len(v.shape) == 2 else v.at[micro - 1] for v in x]
    tokens = copies(s_in, [(x[n], xs.at[n]) for n in range(4)] + weight_rows(ids, wb, w))
    pairs = [(table.at[0 : TRUNK + SEG, :], kcat.at[0 : TRUNK + SEG, 0:D])]
    for n in range(1, BRANCHES):
        at = TRUNK + n * SEG
        pairs.append((table.at[TRUNK : TRUNK + SEG, :], kcat.at[at : at + SEG, 0:D]))
    for n in range(LEAVES):
        at = TRUNK + (BRANCHES + n) * SEG
        row = pl.multiple_of(TRUNK + SEG * raised(hosts, micro, n), SEG)
        pairs.append((table.at[pl.ds(row, SEG), :], kcat.at[at : at + SEG, 0:D]))
    pairs.append((sincos.at[:, 0:TRUNK], sct.at[:, 0:TRUNK]))
    pairs.append((sincos.at[:, TRUNK:DEPTH], near))
    wait(tokens[4:])
    for n in range(4):
        tokens[n].wait()
        if n == 1:
            tables = copies(s_tab, pairs)
        y = nn(xs[n], w[:, 0 : 3 * COLS])
        rows = token_rows(ids, n)
        q = y[:, 0:COLS]
        nat[0, rows, :] = (q + hb[0:1, :]).astype(BF)
        nat[1, rows, :] = (q + hb[1:2, :]).astype(BF)
        kcat[rows, D : D + COLS] = y[:, COLS : 2 * COLS].astype(BF)
        nat[2, rows, :] = y[:, 2 * COLS : 3 * COLS].astype(BF)
    ct[...] = jnp.transpose(nat[0])
    trn[0] = jnp.transpose(kcat[:, D : D + COLS])
    vt[...] = jnp.transpose(nat[2])
    sent = copies(s_out, [(nat, natural), (trn.at[0], turned.at[0])])
    wait(tables)
    last_columns(near, sct, hosts, micro)
    factor = math.log2(math.e) / math.sqrt(HD)

    order = (4, 3, 2, 1, 0)

    def saved(head, at):
        rows = pl.ds(OFFSETS[order[at]], 256 * len(CHUNKS[order[at]]))
        return pltpu.make_async_copy(
            ps.at[head, rows, :], probs.at[head, rows, :], s_probs.at[head * 5 + at]
        )

    def one_head(head, _):
        mine = lax.broadcasted_iota(jnp.int32, (1, COLS), 1) // HD == head
        mine_t = lax.broadcasted_iota(jnp.int32, (COLS, 1), 0) // HD == head

        def rotate(block):
            cols = slice(block * QB, (block + 1) * QB)
            qt = qts.at[block]
            position = jnp.where(mine, nat[1, cols, :], 0)
            relative = nt(w[:, 3 * COLS : 4 * COLS], position)
            rs, rc = relative[0:256], relative[256:512]
            sines, cosines = sct[0:256, cols], sct[256:512, cols]
            qt[0:256, :] = (rs * sines + rc * cosines).astype(BF)
            qt[256:512, :] = (rc * sines - rs * cosines).astype(BF)
            qt[512:640, :] = jnp.where(mine_t, ct[:, cols], 0)

        def score(block, n):
            start, kind = CHUNKS[block][n]
            s = nn(kcat[start : start + 256, :], qts[block])
            if kind is not None:
                s = jnp.where(chunk_mask(kind, block, hosts, micro), s, -1e30)
            scores[block % 2, n * 256 : (n + 1) * 256, :] = s
            return jnp.max(s, axis=0, keepdims=True)

        def grow(block, n, peak):
            e = jnp.exp2((scores[block % 2, n * 256 : (n + 1) * 256, :] - peak) * factor)
            row = OFFSETS[block] + n * 256
            ps[head, row : row + 256, :] = e.astype(BF)
            return jnp.sum(e, axis=0, keepdims=True)

        def finish(block, total, at):
            cols = slice(block * QB, (block + 1) * QB)
            out = None
            for start, keys, row in key_runs(block):
                row = OFFSETS[block] + row
                term = nn(vt[:, start : start + keys], ps[head, row : row + keys, :])
                out = term if out is None else out + term
            over = 1.0 / total
            inv[head, :, cols] = jnp.broadcast_to(over, (8, QB))
            att_t[:, cols] = jnp.where(mine_t, out * over, att_t[:, cols])
            saved(head, at).start()

        rotate(order[0])
        peak = None
        for n in range(len(CHUNKS[order[0]])):
            high = score(order[0], n)
            peak = high if peak is None else jnp.maximum(peak, high)
        rotate(order[1])
        todo = []
        for at, block in enumerate(order):
            after = order[at + 1] if at < 4 else None
            count = len(CHUNKS[block])
            ahead = len(CHUNKS[after]) if after is not None else 0
            if at < 3:
                todo.append(functools.partial(rotate, order[at + 2]))
            total, high = None, None
            for n in range(max(count, ahead)):
                if n < ahead:
                    top = score(after, n)
                    high = top if high is None else jnp.maximum(high, top)
                if n < count:
                    part = grow(block, n, peak)
                    total = part if total is None else total + part
                if todo:
                    todo.pop(0)()
            for task in todo:
                task()
            todo = [functools.partial(finish, block, total, at)]
            peak = high
        for task in todo:
            task()
        return 0

    lax.fori_loop(0, 2, one_head, 0)
    wait(sent)
    full = att_t[...].astype(BF)
    trn[1] = full
    att_n[...] = jnp.transpose(full)
    sent = copies(
        s_out,
        [(att_n.at[token_rows(ids, n), :], att[n]) for n in range(4)]
        + [(inv, inverse), (trn.at[1], turned.at[1])],
    )
    for head in range(2):
        for at in range(5):
            saved(head, at).wait()
    wait(sent)


def middle_kernel(ids, *refs):
    a, refs = refs[0 : 4 * MB], refs[4 * MB :]
    x, cot, w_ref, gain, bias, down_bias, out, mgrad, send, keep = refs[:10]
    g = refs[10:18]
    (
        small, a_s, w, hid_all, pg_all, n2_all, mix_all, cot_all, att_all, n2t, cott, mixt,
        mid, xhat, inverse, ffn, n2g, pres, hgs, sems,
    ) = refs[18:]
    m = pl.program_id(0)

    @pl.when(m < MB)
    def _():
        tree_rows(
            m, ids, a, x, cot, w_ref, gain, bias, down_bias, out, mgrad, g, small, a_s, w,
            hid_all, pg_all, n2_all, mix_all, cot_all, att_all, mid, xhat, inverse, ffn, n2g,
            pres, hgs, sems,
        )

    @pl.when(m == MB)
    def _():
        n2t[...] = jnp.transpose(n2_all[...])
        cott[...] = jnp.transpose(cot_all[...])
        mixt[...] = jnp.transpose(mix_all[...])

    @pl.when(m >= MB)
    def _():
        step = m - MB
        part = ids[jnp.where(step < 2, 2 * step + 1, 2 * step - 4)]
        wide = pl.ds(pl.multiple_of(part * D, D), D)
        slim = pl.ds(pl.multiple_of(part * COLS, COLS), COLS)
        value = jnp.concatenate(
            [
                nn(n2t[...], pg_all[:, wide]).astype(BF),
                nn(cott[...], hid_all[:, wide]).astype(BF),
                nn(mixt[...], att_all[:, slim]).astype(BF),
            ],
            axis=1,
        )

        @pl.when(step < 2)
        def _():
            send[0] = value

        @pl.when(step >= 2)
        def _():
            keep[0] = value


def tree_rows(
    m, ids, a, x, cot, w_ref, gain, bias, down_bias, out, mgrad, g, small, a_s, w,
    hid_all, pg_all, n2_all, mix_all, cot_all, att_all, mid, xhat, inverse, ffn, n2g,
    pres, hgs, sems,
):
    groups, rows = w.shape[0], w.shape[2]
    here = pl.ds(pl.multiple_of(m * QUARTER, SEG), QUARTER)
    hid, pg, n2 = hid_all.at[here, :], pg_all.at[here, :], n2_all.at[here, :]

    def part(t, first, last):
        return w[:, t, :, first:last].reshape(D, last - first)

    def loads(first, last):
        pairs = [(a[4 * k + n], a_s.at[k, n]) for k in range(MB) for n in range(4)]
        pairs.append((w_ref.at[:, :, :, 2 * D :], w.at[:, :, :, 2 * D :]))
        pairs += [(w_ref.at[:, t, :, 0 : 2 * D], w.at[:, t, :, 0 : 2 * D]) for t in range(4)]
        pairs = list(enumerate(pairs))[first:last]
        return [pltpu.make_async_copy(p, q, sems.at[n]) for n, (p, q) in pairs]

    @pl.when(m == 0)
    def _():
        made = loads(0, 4 * MB + 5)
        for copy in made:
            copy.start()
        wait(made[: 4 * MB + 1])

    cot_all[here, :] = cot[0, 0]
    total = x[0, 0].astype(F32)
    later = jnp.maximum(m - 1, 0)
    for n in range(4):
        block = a_s[m, n]
        total = total + nt(block, part(ids[n], 2 * D, 2 * D + COLS))
        att_all[here, pl.ds(pl.multiple_of(ids[n] * COLS, COLS), COLS)] = block
    centered = total - jnp.mean(total, axis=-1, keepdims=True)
    spread = jnp.mean(centered * centered, axis=-1, keepdims=True)
    inv = lax.rsqrt(spread + EPS)
    mid[...] = total
    inverse[...] = inv
    xhat[...] = centered * inv
    n2[...] = (centered * inv * gain[...] + bias[...]).astype(BF)

    @pl.when(m == 0)
    def _():
        small[...] = jnp.zeros_like(small)
        wait(loads(4 * MB + 1, 4 * MB + 5))

    width = 256
    steps = FF // width
    biases = []
    for t in range(4):
        extra = jnp.transpose(part(t, PACKED, PACKED + COLS))
        biases.append(extra[0:1, :].astype(F32) + extra[1:2, :].astype(F32))

    def weights(n):
        t, at = n * width // D, n * width % D
        return part(t, at, at + width), part(t, D + at, D + at + width)

    def start(n):
        up, down = weights(n)
        t, at = n * width // D, n * width % D
        pres[n % 3] = nn(n2[...], up) + biases[t][:, at : at + width]
        hgs[n % 3] = nn(cot[0, 0], down)

    def shape(n):
        cols = slice(n * width, (n + 1) * width)
        pre = pres[n % 3]
        cdf = 0.5 * (1.0 + lax.erf(pre * 0.7071067811865476))
        hid[:, cols] = (pre * cdf).astype(BF)
        slope = cdf + pre * jnp.exp(-0.5 * pre * pre) * 0.3989422804014327
        p = hgs[n % 3] * slope
        pg[:, cols] = p.astype(BF)
        t, at = n * width // D, n * width % D
        small[8 + t : 9 + t, at : at + width] += jnp.sum(
            pg[:, cols].astype(F32), axis=0, keepdims=True
        )

    def gather(n):
        cols = slice(n * width, (n + 1) * width)
        up, down = weights(n)
        f, b = nt(hid[:, cols], down), nt(pg[:, cols], up)
        if n == 0:
            ffn[...] = f
            n2g[...] = b
        else:
            ffn[...] += f
            n2g[...] += b

    for n in range(steps + 2):
        if n < steps:
            start(n)
        if 0 <= n - 1 < steps:
            shape(n - 1)
        if n >= 2:
            gather(n - 2)

    out[0, 0] = mid[...] + ffn[...] + down_bias[...]
    gr = n2g[...]
    inv = inverse[...]
    xh = xhat[...]
    c = cot[0, 0].astype(F32)
    small[4:5, :] += jnp.sum(gr * xh, axis=0, keepdims=True)
    small[5:6, :] += jnp.sum(gr, axis=0, keepdims=True)
    small[6:7, :] += jnp.sum(c, axis=0, keepdims=True)
    e = gr * gain[...]
    mg = c + inv * (
        e - jnp.mean(e, axis=-1, keepdims=True) - xh * jnp.mean(e * xh, axis=-1, keepdims=True)
    )
    mgrad[0] = mg
    mixed = mg.astype(BF)
    mix_all[here, :] = mixed
    for n in range(4):
        block = nn(mixed, part(ids[n], 2 * D, 2 * D + COLS)).astype(BF)

        @pl.when(m == 0)
        def _():
            g[n][...] = block

        @pl.when(m > 0)
        def _():
            g[4 + n][later] = block


def backward_kernel(micro, blocks, ids, hosts, *refs):
    d, x, wb = refs[0:4], refs[4:8], refs[8 : 8 + blocks]
    sincos, probs, inverse, natural, turned = refs[8 + blocks : 13 + blocks]
    refs = refs[13 + blocks :]
    last = micro == MB - 1
    before, acc = refs[0], refs[1] if micro else None
    refs = refs[2 if micro else 1 :]
    if last:
        dall_out, out_s, out_g = refs[0:3]
        refs = refs[3:]
    else:
        keep, send, out_s, out_g = refs[0:4]
        refs = refs[4:]
    (
        do, w, near, ps, inv, nat, trn, dot, kcat_t, sct, ds, dqs, dk, dv, dq_t, hc, hp,
        dall, wrt, rel, cg, grel, xall, gw, result, dps, s_in, s_probs, s_x, s_out,
    ) = refs

    grads = [v if len(v.shape) == 2 else v.at[micro - 1] for v in d]
    x = [v if len(v.shape) == 2 else v.at[micro - 1] for v in x]
    first = copies(
        s_in,
        [(grads[n], do.at[token_rows(ids, n), :]) for n in range(4)]
        + [(turned, trn), (inverse, inv), (sincos.at[:, TRUNK:DEPTH], near)]
        + [(sincos.at[:, 0:TRUNK], sct.at[:, 0:TRUNK]), (natural, nat)]
        + weight_rows(ids, wb, w),
    )
    order = (4, 3, 2, 1, 0)
    dk[...] = jnp.zeros_like(dk)
    dv[...] = jnp.zeros_like(dv)
    hc[...] = jnp.zeros_like(hc)
    hp[...] = jnp.zeros_like(hp)
    wait(first[:6])
    chunks = [(0, block) for block in order] + [(1, block) for block in order]
    for n, (head, block) in enumerate(chunks):
        rows = pl.ds(OFFSETS[block], 256 * len(CHUNKS[block]))
        pltpu.make_async_copy(
            probs.at[head, rows, :], ps.at[head, rows, :], s_probs.at[n]
        ).start()
    tokens = copies(s_x, token_pairs(ids, x, xall) + ([(acc, gw)] if micro else []))
    dot[...] = jnp.transpose(do[...])
    kcat_t[512:640, :] = trn[0]
    wait(first[6:8])
    last_columns(near, sct, hosts, micro)
    kcat_t[0:256, :] = sct[256:512, :].astype(BF)
    kcat_t[256:512, :] = sct[0:256, :].astype(BF)
    wait(first[8:])
    wrt[...] = jnp.transpose(w[:, 3 * COLS : 4 * COLS])
    factor = 1.0 / math.sqrt(HD)

    def one_head(head, _):
        mine = lax.broadcasted_iota(jnp.int32, (1, COLS), 1) // HD == head
        mine_t = lax.broadcasted_iota(jnp.int32, (COLS, 1), 0) // HD == head

        def begin(block):
            cols = slice(block * QB, (block + 1) * QB)
            over = inv[head, 0:1, cols]
            grad = jnp.where(mine_t, dot[:, cols].astype(F32), 0.0) * (over * factor)
            delta = jnp.sum(grad * trn[1, :, cols].astype(F32), axis=0, keepdims=True)
            grad_t = grad.astype(BF)
            content = jnp.where(mine, nat[0, cols, :], 0)
            return grad_t, jnp.transpose(grad_t), delta, content

        def gain(block, n, state, slot):
            start = CHUNKS[block][n][0]
            dps[slot] = nn(nat[2, start : start + 256, :], state[0]) - state[2]

        def weigh(block, n, slot):
            row = OFFSETS[block] + n * 256
            p = ps[head, row : row + 256, :].astype(F32)
            ds[block, n * 256 : (n + 1) * 256, :] = (p * dps[slot]).astype(BF)

        def spend(block, n, state):
            row = OFFSETS[block] + n * 256
            keys = slice(CHUNKS[block][n][0], CHUNKS[block][n][0] + 256)
            dv[keys, :] += nn(ps[head, row : row + 256, :], state[1])
            dk[keys, :] += nn(ds[block, n * 256 : (n + 1) * 256, :], state[3])

        def back(block, first, last):
            dq = None
            for start, keys, row in key_runs(block):
                term = nn(
                    kcat_t[first:last, start : start + keys], ds[block, row : row + keys, :]
                )
                dq = term if dq is None else dq + term
            if first < D:
                dqs[block, first:last, :] = dq
            else:
                cg[:, block * QB : (block + 1) * QB] = dq

        def turn(block, first, last):
            cols = slice(block * QB, (block + 1) * QB)
            s1, s2 = dqs[block, first:last, :], dqs[block, 256 + first : 256 + last, :]
            sines, cosines = sct[first:last, cols], sct[256 + first : 256 + last, cols]
            rel[first:last, cols] = (s1 * sines - s2 * cosines).astype(BF)
            rel[256 + first : 256 + last, cols] = (s1 * cosines + s2 * sines).astype(BF)

        items = [(block, n) for block in order for n in range(len(CHUNKS[block]))]
        states = {}
        todo = []
        for i in range(len(items) + 2):
            for task in todo[:2]:
                task()
            todo = todo[2:]
            if i < len(items):
                block, n = items[i]
                if n == 0:
                    at = order.index(block)
                    rows = pl.ds(OFFSETS[block], 256 * len(CHUNKS[block]))
                    pltpu.make_async_copy(
                        probs.at[head, rows, :], ps.at[head, rows, :], s_probs.at[head * 5 + at]
                    ).wait()
                    states[block] = begin(block)
                gain(block, n, states[block], i % 3)
            if 0 <= i - 1 < len(items):
                weigh(*items[i - 1], (i - 1) % 3)
            if i >= 2:
                block, n = items[i - 2]
                spend(block, n, states[block])
                if n + 1 == len(CHUNKS[block]):
                    for cut in (0, 128):
                        todo.append(functools.partial(back, block, cut, cut + 128))
                        todo.append(functools.partial(back, block, 256 + cut, 384 + cut))
                    todo.append(functools.partial(back, block, D, D + COLS))
                    for cut in (0, 128):
                        todo.append(functools.partial(turn, block, cut, cut + 128))
        for task in todo:
            task()
        position = jnp.where(mine, nat[1], 0)
        grel[...] = grel[...] + nn(rel[...], position)
        pgrad = jnp.where(mine_t, nn(wrt[...], rel[...]), 0.0)
        cgrad = jnp.where(mine_t, cg[...], 0.0)
        for n in range(TREE // 128):
            hp[...] += pgrad[:, n * 128 : (n + 1) * 128]
            hc[...] += cgrad[:, n * 128 : (n + 1) * 128]
        dq_t[...] = jnp.where(mine_t, (pgrad + cgrad).astype(BF), dq_t[...])
        return 0

    grel[...] = jnp.zeros_like(grel)
    lax.fori_loop(0, 2, one_head, 0)
    dall[:, 0:COLS] = jnp.transpose(dq_t[...])
    dall[:, COLS : 2 * COLS] = dk[...].astype(BF)
    dall[:, 2 * COLS :] = (dv[...] * math.sqrt(HD)).astype(BF)
    wait(tokens)
    sent = []
    if last:
        sent += copies(s_in, [(dall, dall_out)])
    if not micro:
        gw[...] = jnp.zeros_like(gw)
    new = lax.dot_general(
        xall[...], dall[...], (((0,), (0,)), ((), ())), preferred_element_type=F32
    )
    gw[:, 0 : 3 * COLS] += new
    gw[:, 3 * COLS :] += grel[...]
    if last:
        result[...] = gw[...].astype(BF)
    sent += copies(s_x, [(result if last else gw, out_g)])
    if not last:
        sent += token_grads(ids, dall, w, result, keep, send, s_out)

    columns = jnp.sum(dall[...].astype(F32), axis=0, keepdims=True)
    scaled, plain = None, None
    for n in range(3):
        cols = slice(n * COLS, (n + 1) * COLS)
        weight = w[:, cols].astype(F32)
        one, two = new[:, cols] * weight, columns[:, cols] * weight
        scaled = one if scaled is None else scaled + one
        plain = two if plain is None else plain + two
    out_s[...] = before[...]
    for n, v in enumerate((scaled, plain)):
        v = jnp.sum(jnp.transpose(v), axis=0, keepdims=True)
        out_s[n : n + 1, :] = before[n : n + 1, :] + v
    lanes = pl.ds(pl.multiple_of(ids[0] * COLS, COLS), COLS)
    for n, h in enumerate((hc, hp)):
        v = jnp.sum(jnp.transpose(h[...]), axis=0, keepdims=True)
        out_s[2 + n : 3 + n, lanes] = before[2 + n : 3 + n, lanes] + v
    wait(sent)


def token_pairs(ids, x, target):
    return [(x[n], target.at[token_rows(ids, n), :]) for n in range(4)]


def token_grads(ids, dall, w, dns, keep, send, sems):
    sent = []
    for n, target in ((1, send.at[0]), (3, send.at[1]), (0, keep.at[0]), (2, keep.at[1])):
        dns[n] = nt(dall[token_rows(ids, n), :], w[:, 0 : 3 * COLS]).astype(BF)
        sent.append(pltpu.make_async_copy(dns.at[n], target, sems.at[n]))
        sent[-1].start()
    return sent


def token_grads_kernel(blocks, ids, *refs):
    dall_in, wb = refs[0], refs[1 : 1 + blocks]
    keep, send, dall, w, dns, s_in, s_out = refs[1 + blocks :]
    wait(copies(s_in, weight_rows(ids, wb, w) + [(dall_in, dall)]))
    wait(token_grads(ids, dall, w, dns, keep, send, s_out))


def tail_kernel(gain, x, mgrad, *refs):
    parts, (out, xs, ms, gs, result, sems) = refs[:-6], refs[-6:]
    made = []
    for m in range(MB):
        own, near, far = parts[3 * m : 3 * m + 3]
        made.append(
            copies(
                sems.at[m],
                [
                    (x.at[m, 0], xs.at[m]),
                    (mgrad.at[m], ms.at[m]),
                    (own.at[0], gs.at[m, 0]),
                    (near.at[0], gs.at[m, 1]),
                    (far, gs.at[m, 2]),
                ],
            )
        )
    sent = []
    for m in range(MB):
        wait(made[m])
        g = gs[m, 0].astype(F32) + gs[m, 1].astype(F32) + gs[m, 2].astype(F32)
        xf = xs[m].astype(F32)
        centered = xf - jnp.mean(xf, axis=-1, keepdims=True)
        spread = jnp.mean(centered * centered, axis=-1, keepdims=True)
        inv = lax.rsqrt(spread + EPS)
        xh = centered * inv
        e = g * gain[...]
        result[m] = ms[m] + inv * (
            e
            - jnp.mean(e, axis=-1, keepdims=True)
            - xh * jnp.mean(e * xh, axis=-1, keepdims=True)
        )
        sent += copies(sems.at[MB + m], [(result.at[m], out.at[m, 0])])
    wait(sent)


def pack_kernel(grad, own, far, out):
    count, rows = out.shape[0], out.shape[1] - 16
    sums = own[...] + far[...]
    row = lax.broadcasted_iota(jnp.int32, (8, D), 0)
    lane = lax.broadcasted_iota(jnp.int32, (8, D), 1)
    some, more = D // count, FF // count
    for n in range(count):
        out[n, 0:rows, :] = grad[n * rows : (n + 1) * rows, :]
        value = pltpu.roll(sums[0:8, :], (D - n * some) % D, 1)
        line, at = 8 + n * more // D, n * more % D
        line = jnp.broadcast_to(sums[line : line + 1, :], (8, D))
        line = pltpu.roll(line, (D + 128 - at) % D, 1)
        there = (row == 0) & (lane >= 128) & (lane < 128 + more)
        value = jnp.where(lane < some, value, jnp.where(there, line, 0.0))
        high = value.astype(BF).astype(F32)
        out[n, rows : rows + 16, :] = jnp.concatenate([high, value - high], axis=0).astype(BF)


def final_kernel(where, parts, gain, bias, *refs):
    ff, (gq, gk, gv, gr, up, down, out, mg, ms, heads, fg, fs, upb, downb) = refs[:-14], refs[-14:]
    rows = parts.shape[1] - 16
    total = parts[0].astype(F32)
    for n in range(1, parts.shape[0]):
        total = total + parts[n].astype(F32)
    for n, ref in enumerate((gq, gk, gv, gr)):
        ref[...] = total[0:rows, n * COLS : (n + 1) * COLS]
    sums = total[rows : rows + 8] + total[rows + 8 : rows + 16]
    total = ff[0][...].astype(F32)
    for v in ff[1:]:
        total = total + v[...].astype(F32)
    up[...] = total[:, 0:D]
    down[...] = total[:, D : 2 * D]
    out[...] = total[:, 2 * D :]
    each = mg.shape[1]

    def moved(value, at):
        return pltpu.roll(jnp.broadcast_to(value, (8, D)), jnp.where(at > 0, D - at, 0), 1)

    rows = moved(sums, where[1] * each)
    scale = moved(gain[...], where[0] * each)
    shift = moved(bias[...], where[0] * each)
    first = (rows[0:1] - shift[0:1] * rows[1:2]) / scale[0:1]
    mg[...] = first[:, 0:each]
    ms[...] = rows[1:2, 0:each]
    heads[...] = rows[2:4, 0:each]
    fg[...] = rows[4:5, 0:each]
    fs[...] = rows[5:6, 0:each]
    downb[...] = rows[6:7, 0:each]
    upb[...] = moved(sums[0:1], 128 + where[1] * 4 * each)[0:1, 0 : 4 * each]


def whole(shape):
    return pl.BlockSpec(shape, lambda i, *_: (0,) * len(shape))


def cost(flops, nbytes, trans=0):
    return pl.CostEstimate(flops=int(flops), bytes_accessed=int(nbytes), transcendentals=int(trans))


def struct(shape, dtype):
    return jax.ShapeDtypeStruct(shape, dtype)


def call(
    kernel, prefetch, in_specs, out_specs, out_shape, scratch, estimate, *, grid=(), alias=None,
    after=(),
):
    first, last = prefetch + len(in_specs), prefetch + len(in_specs) + len(after)

    def run(*refs):
        kernel(*refs[:first], *refs[last:])

    made = pl.pallas_call(
        run,
        out_shape=out_shape,
        grid_spec=pltpu.PrefetchScalarGridSpec(
            num_scalar_prefetch=prefetch,
            grid=grid,
            in_specs=list(in_specs) + [pl.BlockSpec(memory_space=pl.ANY)] * len(after),
            out_specs=out_specs,
            scratch_shapes=scratch,
        ),
        input_output_aliases=alias or {},
        cost_estimate=estimate,
        compiler_params=pltpu.CompilerParams(
            dimension_semantics=("arbitrary",) * len(grid), vmem_limit_bytes=56 << 20
        ),
    )
    return lambda *operands: made(*operands, *after)


ANY = pl.BlockSpec(memory_space=pl.ANY)


def dma(count):
    return pltpu.SemaphoreType.DMA((count,))


SAVED_SHAPES = [
    ((2, SAVED, QB), BF),
    ((2, 8, TREE), F32),
    ((3, TREE, COLS), BF),
    ((2, COLS, TREE), BF),
]


def of_tree(array, m):
    return array[min(m, 1)]


def attention_forward(m, ids, hosts, tokens, w_heads, head_bias, sincos, table, after=()):
    count = len(w_heads)
    return call(
        functools.partial(forward_kernel, m, count),
        2,
        [ANY] * (4 + count)
        + [pl.BlockSpec(memory_space=pltpu.VMEM), ANY, ANY],
        [ANY] * 8,
        [struct((QUARTER, COLS), BF)] * 4 + [struct(*v) for v in SAVED_SHAPES],
        [
            pltpu.VMEM((4, QUARTER, D), BF),
            pltpu.VMEM((D, D), BF),
            pltpu.VMEM((D, 128), F32),
            pltpu.VMEM((TREE, D + COLS), BF),
            pltpu.VMEM((COLS, TREE), BF),
            pltpu.VMEM((COLS, TREE), BF),
            pltpu.VMEM((D, TREE), F32),
            pltpu.VMEM((5, D + COLS, QB), BF),
            pltpu.VMEM((2, 1024, QB), F32),
            pltpu.VMEM((COLS, TREE), F32),
            *[pltpu.VMEM(*v) for v in SAVED_SHAPES],
            pltpu.VMEM((TREE, COLS), BF),
            dma(4 + count),
            dma(BRANCHES + LEAVES + 2),
            dma(6),
            dma(10),
        ],
        cost(15e9, 12e6, 2e6),
        after=after,
    )(ids, hosts, *tokens, *w_heads, head_bias, sincos, table)


def middle_part(ids, blocks, inputs, cotangent, w_all, gain, bias, down_bias):
    tall = MB * QUARTER
    third = pl.BlockSpec(
        (1, 1, QUARTER, D), lambda m, *_: (jnp.minimum(m, MB - 1), 0, 0, 0)
    )
    small = [(QUARTER, COLS)] * 4 + [(MB - 1, QUARTER, COLS)] * 4
    return call(
        middle_kernel,
        1,
        [ANY] * (4 * MB) + [third, third, ANY, whole((1, D)), whole((1, D)), whole((1, D))],
        [
            third,
            pl.BlockSpec((1, QUARTER, D), lambda m, *_: (jnp.minimum(m, MB - 1), 0, 0)),
            pl.BlockSpec((1, D, PACKED), lambda m, *_: (jnp.clip(m - MB, 0, 1), 0, 0)),
            pl.BlockSpec((1, D, PACKED), lambda m, *_: (jnp.clip(m - MB - 2, 0, 1), 0, 0)),
        ]
        + [whole(v) for v in small]
        + [whole((16, D))],
        [
            struct((MB, 1, QUARTER, D), F32),
            struct((MB, QUARTER, D), F32),
            struct((2, D, PACKED), BF),
            struct((2, D, PACKED), BF),
        ]
        + [struct(v, BF) for v in small]
        + [struct((16, D), F32)],
        [
            pltpu.VMEM((MB, 4, QUARTER, COLS), BF),
            pltpu.VMEM(w_all.shape, BF),
            pltpu.VMEM((tall, FF), BF),
            pltpu.VMEM((tall, FF), BF),
            pltpu.VMEM((tall, D), BF),
            pltpu.VMEM((tall, D), BF),
            pltpu.VMEM((tall, D), BF),
            pltpu.VMEM((tall, D), BF),
            pltpu.VMEM((D, tall), BF),
            pltpu.VMEM((D, tall), BF),
            pltpu.VMEM((D, tall), BF),
            pltpu.VMEM((QUARTER, D), F32),
            pltpu.VMEM((QUARTER, D), F32),
            pltpu.VMEM((QUARTER, 1), F32),
            pltpu.VMEM((QUARTER, D), F32),
            pltpu.VMEM((QUARTER, D), F32),
            pltpu.VMEM((3, QUARTER, 256), F32),
            pltpu.VMEM((3, QUARTER, 256), F32),
            dma(4 * MB + 5),
        ],
        cost(36e9, 36e6, 4e6),
        grid=(MB + 4,),
    )(ids, *blocks, inputs, cotangent, w_all, gain, bias, down_bias.reshape(1, D))


def attention_backward(m, ids, hosts, blocks, tokens, w_heads, sincos, saved, sums, after=()):
    count = len(w_heads)
    last = m == MB - 1
    vmem = pl.BlockSpec(memory_space=pltpu.VMEM)
    if last:
        first = [struct((TREE, 3 * COLS), BF)]
    else:
        first = [struct((2, QUARTER, D), BF)] * 2
    return call(
        functools.partial(backward_kernel, m, count),
        2,
        [ANY] * (13 + count) + [vmem, ANY][: len(sums)],
        [ANY] * len(first) + [vmem, ANY],
        first + [struct((16, D), F32), struct((D, D), BF if last else F32)],
        [
            pltpu.VMEM((TREE, COLS), BF),
            pltpu.VMEM((D, D), BF),
            pltpu.VMEM((D, 128), F32),
            *[pltpu.VMEM(*v) for v in SAVED_SHAPES],
            pltpu.VMEM((COLS, TREE), BF),
            pltpu.VMEM((D + COLS, TREE), BF),
            pltpu.VMEM((D, TREE), F32),
            pltpu.VMEM((5, 1024, QB), BF),
            pltpu.VMEM((5, D, QB), F32),
            pltpu.VMEM((TREE, COLS), F32),
            pltpu.VMEM((TREE, COLS), F32),
            pltpu.VMEM((COLS, TREE), BF),
            pltpu.VMEM((COLS, 128), F32),
            pltpu.VMEM((COLS, 128), F32),
            pltpu.VMEM((TREE, 3 * COLS), BF),
            pltpu.VMEM((COLS, D), BF),
            pltpu.VMEM((D, TREE), BF),
            pltpu.VMEM((COLS, TREE), F32),
            pltpu.VMEM((D, COLS), F32),
            pltpu.VMEM((TREE, D), BF),
            pltpu.VMEM((D, D), F32),
            pltpu.VMEM((D, D) if last else (4, QUARTER, D), BF),
            pltpu.VMEM((3, 256, QB), F32),
            dma(9 + count),
            dma(10),
            dma(5),
            dma(4),
        ],
        cost(20e9, 16e6),
        after=after,
    )(ids, hosts, *blocks, *tokens, *w_heads, sincos, *saved, *sums)


def token_gradients(ids, dall, w_heads, after=()):
    count = len(w_heads)
    return call(
        functools.partial(token_grads_kernel, count),
        1,
        [ANY] * (1 + count),
        [ANY, ANY],
        [struct((2, QUARTER, D), BF)] * 2,
        [
            pltpu.VMEM((TREE, 3 * COLS), BF),
            pltpu.VMEM((D, D), BF),
            pltpu.VMEM((4, QUARTER, D), BF),
            dma(1 + count),
            dma(4),
        ],
        cost(4e9, 8e6),
        after=after,
    )(ids, dall, *w_heads)


def input_gradient(gain, inputs, mgrad, kept, after=()):
    return call(
        tail_kernel,
        0,
        [pl.BlockSpec(memory_space=pltpu.VMEM)] + [ANY] * (2 + 3 * MB),
        ANY,
        struct((MB, 1, QUARTER, D), F32),
        [
            pltpu.VMEM((MB, QUARTER, D), BF),
            pltpu.VMEM((MB, QUARTER, D), F32),
            pltpu.VMEM((MB, 3, QUARTER, D), BF),
            pltpu.VMEM((MB, QUARTER, D), F32),
            pltpu.SemaphoreType.DMA((2 * MB, 5)),
        ],
        cost(MB * QUARTER * D * 20, MB * QUARTER * D * 14),
        after=after,
    )(gain, inputs, mgrad, *kept)


def packed_sums(grad, own, far, n_dp):
    vmem = pl.BlockSpec(memory_space=pltpu.VMEM)
    return call(
        pack_kernel,
        0,
        [vmem] * 3,
        vmem,
        struct((n_dp, D // n_dp + 16, D), BF),
        [],
        cost(1e6, 2e6),
    )(grad, own, far)


def final_sums(where, parts, gain, bias, ff, after=()):
    rows = ff[0].shape[0]
    each = rows // 4
    vmem = pl.BlockSpec(memory_space=pltpu.VMEM)
    shapes = (
        [(rows, COLS)] * 4
        + [(rows, D), (rows, D), (rows, COLS), (1, each), (1, each), (2, each)]
        + [(1, each), (1, each), (1, 4 * each), (1, each)]
    )
    return call(
        final_kernel,
        1,
        [vmem] * (3 + len(ff)),
        [vmem] * len(shapes),
        [struct(v, F32) for v in shapes],
        [],
        cost(1e6, 4e6),
        after=after,
    )(where, parts, gain, bias, *ff)


def swap(value, bits):
    return lax.ppermute(value, "tensor", [(n, n ^ bits) for n in range(4)])


def dp_swap(value, bits):
    return lax.ppermute(value, "dp", [(n, n ^ bits) for n in range(lax.axis_size("dp"))])


def ordered(value, *others):
    return lax.optimization_barrier((value, *others))[0]


def body(
    inputs,
    attention_norm_gain,
    attention_norm_bias,
    query_weight,
    key_weight,
    value_weight,
    relative_weight,
    head_bias,
    output_weight,
    feedforward_norm_gain,
    feedforward_norm_bias,
    up_weight,
    up_bias,
    down_weight,
    down_bias,
    parents,
    positions,
    cotangent,
):
    del positions
    n_dp = lax.axis_size("dp")
    rows = query_weight.shape[0]
    me = lax.axis_index("tensor").astype(jnp.int32)
    place = lax.axis_index("dp").astype(jnp.int32)
    ids = jnp.where(jnp.arange(8) < 4, me ^ jnp.arange(8, dtype=jnp.int32), place)
    hosts = parents.reshape(MB, LEAVES)
    gain1 = attention_norm_gain.reshape(1, D)

    vmem = pl.BlockSpec(memory_space=pltpu.VMEM)
    shards, shard = call(
        prepare_kernel,
        1,
        [vmem] * 8,
        [vmem] * 2,
        [struct((n_dp, rows, 4 * COLS), BF), struct((rows, PACKED + COLS), BF)],
        [],
        cost(1e6, 1e6),
    )(
        ids, query_weight, key_weight, value_weight, relative_weight, up_weight, down_weight.T,
        output_weight.T, up_bias.reshape(1, D),
    )
    freq = 10000.0 ** (-2.0 * np.arange(D // 2) / D)[:, None]
    fine, coarse = (
        jnp.asarray(np.concatenate([np.sin(v), np.cos(v)]), F32)
        for v in (freq * np.arange(128), freq * (128.0 * np.arange(8)))
    )
    *normed, sincos, table = call(
        norm_kernel,
        0,
        [vmem] * 5,
        [vmem] * 4,
        [
            struct((QUARTER, D), BF),
            struct((MB - 1, QUARTER, D), BF),
            struct((D, DEPTH), F32),
            struct((DEPTH, D), BF),
        ],
        [],
        cost(MB * QUARTER * D * 10, MB * QUARTER * D * 4),
        after=(shards,),
    )(inputs, gain1, attention_norm_bias.reshape(1, D), fine, coarse)
    w_heads = (lax.all_to_all(shards, "dp", 0, 0, tiled=True).reshape(D, 4 * COLS),)
    first_far = swap(normed[0], 2)
    rest_far = swap(ordered(normed[1], first_far), 2)
    first_tokens = (normed[0], swap(normed[0], 1), first_far, swap(first_far, 1))

    w_all = lax.all_gather(shard, ("dp", "tensor"), axis=0, tiled=False)
    w_all = w_all.reshape(n_dp, 4, rows, PACKED + COLS)
    if rows % 16:
        w_all = jnp.swapaxes(w_all, 0, 1).reshape(1, 4, D, PACKED + COLS)

    forward = []
    tokens = (first_tokens,)
    for m in range(MB):
        if m == 1:
            rest_far = ordered(rest_far, forward[0][0])
            tokens += ((normed[1], swap(normed[1], 1), rest_far, swap(rest_far, 1)),)
        forward.append(
            attention_forward(
                m, ids, hosts, of_tree(tokens, m), w_heads, head_bias, sincos, table
            )
        )

    def spread(blocks):
        return [blocks[0], *(swap(blocks[k], k) for k in (1, 2, 3))]

    middle = middle_part(
        ids, sum((spread(v[:4]) for v in forward), []), inputs, cotangent, w_all,
        feedforward_norm_gain.reshape(1, D), feedforward_norm_bias.reshape(1, D), down_bias,
    )
    out, mgrad, send, keep = middle[:4]
    grads = (spread(middle[4:8]), spread(middle[8:12]))
    smalls = middle[12]

    other = swap(send, 1)
    half = n_dp // 2
    cut = 640
    low_bit = place & 1

    def pick(value, axis, index):
        return lax.dynamic_index_in_dim(value, index, axis, keepdims=False)

    def plus(a, b):
        return (a.astype(F32) + b.astype(F32)).astype(BF)

    both = plus(keep, other)
    first = both[..., :cut]
    second = both[..., cut:].reshape(2, half, 2, rows, PACKED - cut)
    first_away, second_away = first[1], pick(second, 2, 1 - low_bit)
    stage1 = (first_away, second_away)
    first = plus(first[0], swap(first_away, 2)).reshape(half, 2, rows, cut)
    second = plus(pick(second, 2, low_bit), dp_swap(second_away, 1))
    first_away, second_away = pick(first, 1, 1 - low_bit), second[1]
    stage2 = (first_away, second_away)
    first = plus(pick(first, 1, low_bit), dp_swap(first_away, 1))
    second = plus(second[0], swap(second_away, 2))
    third = jnp.concatenate([first, second], axis=-1)

    others = [dp_swap(pick(third, 0, (place >> 1) ^ k), 2 * k) for k in range(1, half)]
    sums = (smalls,)
    after = [stage1, stage2, (third,)]
    kept = []
    for m in range(MB):
        res = attention_backward(
            m, ids, hosts, of_tree(grads, m), of_tree(tokens, m), w_heads, sincos,
            forward[m][4:], tuple(sums), after[m],
        )
        sums = res[-2:]
        if m == MB - 1:
            keep, send = token_gradients(ids, res[0], w_heads, (*others, kept[3 * m - 1]))
        else:
            keep, send = res[:2]
        other = swap(send, 1)
        away = plus(keep[1], other[1])
        if m + 1 < MB:
            after[m + 1] += (away,)
        kept += [keep, other, swap(away, 2)]
        if m + 2 < MB:
            after[m + 2] += (kept[-1],)
    in_grad = input_gradient(gain1, inputs, mgrad, kept)

    vectors = sums[0] + swap(sums[0], 1)
    parts = packed_sums(sums[1], vectors, swap(vectors, 2), n_dp)
    parts = lax.all_to_all(parts, "dp", 0, 0, tiled=True)
    where = jnp.stack([place * 4 + me, me])
    gq, gk, gv, gr, up, down, o, mg, ms, heads, fg, fs, upb, downb = final_sums(
        where, parts, gain1, attention_norm_bias.reshape(1, D),
        [pick(third, 0, place >> 1), *others], (in_grad,),
    )
    return (
        out, in_grad, mg[0], ms[0], gq, gk, gv, gr, heads, o.T, fg[0], fs[0], up, upb[0], down.T,
        downb[0],
    )


def solution(mesh):
    placed = (
        P(None, "dp", "tensor", None),
        P(),
        P(),
        P("dp", "tensor"),
        P("dp", "tensor"),
        P("dp", "tensor"),
        P("dp", "tensor"),
        P(None, "tensor"),
        P("tensor", "dp"),
        P(),
        P(),
        P("dp", "tensor"),
        P("tensor"),
        P("tensor", "dp"),
        P(),
        P(None, "dp", None),
        P(None, "dp", None),
        P(None, "dp", "tensor", None),
    )
    return jax.shard_map(
        body,
        mesh=mesh,
        in_specs=placed,
        out_specs=(
            P(None, "dp", "tensor", None),
            P(None, "dp", "tensor", None),
            P(("dp", "tensor")),
            P(("dp", "tensor")),
            P("dp", "tensor"),
            P("dp", "tensor"),
            P("dp", "tensor"),
            P("dp", "tensor"),
            P(None, ("dp", "tensor")),
            P("tensor", "dp"),
            P(("dp", "tensor")),
            P(("dp", "tensor")),
            P("dp", "tensor"),
            P(("dp", "tensor")),
            P("tensor", "dp"),
            P(("dp", "tensor")),
        ),
        check_vma=False,
    )
```

```python
import functools
import math

import jax
import jax.numpy as jnp
import numpy as np
from jax import lax
from jax.experimental import pallas as pl
from jax.experimental.pallas import tpu as pltpu
from jax.sharding import PartitionSpec as P

D = 512
HD = 64
FF = 2048
TRUNK = 512
SEG = 64
BRANCHES = 4
LEAVES = 8
MB = 3
TREE = 1280
DEPTH = 640
COLS = 128
QUARTER = 320
PACKED = 2 * D + COLS
QB = 256
EPS = 1e-05
BF = jnp.bfloat16
F32 = jnp.float32

CHUNKS = (
    ((0, "causal"),),
    ((0, None), (256, "causal")),
    ((0, None), (256, None), (512, "segment")),
    ((0, None), (256, None), (512, "host"), (768, "segment")),
    ((0, None), (256, None), (512, "host"), (1024, "segment")),
)
OFFSETS = (0, 256, 768, 1536, 2560)
SAVED = 3584


def nn(a, b):
    return lax.dot_general(a, b, (((1,), (0,)), ((), ())), preferred_element_type=F32)


def nt(a, b):
    return lax.dot_general(a, b, (((1,), (1,)), ((), ())), preferred_element_type=F32)


def key_runs(block):
    runs = []
    for n, (start, _) in enumerate(CHUNKS[block]):
        if runs and runs[-1][0] + runs[-1][1] == start:
            runs[-1][1] += 256
        else:
            runs.append([start, 256, n * 256])
    return runs


def chunk_mask(kind, block, parents, micro):
    key = lax.broadcasted_iota(jnp.int32, (256, QB), 0)
    query = lax.broadcasted_iota(jnp.int32, (256, QB), 1)
    if kind == "causal":
        return key <= query
    if kind == "segment":
        return (key <= query) & (key // SEG == query // SEG)
    lane = lax.broadcasted_iota(jnp.int32, (1, QB), 1) // SEG
    first = (block - 3) * 4
    host = jnp.zeros((1, QB), jnp.int32)
    for n in range(4):
        host = jnp.where(lane == n, parents[micro, first + n], host)
    return (key // SEG + 1) == host


def raised(parents, micro, leaf):
    return (parents[micro, leaf] > 0).astype(jnp.int32)


def last_columns(near, out_ref, parents, micro):
    last = near[...]
    turned = pltpu.roll(last, SEG, 1)
    lane = lax.broadcasted_iota(jnp.int32, (1, 128), 1)
    low = jnp.where(lane < SEG, last, turned)
    out_ref[:, TRUNK : TRUNK + 128] = low
    out_ref[:, TRUNK + 128 : TRUNK + 256] = low
    for pair in range(LEAVES // 2):
        left = raised(parents, micro, 2 * pair)
        right = raised(parents, micro, 2 * pair + 1)
        straight = jnp.where(lane < SEG, 1 - left, right)
        at = TRUNK + 256 + pair * 128
        out_ref[:, at : at + 128] = jnp.where(straight > 0, last, turned)


def norm_kernel(x_ref, gain_ref, bias_ref, fine, coarse, first, rest, sincos, table):
    for n in range(MB):
        x = x_ref[n, 0].astype(F32)
        centered = x - jnp.mean(x, axis=-1, keepdims=True)
        spread = jnp.mean(centered * centered, axis=-1, keepdims=True)
        y = (centered * lax.rsqrt(spread + EPS) * gain_ref[...] + bias_ref[...]).astype(BF)
        if n == 0:
            first[...] = y
        else:
            rest[n - 1] = y
    position_tables(fine, coarse, sincos, table)


def prepare_kernel(where, q, k, v, r, up, down_t, out_t, up_bias, heads, ff):
    for n in range(heads.shape[0]):
        for at, part in enumerate((q, k, v, r)):
            heads[n, :, at * COLS : (at + 1) * COLS] = part[...]
    rows = up.shape[0]
    ff[:, 0:D] = up[...]
    ff[:, D : 2 * D] = down_t[...]
    ff[:, 2 * D : PACKED] = out_t[...]
    at = where[4] * rows
    line = pltpu.roll(jnp.broadcast_to(up_bias[...], (8, D)), jnp.where(at > 0, D - at, 0), 1)
    column = jnp.transpose(jnp.broadcast_to(line[0:1, 0:128], (128, 128)))[0:rows]
    high = column.astype(BF).astype(F32)
    lane = lax.broadcasted_iota(jnp.int32, (rows, COLS), 1)
    ff[:, PACKED:] = jnp.where(lane == 0, high, column - high).astype(BF)


def position_tables(fine, coarse, sincos, table):
    sf, cf = fine[0:256, :], fine[256:512, :]
    for n in range(DEPTH // 128):
        sc, cc = coarse[0:256, n : n + 1], coarse[256:512, n : n + 1]
        cols = slice(n * 128, (n + 1) * 128)
        sines = sc * cf + cc * sf
        cosines = cc * cf - sc * sf
        sincos[0:256, cols] = sines
        sincos[256:512, cols] = cosines
        table[cols, 0:256] = jnp.transpose(cosines.astype(BF))
        table[cols, 256:512] = jnp.transpose(sines.astype(BF))


def copies(sems, pairs):
    made = []
    for n, (source, target) in enumerate(pairs):
        made.append(pltpu.make_async_copy(source, target, sems.at[n]))
        made[-1].start()
    return made


def wait(made):
    for copy in made:
        copy.wait()


def weight_rows(ids, blocks, target):
    rows = blocks[0].shape[0]
    count = len(blocks)
    pairs = []
    for n, block in enumerate(blocks):
        place = (ids[4] ^ n) if count > 1 else 0
        at = pl.multiple_of(place * rows, rows) if count > 1 else 0
        pairs.append((block, target.at[pl.ds(at, rows), :]))
    return pairs


def token_rows(ids, n):
    return pl.ds(pl.multiple_of(ids[n] * QUARTER, SEG), QUARTER)


def forward_kernel(micro, blocks, ids, hosts, *refs):
    x = refs[0:4]
    wb = refs[4 : 4 + blocks]
    hb, sincos, table = refs[4 + blocks : 7 + blocks]
    refs = refs[7 + blocks :]
    att, (probs, inverse, natural, turned) = refs[0:4], refs[4:8]
    xs, w, near, kcat, vt, ct, sct, qts, scores, att_t, ps, inv, nat, trn, att_n, s_in, s_tab, s_out, s_probs = refs[8:]

    x = [v if len(v.shape) == 2 else v.at[micro - 1] for v in x]
    tokens = copies(s_in, [(x[n], xs.at[n]) for n in range(4)] + weight_rows(ids, wb, w))
    pairs = [(table.at[0 : TRUNK + SEG, :], kcat.at[0 : TRUNK + SEG, 0:D])]
    for n in range(1, BRANCHES):
        at = TRUNK + n * SEG
        pairs.append((table.at[TRUNK : TRUNK + SEG, :], kcat.at[at : at + SEG, 0:D]))
    for n in range(LEAVES):
        at = TRUNK + (BRANCHES + n) * SEG
        row = pl.multiple_of(TRUNK + SEG * raised(hosts, micro, n), SEG)
        pairs.append((table.at[pl.ds(row, SEG), :], kcat.at[at : at + SEG, 0:D]))
    pairs.append((sincos.at[:, 0:TRUNK], sct.at[:, 0:TRUNK]))
    pairs.append((sincos.at[:, TRUNK:DEPTH], near))
    wait(tokens[4:])
    for n in range(4):
        tokens[n].wait()
        if n == 1:
            tables = copies(s_tab, pairs)
        y = nn(xs[n], w[:, 0 : 3 * COLS])
        rows = token_rows(ids, n)
        q = y[:, 0:COLS]
        nat[0, rows, :] = (q + hb[0:1, :]).astype(BF)
        nat[1, rows, :] = (q + hb[1:2, :]).astype(BF)
        kcat[rows, D : D + COLS] = y[:, COLS : 2 * COLS].astype(BF)
        nat[2, rows, :] = y[:, 2 * COLS : 3 * COLS].astype(BF)
    ct[...] = jnp.transpose(nat[0])
    trn[0] = jnp.transpose(kcat[:, D : D + COLS])
    vt[...] = jnp.transpose(nat[2])
    sent = copies(s_out, [(nat, natural), (trn.at[0], turned.at[0])])
    wait(tables)
    last_columns(near, sct, hosts, micro)
    factor = math.log2(math.e) / math.sqrt(HD)

    order = (4, 3, 2, 1, 0)

    def saved(head, at):
        rows = pl.ds(OFFSETS[order[at]], 256 * len(CHUNKS[order[at]]))
        return pltpu.make_async_copy(
            ps.at[head, rows, :], probs.at[head, rows, :], s_probs.at[head * 5 + at]
        )

    def one_head(head, _):
        mine = lax.broadcasted_iota(jnp.int32, (1, COLS), 1) // HD == head
        mine_t = lax.broadcasted_iota(jnp.int32, (COLS, 1), 0) // HD == head

        def rotate(block):
            cols = slice(block * QB, (block + 1) * QB)
            qt = qts.at[block]
            position = jnp.where(mine, nat[1, cols, :], 0)
            relative = nt(w[:, 3 * COLS : 4 * COLS], position)
            rs, rc = relative[0:256], relative[256:512]
            sines, cosines = sct[0:256, cols], sct[256:512, cols]
            qt[0:256, :] = (rs * sines + rc * cosines).astype(BF)
            qt[256:512, :] = (rc * sines - rs * cosines).astype(BF)
            qt[512:640, :] = jnp.where(mine_t, ct[:, cols], 0)

        def score(block, n):
            start, kind = CHUNKS[block][n]
            s = nn(kcat[start : start + 256, :], qts[block])
            if kind is not None:
                s = jnp.where(chunk_mask(kind, block, hosts, micro), s, -1e30)
            scores[block % 2, n * 256 : (n + 1) * 256, :] = s
            return jnp.max(s, axis=0, keepdims=True)

        def grow(block, n, peak):
            e = jnp.exp2((scores[block % 2, n * 256 : (n + 1) * 256, :] - peak) * factor)
            row = OFFSETS[block] + n * 256
            ps[head, row : row + 256, :] = e.astype(BF)
            return jnp.sum(e, axis=0, keepdims=True)

        def finish(block, total, at):
            cols = slice(block * QB, (block + 1) * QB)
            out = None
            for start, keys, row in key_runs(block):
                row = OFFSETS[block] + row
                term = nn(vt[:, start : start + keys], ps[head, row : row + keys, :])
                out = term if out is None else out + term
            over = 1.0 / total
            inv[head, :, cols] = jnp.broadcast_to(over, (8, QB))
            att_t[:, cols] = jnp.where(mine_t, out * over, att_t[:, cols])
            saved(head, at).start()

        rotate(order[0])
        peak = None
        for n in range(len(CHUNKS[order[0]])):
            high = score(order[0], n)
            peak = high if peak is None else jnp.maximum(peak, high)
        rotate(order[1])
        todo = []
        for at, block in enumerate(order):
            after = order[at + 1] if at < 4 else None
            count = len(CHUNKS[block])
            ahead = len(CHUNKS[after]) if after is not None else 0
            if at < 3:
                todo.append(functools.partial(rotate, order[at + 2]))
            total, high = None, None
            for n in range(max(count, ahead)):
                if n < ahead:
                    top = score(after, n)
                    high = top if high is None else jnp.maximum(high, top)
                if n < count:
                    part = grow(block, n, peak)
                    total = part if total is None else total + part
                if todo:
                    todo.pop(0)()
            for task in todo:
                task()
            todo = [functools.partial(finish, block, total, at)]
            peak = high
        for task in todo:
            task()
        return 0

    lax.fori_loop(0, 2, one_head, 0)
    wait(sent)
    full = att_t[...].astype(BF)
    trn[1] = full
    att_n[...] = jnp.transpose(full)
    sent = copies(
        s_out,
        [(att_n.at[token_rows(ids, n), :], att[n]) for n in range(4)]
        + [(inv, inverse), (trn.at[1], turned.at[1])],
    )
    for head in range(2):
        for at in range(5):
            saved(head, at).wait()
    wait(sent)


def middle_kernel(ids, *refs):
    a, refs = refs[0 : 4 * MB], refs[4 * MB :]
    x, cot, w_ref, gain, bias, down_bias, out, mgrad, send, keep = refs[:10]
    g = refs[10:18]
    (
        small, a_s, w, hid_all, pg_all, n2_all, mix_all, cot_all, att_all, n2t, cott, mixt,
        mid, xhat, inverse, ffn, n2g, pres, hgs, sems,
    ) = refs[18:]
    m = pl.program_id(0)

    @pl.when(m < MB)
    def _():
        tree_rows(
            m, ids, a, x, cot, w_ref, gain, bias, down_bias, out, mgrad, g, small, a_s, w,
            hid_all, pg_all, n2_all, mix_all, cot_all, att_all, mid, xhat, inverse, ffn, n2g,
            pres, hgs, sems,
        )

    @pl.when(m == MB)
    def _():
        n2t[...] = jnp.transpose(n2_all[...])
        cott[...] = jnp.transpose(cot_all[...])
        mixt[...] = jnp.transpose(mix_all[...])

    @pl.when(m >= MB)
    def _():
        step = m - MB
        part = ids[jnp.where(step < 2, 2 * step + 1, 2 * step - 4)]
        wide = pl.ds(pl.multiple_of(part * D, D), D)
        slim = pl.ds(pl.multiple_of(part * COLS, COLS), COLS)
        value = jnp.concatenate(
            [
                nn(n2t[...], pg_all[:, wide]).astype(BF),
                nn(cott[...], hid_all[:, wide]).astype(BF),
                nn(mixt[...], att_all[:, slim]).astype(BF),
            ],
            axis=1,
        )

        @pl.when(step < 2)
        def _():
            send[0] = value

        @pl.when(step >= 2)
        def _():
            keep[0] = value


def tree_rows(
    m, ids, a, x, cot, w_ref, gain, bias, down_bias, out, mgrad, g, small, a_s, w,
    hid_all, pg_all, n2_all, mix_all, cot_all, att_all, mid, xhat, inverse, ffn, n2g,
    pres, hgs, sems,
):
    groups, rows = w.shape[0], w.shape[2]
    here = pl.ds(pl.multiple_of(m * QUARTER, SEG), QUARTER)
    hid, pg, n2 = hid_all.at[here, :], pg_all.at[here, :], n2_all.at[here, :]

    def part(t, first, last):
        return w[:, t, :, first:last].reshape(D, last - first)

    def loads(first, last):
        pairs = [(a[4 * k + n], a_s.at[k, n]) for k in range(MB) for n in range(4)]
        pairs.append((w_ref.at[:, :, :, 2 * D :], w.at[:, :, :, 2 * D :]))
        pairs += [(w_ref.at[:, t, :, 0 : 2 * D], w.at[:, t, :, 0 : 2 * D]) for t in range(4)]
        pairs = list(enumerate(pairs))[first:last]
        return [pltpu.make_async_copy(p, q, sems.at[n]) for n, (p, q) in pairs]

    @pl.when(m == 0)
    def _():
        made = loads(0, 4 * MB + 5)
        for copy in made:
            copy.start()
        wait(made[: 4 * MB + 1])

    cot_all[here, :] = cot[0, 0]
    total = x[0, 0].astype(F32)
    later = jnp.maximum(m - 1, 0)
    for n in range(4):
        block = a_s[m, n]
        total = total + nt(block, part(ids[n], 2 * D, 2 * D + COLS))
        att_all[here, pl.ds(pl.multiple_of(ids[n] * COLS, COLS), COLS)] = block
    centered = total - jnp.mean(total, axis=-1, keepdims=True)
    spread = jnp.mean(centered * centered, axis=-1, keepdims=True)
    inv = lax.rsqrt(spread + EPS)
    mid[...] = total
    inverse[...] = inv
    xhat[...] = centered * inv
    n2[...] = (centered * inv * gain[...] + bias[...]).astype(BF)

    @pl.when(m == 0)
    def _():
        small[...] = jnp.zeros_like(small)
        wait(loads(4 * MB + 1, 4 * MB + 5))

    width = 256
    steps = FF // width
    biases = []
    for t in range(4):
        extra = jnp.transpose(part(t, PACKED, PACKED + COLS))
        biases.append(extra[0:1, :].astype(F32) + extra[1:2, :].astype(F32))

    def weights(n):
        t, at = n * width // D, n * width % D
        return part(t, at, at + width), part(t, D + at, D + at + width)

    def start(n):
        up, down = weights(n)
        t, at = n * width // D, n * width % D
        pres[n % 3] = nn(n2[...], up) + biases[t][:, at : at + width]
        hgs[n % 3] = nn(cot[0, 0], down)

    def shape(n):
        cols = slice(n * width, (n + 1) * width)
        pre = pres[n % 3]
        cdf = 0.5 * (1.0 + lax.erf(pre * 0.7071067811865476))
        hid[:, cols] = (pre * cdf).astype(BF)
        slope = cdf + pre * jnp.exp(-0.5 * pre * pre) * 0.3989422804014327
        p = hgs[n % 3] * slope
        pg[:, cols] = p.astype(BF)
        t, at = n * width // D, n * width % D
        small[8 + t : 9 + t, at : at + width] += jnp.sum(
            pg[:, cols].astype(F32), axis=0, keepdims=True
        )

    def gather(n):
        cols = slice(n * width, (n + 1) * width)
        up, down = weights(n)
        f, b = nt(hid[:, cols], down), nt(pg[:, cols], up)
        if n == 0:
            ffn[...] = f
            n2g[...] = b
        else:
            ffn[...] += f
            n2g[...] += b

    for n in range(steps + 2):
        if n < steps:
            start(n)
        if 0 <= n - 1 < steps:
            shape(n - 1)
        if n >= 2:
            gather(n - 2)

    out[0, 0] = mid[...] + ffn[...] + down_bias[...]
    gr = n2g[...]
    inv = inverse[...]
    xh = xhat[...]
    c = cot[0, 0].astype(F32)
    small[4:5, :] += jnp.sum(gr * xh, axis=0, keepdims=True)
    small[5:6, :] += jnp.sum(gr, axis=0, keepdims=True)
    small[6:7, :] += jnp.sum(c, axis=0, keepdims=True)
    e = gr * gain[...]
    mg = c + inv * (
        e - jnp.mean(e, axis=-1, keepdims=True) - xh * jnp.mean(e * xh, axis=-1, keepdims=True)
    )
    mgrad[0] = mg
    mixed = mg.astype(BF)
    mix_all[here, :] = mixed
    for n in range(4):
        block = nn(mixed, part(ids[n], 2 * D, 2 * D + COLS)).astype(BF)

        @pl.when(m == 0)
        def _():
            g[n][...] = block

        @pl.when(m > 0)
        def _():
            g[4 + n][later] = block


def backward_kernel(micro, blocks, ids, hosts, *refs):
    d, x, wb = refs[0:4], refs[4:8], refs[8 : 8 + blocks]
    sincos, probs, inverse, natural, turned = refs[8 + blocks : 13 + blocks]
    refs = refs[13 + blocks :]
    last = micro == MB - 1
    before, acc = refs[0], refs[1] if micro else None
    refs = refs[2 if micro else 1 :]
    keep, send, out_s, out_g = refs[0:4]
    refs = refs[4:]
    (
        do, w, near, ps, inv, nat, trn, dot, kcat_t, sct, ds, dqs, dk, dv, dq_t, hc, hp,
        dall, wrt, rel, cg, grel, xall, gw, result, dns, dps, s_in, s_probs, s_x, s_out,
    ) = refs

    grads = [v if len(v.shape) == 2 else v.at[micro - 1] for v in d]
    x = [v if len(v.shape) == 2 else v.at[micro - 1] for v in x]
    first = copies(
        s_in,
        [(grads[n], do.at[token_rows(ids, n), :]) for n in range(4)]
        + [(turned, trn), (inverse, inv), (sincos.at[:, TRUNK:DEPTH], near)]
        + [(sincos.at[:, 0:TRUNK], sct.at[:, 0:TRUNK]), (natural, nat)]
        + weight_rows(ids, wb, w),
    )
    order = (4, 3, 2, 1, 0)
    dk[...] = jnp.zeros_like(dk)
    dv[...] = jnp.zeros_like(dv)
    hc[...] = jnp.zeros_like(hc)
    hp[...] = jnp.zeros_like(hp)
    wait(first[:6])
    chunks = [(0, block) for block in order] + [(1, block) for block in order]
    for n, (head, block) in enumerate(chunks):
        rows = pl.ds(OFFSETS[block], 256 * len(CHUNKS[block]))
        pltpu.make_async_copy(
            probs.at[head, rows, :], ps.at[head, rows, :], s_probs.at[n]
        ).start()
    tokens = copies(s_x, token_pairs(ids, x, xall) + ([(acc, gw)] if micro else []))
    dot[...] = jnp.transpose(do[...])
    kcat_t[512:640, :] = trn[0]
    wait(first[6:8])
    last_columns(near, sct, hosts, micro)
    kcat_t[0:256, :] = sct[256:512, :].astype(BF)
    kcat_t[256:512, :] = sct[0:256, :].astype(BF)
    wait(first[8:])
    wrt[...] = jnp.transpose(w[:, 3 * COLS : 4 * COLS])
    factor = 1.0 / math.sqrt(HD)

    def one_head(head, _):
        mine = lax.broadcasted_iota(jnp.int32, (1, COLS), 1) // HD == head
        mine_t = lax.broadcasted_iota(jnp.int32, (COLS, 1), 0) // HD == head

        def begin(block):
            cols = slice(block * QB, (block + 1) * QB)
            over = inv[head, 0:1, cols]
            grad = jnp.where(mine_t, dot[:, cols].astype(F32), 0.0) * (over * factor)
            delta = jnp.sum(grad * trn[1, :, cols].astype(F32), axis=0, keepdims=True)
            grad_t = grad.astype(BF)
            content = jnp.where(mine, nat[0, cols, :], 0)
            return grad_t, jnp.transpose(grad_t), delta, content

        def gain(block, n, state, slot):
            start = CHUNKS[block][n][0]
            dps[slot] = nn(nat[2, start : start + 256, :], state[0]) - state[2]

        def weigh(block, n, slot):
            row = OFFSETS[block] + n * 256
            p = ps[head, row : row + 256, :].astype(F32)
            ds[block, n * 256 : (n + 1) * 256, :] = (p * dps[slot]).astype(BF)

        def spend(block, n, state):
            row = OFFSETS[block] + n * 256
            keys = slice(CHUNKS[block][n][0], CHUNKS[block][n][0] + 256)
            dv[keys, :] += nn(ps[head, row : row + 256, :], state[1])
            dk[keys, :] += nn(ds[block, n * 256 : (n + 1) * 256, :], state[3])

        def back(block, first, last):
            dq = None
            for start, keys, row in key_runs(block):
                term = nn(
                    kcat_t[first:last, start : start + keys], ds[block, row : row + keys, :]
                )
                dq = term if dq is None else dq + term
            if first < D:
                dqs[block, first:last, :] = dq
            else:
                cg[:, block * QB : (block + 1) * QB] = dq

        def turn(block, first, last):
            cols = slice(block * QB, (block + 1) * QB)
            s1, s2 = dqs[block, first:last, :], dqs[block, 256 + first : 256 + last, :]
            sines, cosines = sct[first:last, cols], sct[256 + first : 256 + last, cols]
            rel[first:last, cols] = (s1 * sines - s2 * cosines).astype(BF)
            rel[256 + first : 256 + last, cols] = (s1 * cosines + s2 * sines).astype(BF)

        items = [(block, n) for block in order for n in range(len(CHUNKS[block]))]
        states = {}
        todo = []
        for i in range(len(items) + 2):
            for task in todo[:2]:
                task()
            todo = todo[2:]
            if i < len(items):
                block, n = items[i]
                if n == 0:
                    at = order.index(block)
                    rows = pl.ds(OFFSETS[block], 256 * len(CHUNKS[block]))
                    pltpu.make_async_copy(
                        probs.at[head, rows, :], ps.at[head, rows, :], s_probs.at[head * 5 + at]
                    ).wait()
                    states[block] = begin(block)
                gain(block, n, states[block], i % 3)
            if 0 <= i - 1 < len(items):
                weigh(*items[i - 1], (i - 1) % 3)
            if i >= 2:
                block, n = items[i - 2]
                spend(block, n, states[block])
                if n + 1 == len(CHUNKS[block]):
                    for cut in (0, 128):
                        todo.append(functools.partial(back, block, cut, cut + 128))
                        todo.append(functools.partial(back, block, 256 + cut, 384 + cut))
                    todo.append(functools.partial(back, block, D, D + COLS))
                    for cut in (0, 128):
                        todo.append(functools.partial(turn, block, cut, cut + 128))
        for task in todo:
            task()
        position = jnp.where(mine, nat[1], 0)
        grel[...] = grel[...] + nn(rel[...], position)
        pgrad = jnp.where(mine_t, nn(wrt[...], rel[...]), 0.0)
        cgrad = jnp.where(mine_t, cg[...], 0.0)
        for n in range(TREE // 128):
            hp[...] += pgrad[:, n * 128 : (n + 1) * 128]
            hc[...] += cgrad[:, n * 128 : (n + 1) * 128]
        dq_t[...] = jnp.where(mine_t, (pgrad + cgrad).astype(BF), dq_t[...])
        return 0

    grel[...] = jnp.zeros_like(grel)
    lax.fori_loop(0, 2, one_head, 0)
    dall[:, 0:COLS] = jnp.transpose(dq_t[...])
    dall[:, COLS : 2 * COLS] = dk[...].astype(BF)
    dall[:, 2 * COLS :] = (dv[...] * math.sqrt(HD)).astype(BF)
    wait(tokens)
    sent = []
    if not micro:
        gw[...] = jnp.zeros_like(gw)
    new = lax.dot_general(
        xall[...], dall[...], (((0,), (0,)), ((), ())), preferred_element_type=F32
    )
    gw[:, 0 : 3 * COLS] += new
    gw[:, 3 * COLS :] += grel[...]
    if last:
        result[...] = gw[...].astype(BF)
    sent += copies(s_x, [(result if last else gw, out_g)])
    sent += token_grads(ids, dall, w, dns, keep, send, s_out)

    columns = jnp.sum(dall[...].astype(F32), axis=0, keepdims=True)
    scaled, plain = None, None
    for n in range(3):
        cols = slice(n * COLS, (n + 1) * COLS)
        weight = w[:, cols].astype(F32)
        one, two = new[:, cols] * weight, columns[:, cols] * weight
        scaled = one if scaled is None else scaled + one
        plain = two if plain is None else plain + two
    out_s[...] = before[...]
    for n, v in enumerate((scaled, plain)):
        v = jnp.sum(jnp.transpose(v), axis=0, keepdims=True)
        out_s[n : n + 1, :] = before[n : n + 1, :] + v
    lanes = pl.ds(pl.multiple_of(ids[0] * COLS, COLS), COLS)
    for n, h in enumerate((hc, hp)):
        v = jnp.sum(jnp.transpose(h[...]), axis=0, keepdims=True)
        out_s[2 + n : 3 + n, lanes] = before[2 + n : 3 + n, lanes] + v
    wait(sent)


def token_pairs(ids, x, target):
    return [(x[n], target.at[token_rows(ids, n), :]) for n in range(4)]


def token_grads(ids, dall, w, dns, keep, send, sems):
    sent = []
    for n, target in ((1, send.at[0]), (3, send.at[1]), (0, keep.at[0]), (2, keep.at[1])):
        dns[n] = nt(dall[token_rows(ids, n), :], w[:, 0 : 3 * COLS]).astype(BF)
        sent.append(pltpu.make_async_copy(dns.at[n], target, sems.at[n]))
        sent[-1].start()
    return sent


def tail_kernel(gain, x, mgrad, *refs):
    parts, (out, xs, ms, gs, result, sems) = refs[:-6], refs[-6:]
    made = []
    for m in range(MB):
        own, near, far = parts[3 * m : 3 * m + 3]
        made.append(
            copies(
                sems.at[m],
                [
                    (x.at[m, 0], xs.at[m]),
                    (mgrad.at[m], ms.at[m]),
                    (own.at[0], gs.at[m, 0]),
                    (near.at[0], gs.at[m, 1]),
                    (far, gs.at[m, 2]),
                ],
            )
        )
    sent = []
    for m in range(MB):
        wait(made[m])
        g = gs[m, 0].astype(F32) + gs[m, 1].astype(F32) + gs[m, 2].astype(F32)
        xf = xs[m].astype(F32)
        centered = xf - jnp.mean(xf, axis=-1, keepdims=True)
        spread = jnp.mean(centered * centered, axis=-1, keepdims=True)
        inv = lax.rsqrt(spread + EPS)
        xh = centered * inv
        e = g * gain[...]
        result[m] = ms[m] + inv * (
            e
            - jnp.mean(e, axis=-1, keepdims=True)
            - xh * jnp.mean(e * xh, axis=-1, keepdims=True)
        )
        sent += copies(sems.at[MB + m], [(result.at[m], out.at[m, 0])])
    wait(sent)


def pack_kernel(grad, own, far, out):
    count, rows = out.shape[0], out.shape[1] - 16
    sums = own[...] + far[...]
    row = lax.broadcasted_iota(jnp.int32, (8, D), 0)
    lane = lax.broadcasted_iota(jnp.int32, (8, D), 1)
    some, more = D // count, FF // count
    for n in range(count):
        out[n, 0:rows, :] = grad[n * rows : (n + 1) * rows, :]
        value = pltpu.roll(sums[0:8, :], (D - n * some) % D, 1)
        line, at = 8 + n * more // D, n * more % D
        line = jnp.broadcast_to(sums[line : line + 1, :], (8, D))
        line = pltpu.roll(line, (D + 128 - at) % D, 1)
        there = (row == 0) & (lane >= 128) & (lane < 128 + more)
        value = jnp.where(lane < some, value, jnp.where(there, line, 0.0))
        high = value.astype(BF).astype(F32)
        out[n, rows : rows + 16, :] = jnp.concatenate([high, value - high], axis=0).astype(BF)


def final_kernel(where, parts, gain, bias, *refs):
    ff, (gq, gk, gv, gr, up, down, out, mg, ms, heads, fg, fs, upb, downb) = refs[:-14], refs[-14:]
    rows = parts.shape[1] - 16
    total = parts[0].astype(F32)
    for n in range(1, parts.shape[0]):
        total = total + parts[n].astype(F32)
    for n, ref in enumerate((gq, gk, gv, gr)):
        ref[...] = total[0:rows, n * COLS : (n + 1) * COLS]
    sums = total[rows : rows + 8] + total[rows + 8 : rows + 16]
    total = ff[0][...].astype(F32)
    for v in ff[1:]:
        total = total + v[...].astype(F32)
    up[...] = total[:, 0:D]
    down[...] = total[:, D : 2 * D]
    out[...] = total[:, 2 * D :]
    each = mg.shape[1]

    def moved(value, at):
        return pltpu.roll(jnp.broadcast_to(value, (8, D)), jnp.where(at > 0, D - at, 0), 1)

    rows = moved(sums, where[1] * each)
    scale = moved(gain[...], where[0] * each)
    shift = moved(bias[...], where[0] * each)
    first = (rows[0:1] - shift[0:1] * rows[1:2]) / scale[0:1]
    mg[...] = first[:, 0:each]
    ms[...] = rows[1:2, 0:each]
    heads[...] = rows[2:4, 0:each]
    fg[...] = rows[4:5, 0:each]
    fs[...] = rows[5:6, 0:each]
    downb[...] = rows[6:7, 0:each]
    upb[...] = moved(sums[0:1], 128 + where[1] * 4 * each)[0:1, 0 : 4 * each]


def whole(shape):
    return pl.BlockSpec(shape, lambda i, *_: (0,) * len(shape))


def cost(flops, nbytes, trans=0):
    return pl.CostEstimate(flops=int(flops), bytes_accessed=int(nbytes), transcendentals=int(trans))


def struct(shape, dtype):
    return jax.ShapeDtypeStruct(shape, dtype)


def call(
    kernel, prefetch, in_specs, out_specs, out_shape, scratch, estimate, *, grid=(), alias=None,
    after=(),
):
    first, last = prefetch + len(in_specs), prefetch + len(in_specs) + len(after)

    def run(*refs):
        kernel(*refs[:first], *refs[last:])

    made = pl.pallas_call(
        run,
        out_shape=out_shape,
        grid_spec=pltpu.PrefetchScalarGridSpec(
            num_scalar_prefetch=prefetch,
            grid=grid,
            in_specs=list(in_specs) + [pl.BlockSpec(memory_space=pl.ANY)] * len(after),
            out_specs=out_specs,
            scratch_shapes=scratch,
        ),
        input_output_aliases=alias or {},
        cost_estimate=estimate,
        compiler_params=pltpu.CompilerParams(
            dimension_semantics=("arbitrary",) * len(grid), vmem_limit_bytes=56 << 20
        ),
    )
    return lambda *operands: made(*operands, *after)


ANY = pl.BlockSpec(memory_space=pl.ANY)


def dma(count):
    return pltpu.SemaphoreType.DMA((count,))


SAVED_SHAPES = [
    ((2, SAVED, QB), BF),
    ((2, 8, TREE), F32),
    ((3, TREE, COLS), BF),
    ((2, COLS, TREE), BF),
]


def of_tree(array, m):
    return array[min(m, 1)]


def attention_forward(m, ids, hosts, tokens, w_heads, head_bias, sincos, table, after=()):
    count = len(w_heads)
    return call(
        functools.partial(forward_kernel, m, count),
        2,
        [ANY] * (4 + count)
        + [pl.BlockSpec(memory_space=pltpu.VMEM), ANY, ANY],
        [ANY] * 8,
        [struct((QUARTER, COLS), BF)] * 4 + [struct(*v) for v in SAVED_SHAPES],
        [
            pltpu.VMEM((4, QUARTER, D), BF),
            pltpu.VMEM((D, D), BF),
            pltpu.VMEM((D, 128), F32),
            pltpu.VMEM((TREE, D + COLS), BF),
            pltpu.VMEM((COLS, TREE), BF),
            pltpu.VMEM((COLS, TREE), BF),
            pltpu.VMEM((D, TREE), F32),
            pltpu.VMEM((5, D + COLS, QB), BF),
            pltpu.VMEM((2, 1024, QB), F32),
            pltpu.VMEM((COLS, TREE), F32),
            *[pltpu.VMEM(*v) for v in SAVED_SHAPES],
            pltpu.VMEM((TREE, COLS), BF),
            dma(4 + count),
            dma(BRANCHES + LEAVES + 2),
            dma(6),
            dma(10),
        ],
        cost(15e9, 12e6, 2e6),
        after=after,
    )(ids, hosts, *tokens, *w_heads, head_bias, sincos, table)


def middle_part(ids, blocks, inputs, cotangent, w_all, gain, bias, down_bias):
    tall = MB * QUARTER
    third = pl.BlockSpec(
        (1, 1, QUARTER, D), lambda m, *_: (jnp.minimum(m, MB - 1), 0, 0, 0)
    )
    small = [(QUARTER, COLS)] * 4 + [(MB - 1, QUARTER, COLS)] * 4
    return call(
        middle_kernel,
        1,
        [ANY] * (4 * MB) + [third, third, ANY, whole((1, D)), whole((1, D)), whole((1, D))],
        [
            third,
            pl.BlockSpec((1, QUARTER, D), lambda m, *_: (jnp.minimum(m, MB - 1), 0, 0)),
            pl.BlockSpec((1, D, PACKED), lambda m, *_: (jnp.clip(m - MB, 0, 1), 0, 0)),
            pl.BlockSpec((1, D, PACKED), lambda m, *_: (jnp.clip(m - MB - 2, 0, 1), 0, 0)),
        ]
        + [whole(v) for v in small]
        + [whole((16, D))],
        [
            struct((MB, 1, QUARTER, D), F32),
            struct((MB, QUARTER, D), F32),
            struct((2, D, PACKED), BF),
            struct((2, D, PACKED), BF),
        ]
        + [struct(v, BF) for v in small]
        + [struct((16, D), F32)],
        [
            pltpu.VMEM((MB, 4, QUARTER, COLS), BF),
            pltpu.VMEM(w_all.shape, BF),
            pltpu.VMEM((tall, FF), BF),
            pltpu.VMEM((tall, FF), BF),
            pltpu.VMEM((tall, D), BF),
            pltpu.VMEM((tall, D), BF),
            pltpu.VMEM((tall, D), BF),
            pltpu.VMEM((tall, D), BF),
            pltpu.VMEM((D, tall), BF),
            pltpu.VMEM((D, tall), BF),
            pltpu.VMEM((D, tall), BF),
            pltpu.VMEM((QUARTER, D), F32),
            pltpu.VMEM((QUARTER, D), F32),
            pltpu.VMEM((QUARTER, 1), F32),
            pltpu.VMEM((QUARTER, D), F32),
            pltpu.VMEM((QUARTER, D), F32),
            pltpu.VMEM((3, QUARTER, 256), F32),
            pltpu.VMEM((3, QUARTER, 256), F32),
            dma(4 * MB + 5),
        ],
        cost(36e9, 36e6, 4e6),
        grid=(MB + 4,),
    )(ids, *blocks, inputs, cotangent, w_all, gain, bias, down_bias.reshape(1, D))


def attention_backward(m, ids, hosts, blocks, tokens, w_heads, sincos, saved, sums, after=()):
    count = len(w_heads)
    last = m == MB - 1
    vmem = pl.BlockSpec(memory_space=pltpu.VMEM)
    first = [struct((2, QUARTER, D), BF)] * 2
    return call(
        functools.partial(backward_kernel, m, count),
        2,
        [ANY] * (13 + count) + [vmem, ANY][: len(sums)],
        [ANY] * len(first) + [vmem, ANY],
        first + [struct((16, D), F32), struct((D, D), BF if last else F32)],
        [
            pltpu.VMEM((TREE, COLS), BF),
            pltpu.VMEM((D, D), BF),
            pltpu.VMEM((D, 128), F32),
            *[pltpu.VMEM(*v) for v in SAVED_SHAPES],
            pltpu.VMEM((COLS, TREE), BF),
            pltpu.VMEM((D + COLS, TREE), BF),
            pltpu.VMEM((D, TREE), F32),
            pltpu.VMEM((5, 1024, QB), BF),
            pltpu.VMEM((5, D, QB), F32),
            pltpu.VMEM((TREE, COLS), F32),
            pltpu.VMEM((TREE, COLS), F32),
            pltpu.VMEM((COLS, TREE), BF),
            pltpu.VMEM((COLS, 128), F32),
            pltpu.VMEM((COLS, 128), F32),
            pltpu.VMEM((TREE, 3 * COLS), BF),
            pltpu.VMEM((COLS, D), BF),
            pltpu.VMEM((D, TREE), BF),
            pltpu.VMEM((COLS, TREE), F32),
            pltpu.VMEM((D, COLS), F32),
            pltpu.VMEM((TREE, D), BF),
            pltpu.VMEM((D, D), F32),
            pltpu.VMEM((D, D) if last else (16, 128), BF),
            pltpu.VMEM((4, QUARTER, D), BF),
            pltpu.VMEM((3, 256, QB), F32),
            dma(9 + count),
            dma(10),
            dma(5),
            dma(4),
        ],
        cost(20e9, 16e6),
        after=after,
    )(ids, hosts, *blocks, *tokens, *w_heads, sincos, *saved, *sums)


def input_gradient(gain, inputs, mgrad, kept, after=()):
    return call(
        tail_kernel,
        0,
        [pl.BlockSpec(memory_space=pltpu.VMEM)] + [ANY] * (2 + 3 * MB),
        ANY,
        struct((MB, 1, QUARTER, D), F32),
        [
            pltpu.VMEM((MB, QUARTER, D), BF),
            pltpu.VMEM((MB, QUARTER, D), F32),
            pltpu.VMEM((MB, 3, QUARTER, D), BF),
            pltpu.VMEM((MB, QUARTER, D), F32),
            pltpu.SemaphoreType.DMA((2 * MB, 5)),
        ],
        cost(MB * QUARTER * D * 20, MB * QUARTER * D * 14),
        after=after,
    )(gain, inputs, mgrad, *kept)


def packed_sums(grad, own, far, n_dp, after):
    vmem = pl.BlockSpec(memory_space=pltpu.VMEM)
    return call(
        pack_kernel,
        0,
        [vmem] * 3,
        vmem,
        struct((n_dp, D // n_dp + 16, D), BF),
        [],
        cost(1e6, 2e6),
        after=after,
    )(grad, own, far)


def final_sums(where, parts, gain, bias, ff, after=()):
    rows = ff[0].shape[0]
    each = rows // 4
    vmem = pl.BlockSpec(memory_space=pltpu.VMEM)
    shapes = (
        [(rows, COLS)] * 4
        + [(rows, D), (rows, D), (rows, COLS), (1, each), (1, each), (2, each)]
        + [(1, each), (1, each), (1, 4 * each), (1, each)]
    )
    return call(
        final_kernel,
        1,
        [vmem] * (3 + len(ff)),
        [vmem] * len(shapes),
        [struct(v, F32) for v in shapes],
        [],
        cost(1e6, 4e6),
        after=after,
    )(where, parts, gain, bias, *ff)


def swap(value, bits):
    return lax.ppermute(value, "tensor", [(n, n ^ bits) for n in range(4)])


def dp_swap(value, bits):
    return lax.ppermute(value, "dp", [(n, n ^ bits) for n in range(lax.axis_size("dp"))])


def ordered(value, *others):
    return lax.optimization_barrier((value, *others))[0]


def body(
    inputs,
    attention_norm_gain,
    attention_norm_bias,
    query_weight,
    key_weight,
    value_weight,
    relative_weight,
    head_bias,
    output_weight,
    feedforward_norm_gain,
    feedforward_norm_bias,
    up_weight,
    up_bias,
    down_weight,
    down_bias,
    parents,
    positions,
    cotangent,
):
    del positions
    n_dp = lax.axis_size("dp")
    rows = query_weight.shape[0]
    me = lax.axis_index("tensor").astype(jnp.int32)
    place = lax.axis_index("dp").astype(jnp.int32)
    ids = jnp.where(jnp.arange(8) < 4, me ^ jnp.arange(8, dtype=jnp.int32), place)
    hosts = parents.reshape(MB, LEAVES)
    gain1 = attention_norm_gain.reshape(1, D)

    vmem = pl.BlockSpec(memory_space=pltpu.VMEM)
    shards, shard = call(
        prepare_kernel,
        1,
        [vmem] * 8,
        [vmem] * 2,
        [struct((n_dp, rows, 4 * COLS), BF), struct((rows, PACKED + COLS), BF)],
        [],
        cost(1e6, 1e6),
    )(
        ids, query_weight, key_weight, value_weight, relative_weight, up_weight, down_weight.T,
        output_weight.T, up_bias.reshape(1, D),
    )
    freq = 10000.0 ** (-2.0 * np.arange(D // 2) / D)[:, None]
    fine, coarse = (
        jnp.asarray(np.concatenate([np.sin(v), np.cos(v)]), F32)
        for v in (freq * np.arange(128), freq * (128.0 * np.arange(8)))
    )
    *normed, sincos, table = call(
        norm_kernel,
        0,
        [vmem] * 5,
        [vmem] * 4,
        [
            struct((QUARTER, D), BF),
            struct((MB - 1, QUARTER, D), BF),
            struct((D, DEPTH), F32),
            struct((DEPTH, D), BF),
        ],
        [],
        cost(MB * QUARTER * D * 10, MB * QUARTER * D * 4),
        after=(shards,),
    )(inputs, gain1, attention_norm_bias.reshape(1, D), fine, coarse)
    w_heads = (lax.all_to_all(shards, "dp", 0, 0, tiled=True).reshape(D, 4 * COLS),)
    first_far = swap(normed[0], 2)
    rest_far = swap(ordered(normed[1], first_far), 2)
    first_tokens = (normed[0], swap(normed[0], 1), first_far, swap(first_far, 1))

    w_all = lax.all_gather(shard, ("dp", "tensor"), axis=0, tiled=False)
    w_all = w_all.reshape(n_dp, 4, rows, PACKED + COLS)
    if rows % 16:
        w_all = jnp.swapaxes(w_all, 0, 1).reshape(1, 4, D, PACKED + COLS)

    forward = []
    tokens = (first_tokens,)
    for m in range(MB):
        if m == 1:
            rest_far = ordered(rest_far, forward[0][0])
            tokens += ((normed[1], swap(normed[1], 1), rest_far, swap(rest_far, 1)),)
        forward.append(
            attention_forward(
                m, ids, hosts, of_tree(tokens, m), w_heads, head_bias, sincos, table
            )
        )

    def spread(blocks):
        return [blocks[0], *(swap(blocks[k], k) for k in (1, 2, 3))]

    middle = middle_part(
        ids, sum((spread(v[:4]) for v in forward), []), inputs, cotangent, w_all,
        feedforward_norm_gain.reshape(1, D), feedforward_norm_bias.reshape(1, D), down_bias,
    )
    out, mgrad, send, keep = middle[:4]
    grads = (spread(middle[4:8]), spread(middle[8:12]))
    smalls = middle[12]

    other = swap(send, 1)
    half = n_dp // 2
    cut = 640
    low_bit = place & 1

    def pick(value, axis, index):
        return lax.dynamic_index_in_dim(value, index, axis, keepdims=False)

    def plus(a, b):
        return (a.astype(F32) + b.astype(F32)).astype(BF)

    both = plus(keep, other)
    first = both[..., :cut]
    second = both[..., cut:].reshape(2, half, 2, rows, PACKED - cut)
    first_away, second_away = first[1], pick(second, 2, 1 - low_bit)
    stage1 = (first_away, second_away)
    first = plus(first[0], swap(first_away, 2)).reshape(half, 2, rows, cut)
    second = plus(pick(second, 2, low_bit), dp_swap(second_away, 1))
    first_away, second_away = pick(first, 1, 1 - low_bit), second[1]
    stage2 = (first_away, second_away)
    first = plus(pick(first, 1, low_bit), dp_swap(first_away, 1))
    second = plus(second[0], swap(second_away, 2))
    third = jnp.concatenate([first, second], axis=-1)

    others = [dp_swap(pick(third, 0, (place >> 1) ^ k), 2 * k) for k in range(1, half)]
    sums = (smalls,)
    after = [stage1, stage2, (third,)]
    kept = []
    for m in range(MB):
        res = attention_backward(
            m, ids, hosts, of_tree(grads, m), of_tree(tokens, m), w_heads, sincos,
            forward[m][4:], tuple(sums), after[m],
        )
        sums = res[-2:]
        keep, send = res[:2]
        other = swap(send, 1)
        away = plus(keep[1], other[1])
        if m + 1 < MB:
            after[m + 1] += (away,)
        kept += [keep, other, swap(away, 2)]
        if m + 2 < MB:
            after[m + 2] += (kept[-1],)
    in_grad = input_gradient(gain1, inputs, mgrad, kept)

    vectors = sums[0] + swap(sums[0], 1)
    parts = packed_sums(sums[1], vectors, swap(vectors, 2), n_dp, (*others, kept[5]))
    parts = lax.all_to_all(parts, "dp", 0, 0, tiled=True)
    where = jnp.stack([place * 4 + me, me])
    gq, gk, gv, gr, up, down, o, mg, ms, heads, fg, fs, upb, downb = final_sums(
        where, parts, gain1, attention_norm_bias.reshape(1, D),
        [pick(third, 0, place >> 1), *others], (in_grad,),
    )
    return (
        out, in_grad, mg[0], ms[0], gq, gk, gv, gr, heads, o.T, fg[0], fs[0], up, upb[0], down.T,
        downb[0],
    )


def solution(mesh):
    placed = (
        P(None, "dp", "tensor", None),
        P(),
        P(),
        P("dp", "tensor"),
        P("dp", "tensor"),
        P("dp", "tensor"),
        P("dp", "tensor"),
        P(None, "tensor"),
        P("tensor", "dp"),
        P(),
        P(),
        P("dp", "tensor"),
        P("tensor"),
        P("tensor", "dp"),
        P(),
        P(None, "dp", None),
        P(None, "dp", None),
        P(None, "dp", "tensor", None),
    )
    return jax.shard_map(
        body,
        mesh=mesh,
        in_specs=placed,
        out_specs=(
            P(None, "dp", "tensor", None),
            P(None, "dp", "tensor", None),
            P(("dp", "tensor")),
            P(("dp", "tensor")),
            P("dp", "tensor"),
            P("dp", "tensor"),
            P("dp", "tensor"),
            P("dp", "tensor"),
            P(None, ("dp", "tensor")),
            P("tensor", "dp"),
            P(("dp", "tensor")),
            P(("dp", "tensor")),
            P("dp", "tensor"),
            P(("dp", "tensor")),
            P("tensor", "dp"),
            P(("dp", "tensor")),
        ),
        check_vma=False,
    )
```

```python
import functools
import math

import jax
import jax.numpy as jnp
import numpy as np
from jax import lax
from jax.experimental import pallas as pl
from jax.experimental.pallas import tpu as pltpu
from jax.sharding import PartitionSpec as P

D = 512
HD = 64
FF = 2048
TRUNK = 512
SEG = 64
BRANCHES = 4
LEAVES = 8
MB = 3
TREE = 1280
DEPTH = 640
COLS = 128
QUARTER = 320
PACKED = 2 * D + COLS
QB = 256
EPS = 1e-05
BF = jnp.bfloat16
F32 = jnp.float32

CHUNKS = (
    ((0, "causal"),),
    ((0, None), (256, "causal")),
    ((0, None), (256, None), (512, "segment")),
    ((0, None), (256, None), (512, "host"), (768, "segment")),
    ((0, None), (256, None), (512, "host"), (1024, "segment")),
)
OFFSETS = (0, 256, 768, 1536, 2560)
SAVED = 3584


def nn(a, b):
    return lax.dot_general(a, b, (((1,), (0,)), ((), ())), preferred_element_type=F32)


def nt(a, b):
    return lax.dot_general(a, b, (((1,), (1,)), ((), ())), preferred_element_type=F32)


def key_runs(block):
    runs = []
    for n, (start, _) in enumerate(CHUNKS[block]):
        if runs and runs[-1][0] + runs[-1][1] == start:
            runs[-1][1] += 256
        else:
            runs.append([start, 256, n * 256])
    return runs


def chunk_mask(kind, block, parents, micro):
    key = lax.broadcasted_iota(jnp.int32, (256, QB), 0)
    query = lax.broadcasted_iota(jnp.int32, (256, QB), 1)
    if kind == "causal":
        return key <= query
    if kind == "segment":
        return (key <= query) & (key // SEG == query // SEG)
    lane = lax.broadcasted_iota(jnp.int32, (1, QB), 1) // SEG
    first = (block - 3) * 4
    host = jnp.zeros((1, QB), jnp.int32)
    for n in range(4):
        host = jnp.where(lane == n, parents[micro, first + n], host)
    return (key // SEG + 1) == host


def raised(parents, micro, leaf):
    return (parents[micro, leaf] > 0).astype(jnp.int32)


def last_columns(near, out_ref, parents, micro):
    last = near[...]
    turned = pltpu.roll(last, SEG, 1)
    lane = lax.broadcasted_iota(jnp.int32, (1, 128), 1)
    low = jnp.where(lane < SEG, last, turned)
    out_ref[:, TRUNK : TRUNK + 128] = low
    out_ref[:, TRUNK + 128 : TRUNK + 256] = low
    for pair in range(LEAVES // 2):
        left = raised(parents, micro, 2 * pair)
        right = raised(parents, micro, 2 * pair + 1)
        straight = jnp.where(lane < SEG, 1 - left, right)
        at = TRUNK + 256 + pair * 128
        out_ref[:, at : at + 128] = jnp.where(straight > 0, last, turned)


def norm_kernel(x_ref, gain_ref, bias_ref, fine, coarse, first, rest, sincos, table):
    for n in range(MB):
        x = x_ref[n, 0].astype(F32)
        centered = x - jnp.mean(x, axis=-1, keepdims=True)
        spread = jnp.mean(centered * centered, axis=-1, keepdims=True)
        y = (centered * lax.rsqrt(spread + EPS) * gain_ref[...] + bias_ref[...]).astype(BF)
        if n == 0:
            first[...] = y
        else:
            rest[n - 1] = y
    position_tables(fine, coarse, sincos, table)


def prepare_kernel(where, q, k, v, r, up, down_t, out_t, up_bias, heads, ff):
    for n in range(heads.shape[0]):
        for at, part in enumerate((q, k, v, r)):
            heads[n, :, at * COLS : (at + 1) * COLS] = part[...]
    rows = up.shape[0]
    ff[:, 0:D] = up[...]
    ff[:, D : 2 * D] = down_t[...]
    ff[:, 2 * D : PACKED] = out_t[...]
    at = where[4] * rows
    line = pltpu.roll(jnp.broadcast_to(up_bias[...], (8, D)), jnp.where(at > 0, D - at, 0), 1)
    column = jnp.transpose(jnp.broadcast_to(line[0:1, 0:128], (128, 128)))[0:rows]
    high = column.astype(BF).astype(F32)
    lane = lax.broadcasted_iota(jnp.int32, (rows, COLS), 1)
    ff[:, PACKED:] = jnp.where(lane == 0, high, column - high).astype(BF)


def position_tables(fine, coarse, sincos, table):
    sf, cf = fine[0:256, :], fine[256:512, :]
    for n in range(DEPTH // 128):
        sc, cc = coarse[0:256, n : n + 1], coarse[256:512, n : n + 1]
        cols = slice(n * 128, (n + 1) * 128)
        sines = sc * cf + cc * sf
        cosines = cc * cf - sc * sf
        sincos[0:256, cols] = sines
        sincos[256:512, cols] = cosines
        table[cols, 0:256] = jnp.transpose(cosines.astype(BF))
        table[cols, 256:512] = jnp.transpose(sines.astype(BF))


def copies(sems, pairs):
    made = []
    for n, (source, target) in enumerate(pairs):
        made.append(pltpu.make_async_copy(source, target, sems.at[n]))
        made[-1].start()
    return made


def wait(made):
    for copy in made:
        copy.wait()


def weight_rows(ids, blocks, target):
    rows = blocks[0].shape[0]
    count = len(blocks)
    pairs = []
    for n, block in enumerate(blocks):
        place = (ids[4] ^ n) if count > 1 else 0
        at = pl.multiple_of(place * rows, rows) if count > 1 else 0
        pairs.append((block, target.at[pl.ds(at, rows), :]))
    return pairs


def token_rows(ids, n):
    return pl.ds(pl.multiple_of(ids[n] * QUARTER, SEG), QUARTER)


def forward_kernel(micro, blocks, ids, hosts, *refs):
    x = refs[0:4]
    wb = refs[4 : 4 + blocks]
    hb, sincos, table = refs[4 + blocks : 7 + blocks]
    refs = refs[7 + blocks :]
    att, (probs, inverse, natural, turned) = refs[0:4], refs[4:8]
    xs, w, near, kcat, vt, ct, sct, qts, scores, att_t, ps, inv, nat, trn, att_n, s_in, s_tab, s_out, s_probs = refs[8:]

    x = [v if len(v.shape) == 2 else v.at[micro - 1] for v in x]
    tokens = copies(s_in, [(x[n], xs.at[n]) for n in range(4)] + weight_rows(ids, wb, w))
    pairs = [(table.at[0 : TRUNK + SEG, :], kcat.at[0 : TRUNK + SEG, 0:D])]
    for n in range(1, BRANCHES):
        at = TRUNK + n * SEG
        pairs.append((table.at[TRUNK : TRUNK + SEG, :], kcat.at[at : at + SEG, 0:D]))
    for n in range(LEAVES):
        at = TRUNK + (BRANCHES + n) * SEG
        row = pl.multiple_of(TRUNK + SEG * raised(hosts, micro, n), SEG)
        pairs.append((table.at[pl.ds(row, SEG), :], kcat.at[at : at + SEG, 0:D]))
    pairs.append((sincos.at[:, 0:TRUNK], sct.at[:, 0:TRUNK]))
    pairs.append((sincos.at[:, TRUNK:DEPTH], near))
    wait(tokens[4:])
    for n in range(4):
        tokens[n].wait()
        if n == 1:
            tables = copies(s_tab, pairs)
        y = nn(xs[n], w[:, 0 : 3 * COLS])
        rows = token_rows(ids, n)
        q = y[:, 0:COLS]
        nat[0, rows, :] = (q + hb[0:1, :]).astype(BF)
        nat[1, rows, :] = (q + hb[1:2, :]).astype(BF)
        kcat[rows, D : D + COLS] = y[:, COLS : 2 * COLS].astype(BF)
        nat[2, rows, :] = y[:, 2 * COLS : 3 * COLS].astype(BF)
    ct[...] = jnp.transpose(nat[0])
    trn[0] = jnp.transpose(kcat[:, D : D + COLS])
    vt[...] = jnp.transpose(nat[2])
    sent = copies(s_out, [(nat, natural), (trn.at[0], turned.at[0])])
    wait(tables)
    last_columns(near, sct, hosts, micro)
    factor = math.log2(math.e) / math.sqrt(HD)

    order = (4, 3, 2, 1, 0)

    def saved(head, at):
        rows = pl.ds(OFFSETS[order[at]], 256 * len(CHUNKS[order[at]]))
        return pltpu.make_async_copy(
            ps.at[head, rows, :], probs.at[head, rows, :], s_probs.at[head * 5 + at]
        )

    def one_head(head, _):
        mine = lax.broadcasted_iota(jnp.int32, (1, COLS), 1) // HD == head
        mine_t = lax.broadcasted_iota(jnp.int32, (COLS, 1), 0) // HD == head

        def rotate(block):
            cols = slice(block * QB, (block + 1) * QB)
            qt = qts.at[block]
            position = jnp.where(mine, nat[1, cols, :], 0)
            relative = nt(w[:, 3 * COLS : 4 * COLS], position)
            rs, rc = relative[0:256], relative[256:512]
            sines, cosines = sct[0:256, cols], sct[256:512, cols]
            qt[0:256, :] = (rs * sines + rc * cosines).astype(BF)
            qt[256:512, :] = (rc * sines - rs * cosines).astype(BF)
            qt[512:640, :] = jnp.where(mine_t, ct[:, cols], 0)

        def score(block, n):
            start, kind = CHUNKS[block][n]
            s = nn(kcat[start : start + 256, :], qts[block])
            if kind is not None:
                s = jnp.where(chunk_mask(kind, block, hosts, micro), s, -1e30)
            scores[block % 2, n * 256 : (n + 1) * 256, :] = s
            return jnp.max(s, axis=0, keepdims=True)

        def grow(block, n, peak):
            e = jnp.exp2((scores[block % 2, n * 256 : (n + 1) * 256, :] - peak) * factor)
            row = OFFSETS[block] + n * 256
            ps[head, row : row + 256, :] = e.astype(BF)
            return jnp.sum(e, axis=0, keepdims=True)

        def finish(block, total, at):
            cols = slice(block * QB, (block + 1) * QB)
            out = None
            for start, keys, row in key_runs(block):
                row = OFFSETS[block] + row
                term = nn(vt[:, start : start + keys], ps[head, row : row + keys, :])
                out = term if out is None else out + term
            over = 1.0 / total
            inv[head, :, cols] = jnp.broadcast_to(over, (8, QB))
            att_t[:, cols] = jnp.where(mine_t, out * over, att_t[:, cols])
            saved(head, at).start()

        rotate(order[0])
        peak = None
        for n in range(len(CHUNKS[order[0]])):
            high = score(order[0], n)
            peak = high if peak is None else jnp.maximum(peak, high)
        rotate(order[1])
        todo = []
        todo = []
        for at, block in enumerate(order):
            after = order[at + 1] if at < 4 else None
            count = len(CHUNKS[block])
            ahead = len(CHUNKS[after]) if after is not None else 0
            if at < 3:
                todo.append(functools.partial(rotate, order[at + 2]))
            total, high = None, None
            for n in range(max(count, ahead)):
                if n < ahead:
                    top = score(after, n)
                    high = top if high is None else jnp.maximum(high, top)
                if n < count:
                    part = grow(block, n, peak)
                    total = part if total is None else total + part
                if todo:
                    todo.pop(0)()
            for task in todo:
                task()
            todo = [functools.partial(finish, block, total, at)]
            peak = high
        for task in todo:
            task()
        return 0

    lax.fori_loop(0, 2, one_head, 0)
    wait(sent)
    full = att_t[...].astype(BF)
    trn[1] = full
    att_n[...] = jnp.transpose(full)
    sent = copies(
        s_out,
        [(att_n.at[token_rows(ids, n), :], att[n]) for n in range(4)]
        + [(inv, inverse), (trn.at[1], turned.at[1])],
    )
    for head in range(2):
        for at in range(5):
            saved(head, at).wait()
    wait(sent)


def middle_kernel(ids, *refs):
    a, refs = refs[0 : 4 * MB], refs[4 * MB :]
    x, cot, w_ref, gain, bias, down_bias, out, mgrad, send, keep = refs[:10]
    g = refs[10:18]
    (
        small, a_s, w, hid_all, pg_all, n2_all, mix_all, cot_all, att_all, n2t, cott, mixt,
        mid, xhat, inverse, ffn, n2g, pres, hgs, sems,
    ) = refs[18:]
    m = pl.program_id(0)

    @pl.when(m < MB)
    def _():
        tree_rows(
            m, ids, a, x, cot, w_ref, gain, bias, down_bias, out, mgrad, g, small, a_s, w,
            hid_all, pg_all, n2_all, mix_all, cot_all, att_all, mid, xhat, inverse, ffn, n2g,
            pres, hgs, sems,
        )

    @pl.when(m == MB)
    def _():
        n2t[...] = jnp.transpose(n2_all[...])
        cott[...] = jnp.transpose(cot_all[...])
        mixt[...] = jnp.transpose(mix_all[...])

    @pl.when(m >= MB)
    def _():
        step = m - MB
        part = ids[jnp.where(step < 2, 2 * step + 1, 2 * step - 4)]
        wide = pl.ds(pl.multiple_of(part * D, D), D)
        slim = pl.ds(pl.multiple_of(part * COLS, COLS), COLS)
        value = jnp.concatenate(
            [
                nn(n2t[...], pg_all[:, wide]).astype(BF),
                nn(cott[...], hid_all[:, wide]).astype(BF),
                nn(mixt[...], att_all[:, slim]).astype(BF),
            ],
            axis=1,
        )

        @pl.when(step < 2)
        def _():
            send[0] = value

        @pl.when(step >= 2)
        def _():
            keep[0] = value


def tree_rows(
    m, ids, a, x, cot, w_ref, gain, bias, down_bias, out, mgrad, g, small, a_s, w,
    hid_all, pg_all, n2_all, mix_all, cot_all, att_all, mid, xhat, inverse, ffn, n2g,
    pres, hgs, sems,
):
    groups, rows = w.shape[0], w.shape[2]
    here = pl.ds(pl.multiple_of(m * QUARTER, SEG), QUARTER)
    hid, pg, n2 = hid_all.at[here, :], pg_all.at[here, :], n2_all.at[here, :]

    def part(t, first, last):
        return w[:, t, :, first:last].reshape(D, last - first)

    def loads(first, last):
        pairs = [(a[4 * k + n], a_s.at[k, n]) for k in range(MB) for n in range(4)]
        pairs.append((w_ref.at[:, :, :, 2 * D :], w.at[:, :, :, 2 * D :]))
        pairs += [(w_ref.at[:, t, :, 0 : 2 * D], w.at[:, t, :, 0 : 2 * D]) for t in range(4)]
        pairs = list(enumerate(pairs))[first:last]
        return [pltpu.make_async_copy(p, q, sems.at[n]) for n, (p, q) in pairs]

    @pl.when(m == 0)
    def _():
        made = loads(0, 4 * MB + 5)
        for copy in made:
            copy.start()
        wait(made[: 4 * MB + 1])

    cot_all[here, :] = cot[0, 0]
    total = x[0, 0].astype(F32)
    later = jnp.maximum(m - 1, 0)
    for n in range(4):
        block = a_s[m, n]
        total = total + nt(block, part(ids[n], 2 * D, 2 * D + COLS))
        att_all[here, pl.ds(pl.multiple_of(ids[n] * COLS, COLS), COLS)] = block
    centered = total - jnp.mean(total, axis=-1, keepdims=True)
    spread = jnp.mean(centered * centered, axis=-1, keepdims=True)
    inv = lax.rsqrt(spread + EPS)
    mid[...] = total
    inverse[...] = inv
    xhat[...] = centered * inv
    n2[...] = (centered * inv * gain[...] + bias[...]).astype(BF)

    @pl.when(m == 0)
    def _():
        small[...] = jnp.zeros_like(small)
        wait(loads(4 * MB + 1, 4 * MB + 5))

    width = 256
    steps = FF // width
    biases = []
    for t in range(4):
        extra = jnp.transpose(part(t, PACKED, PACKED + COLS))
        biases.append(extra[0:1, :].astype(F32) + extra[1:2, :].astype(F32))

    def weights(n):
        t, at = n * width // D, n * width % D
        return part(t, at, at + width), part(t, D + at, D + at + width)

    def start(n):
        up, down = weights(n)
        t, at = n * width // D, n * width % D
        pres[n % 3] = nn(n2[...], up) + biases[t][:, at : at + width]
        hgs[n % 3] = nn(cot[0, 0], down)

    def shape(n):
        cols = slice(n * width, (n + 1) * width)
        pre = pres[n % 3]
        cdf = 0.5 * (1.0 + lax.erf(pre * 0.7071067811865476))
        hid[:, cols] = (pre * cdf).astype(BF)
        slope = cdf + pre * jnp.exp(-0.5 * pre * pre) * 0.3989422804014327
        p = hgs[n % 3] * slope
        pg[:, cols] = p.astype(BF)
        t, at = n * width // D, n * width % D
        small[8 + t : 9 + t, at : at + width] += jnp.sum(
            pg[:, cols].astype(F32), axis=0, keepdims=True
        )

    def gather(n):
        cols = slice(n * width, (n + 1) * width)
        up, down = weights(n)
        f, b = nt(hid[:, cols], down), nt(pg[:, cols], up)
        if n == 0:
            ffn[...] = f
            n2g[...] = b
        else:
            ffn[...] += f
            n2g[...] += b

    for n in range(steps + 2):
        if n < steps:
            start(n)
        if 0 <= n - 1 < steps:
            shape(n - 1)
        if n >= 2:
            gather(n - 2)

    out[0, 0] = mid[...] + ffn[...] + down_bias[...]
    gr = n2g[...]
    inv = inverse[...]
    xh = xhat[...]
    c = cot[0, 0].astype(F32)
    small[4:5, :] += jnp.sum(gr * xh, axis=0, keepdims=True)
    small[5:6, :] += jnp.sum(gr, axis=0, keepdims=True)
    small[6:7, :] += jnp.sum(c, axis=0, keepdims=True)
    e = gr * gain[...]
    mg = c + inv * (
        e - jnp.mean(e, axis=-1, keepdims=True) - xh * jnp.mean(e * xh, axis=-1, keepdims=True)
    )
    mgrad[0] = mg
    mixed = mg.astype(BF)
    mix_all[here, :] = mixed
    for n in range(4):
        block = nn(mixed, part(ids[n], 2 * D, 2 * D + COLS)).astype(BF)

        @pl.when(m == 0)
        def _():
            g[n][...] = block

        @pl.when(m > 0)
        def _():
            g[4 + n][later] = block


def backward_kernel(micro, blocks, ids, hosts, *refs):
    d, x, wb = refs[0:4], refs[4:8], refs[8 : 8 + blocks]
    sincos, probs, inverse, natural, turned = refs[8 + blocks : 13 + blocks]
    refs = refs[13 + blocks :]
    last = micro == MB - 1
    before, acc = refs[0], refs[1] if micro else None
    refs = refs[2 if micro else 1 :]
    keep, send, out_s, out_g = refs[0:4]
    refs = refs[4:]
    (
        do, w, near, ps, inv, nat, trn, dot, kcat_t, sct, ds, dqs, dk, dv, dq_t, hc, hp,
        dall, wrt, rel, cg, grel, xall, gw, result, dns, dps, s_in, s_probs, s_x, s_out,
    ) = refs

    grads = [v if len(v.shape) == 2 else v.at[micro - 1] for v in d]
    x = [v if len(v.shape) == 2 else v.at[micro - 1] for v in x]
    first = copies(
        s_in,
        [(grads[n], do.at[token_rows(ids, n), :]) for n in range(4)]
        + [(turned, trn), (inverse, inv), (sincos.at[:, TRUNK:DEPTH], near)]
        + [(sincos.at[:, 0:TRUNK], sct.at[:, 0:TRUNK]), (natural, nat)]
        + weight_rows(ids, wb, w),
    )
    order = (4, 3, 2, 1, 0)
    dk[...] = jnp.zeros_like(dk)
    dv[...] = jnp.zeros_like(dv)
    hc[...] = jnp.zeros_like(hc)
    hp[...] = jnp.zeros_like(hp)
    wait(first[:6])
    chunks = [(0, block) for block in order] + [(1, block) for block in order]
    for n, (head, block) in enumerate(chunks):
        rows = pl.ds(OFFSETS[block], 256 * len(CHUNKS[block]))
        pltpu.make_async_copy(
            probs.at[head, rows, :], ps.at[head, rows, :], s_probs.at[n]
        ).start()
    tokens = copies(s_x, token_pairs(ids, x, xall) + ([(acc, gw)] if micro else []))
    dot[...] = jnp.transpose(do[...])
    kcat_t[512:640, :] = trn[0]
    wait(first[6:8])
    last_columns(near, sct, hosts, micro)
    kcat_t[0:256, :] = sct[256:512, :].astype(BF)
    kcat_t[256:512, :] = sct[0:256, :].astype(BF)
    wait(first[8:])
    wrt[...] = jnp.transpose(w[:, 3 * COLS : 4 * COLS])
    factor = 1.0 / math.sqrt(HD)

    def one_head(head, _):
        mine = lax.broadcasted_iota(jnp.int32, (1, COLS), 1) // HD == head
        mine_t = lax.broadcasted_iota(jnp.int32, (COLS, 1), 0) // HD == head

        def begin(block):
            cols = slice(block * QB, (block + 1) * QB)
            over = inv[head, 0:1, cols]
            grad = jnp.where(mine_t, dot[:, cols].astype(F32), 0.0) * (over * factor)
            delta = jnp.sum(grad * trn[1, :, cols].astype(F32), axis=0, keepdims=True)
            grad_t = grad.astype(BF)
            content = jnp.where(mine, nat[0, cols, :], 0)
            return grad_t, jnp.transpose(grad_t), delta, content

        def gain(block, n, state, slot):
            start = CHUNKS[block][n][0]
            dps[slot] = nn(nat[2, start : start + 256, :], state[0]) - state[2]

        def weigh(block, n, slot):
            row = OFFSETS[block] + n * 256
            p = ps[head, row : row + 256, :].astype(F32)
            ds[block, n * 256 : (n + 1) * 256, :] = (p * dps[slot]).astype(BF)

        def spend(block, n, state):
            row = OFFSETS[block] + n * 256
            keys = slice(CHUNKS[block][n][0], CHUNKS[block][n][0] + 256)
            dv[keys, :] += nn(ps[head, row : row + 256, :], state[1])
            dk[keys, :] += nn(ds[block, n * 256 : (n + 1) * 256, :], state[3])

        def back(block, first, last):
            dq = None
            for start, keys, row in key_runs(block):
                term = nn(
                    kcat_t[first:last, start : start + keys], ds[block, row : row + keys, :]
                )
                dq = term if dq is None else dq + term
            if first < D:
                dqs[block, first:last, :] = dq
            else:
                cg[:, block * QB : (block + 1) * QB] = dq

        def turn(block, first, last):
            cols = slice(block * QB, (block + 1) * QB)
            s1, s2 = dqs[block, first:last, :], dqs[block, 256 + first : 256 + last, :]
            sines, cosines = sct[first:last, cols], sct[256 + first : 256 + last, cols]
            rel[first:last, cols] = (s1 * sines - s2 * cosines).astype(BF)
            rel[256 + first : 256 + last, cols] = (s1 * cosines + s2 * sines).astype(BF)

        items = [(block, n) for block in order for n in range(len(CHUNKS[block]))]
        states = {}
        todo = []
        for i in range(len(items) + 2):
            for task in todo[:3]:
                task()
            todo = todo[3:]
            if i < len(items):
                block, n = items[i]
                if n == 0:
                    at = order.index(block)
                    rows = pl.ds(OFFSETS[block], 256 * len(CHUNKS[block]))
                    pltpu.make_async_copy(
                        probs.at[head, rows, :], ps.at[head, rows, :], s_probs.at[head * 5 + at]
                    ).wait()
                    states[block] = begin(block)
                gain(block, n, states[block], i % 3)
            if 0 <= i - 1 < len(items):
                weigh(*items[i - 1], (i - 1) % 3)
            if i >= 2:
                block, n = items[i - 2]
                spend(block, n, states[block])
                if n + 1 == len(CHUNKS[block]):
                    for cut in (0, 128):
                        todo.append(functools.partial(back, block, cut, cut + 128))
                        todo.append(functools.partial(back, block, 256 + cut, 384 + cut))
                    todo.append(functools.partial(back, block, D, D + COLS))
                    for cut in (0, 128):
                        todo.append(functools.partial(turn, block, cut, cut + 128))
        for task in todo:
            task()
        position = jnp.where(mine, nat[1], 0)
        grel[...] = grel[...] + nn(rel[...], position)
        pgrad = jnp.where(mine_t, nn(wrt[...], rel[...]), 0.0)
        cgrad = jnp.where(mine_t, cg[...], 0.0)
        for n in range(TREE // 128):
            hp[...] += pgrad[:, n * 128 : (n + 1) * 128]
            hc[...] += cgrad[:, n * 128 : (n + 1) * 128]
        dq_t[...] = jnp.where(mine_t, (pgrad + cgrad).astype(BF), dq_t[...])
        return 0

    grel[...] = jnp.zeros_like(grel)
    lax.fori_loop(0, 2, one_head, 0)
    dall[:, 0:COLS] = jnp.transpose(dq_t[...])
    dall[:, COLS : 2 * COLS] = dk[...].astype(BF)
    dall[:, 2 * COLS :] = (dv[...] * math.sqrt(HD)).astype(BF)
    wait(tokens)
    sent = []
    if not micro:
        gw[...] = jnp.zeros_like(gw)
    new = lax.dot_general(
        xall[...], dall[...], (((0,), (0,)), ((), ())), preferred_element_type=F32
    )
    gw[:, 0 : 3 * COLS] += new
    gw[:, 3 * COLS :] += grel[...]
    if last:
        result[...] = gw[...].astype(BF)
    sent += copies(s_x, [(result if last else gw, out_g)])
    sent += token_grads(ids, dall, w, dns, keep, send, s_out)

    columns = jnp.sum(dall[...].astype(F32), axis=0, keepdims=True)
    scaled, plain = None, None
    for n in range(3):
        cols = slice(n * COLS, (n + 1) * COLS)
        weight = w[:, cols].astype(F32)
        one, two = new[:, cols] * weight, columns[:, cols] * weight
        scaled = one if scaled is None else scaled + one
        plain = two if plain is None else plain + two
    out_s[...] = before[...]
    for n, v in enumerate((scaled, plain)):
        v = jnp.sum(jnp.transpose(v), axis=0, keepdims=True)
        out_s[n : n + 1, :] = before[n : n + 1, :] + v
    lanes = pl.ds(pl.multiple_of(ids[0] * COLS, COLS), COLS)
    for n, h in enumerate((hc, hp)):
        v = jnp.sum(jnp.transpose(h[...]), axis=0, keepdims=True)
        out_s[2 + n : 3 + n, lanes] = before[2 + n : 3 + n, lanes] + v
    wait(sent)


def token_pairs(ids, x, target):
    return [(x[n], target.at[token_rows(ids, n), :]) for n in range(4)]


def token_grads(ids, dall, w, dns, keep, send, sems):
    sent = []
    for n, target in ((1, send.at[0]), (3, send.at[1]), (0, keep.at[0]), (2, keep.at[1])):
        dns[n] = nt(dall[token_rows(ids, n), :], w[:, 0 : 3 * COLS]).astype(BF)
        sent.append(pltpu.make_async_copy(dns.at[n], target, sems.at[n]))
        sent[-1].start()
    return sent


def tail_kernel(gain, x, mgrad, *refs):
    parts, (out, xs, ms, gs, result, sems) = refs[:-6], refs[-6:]
    made = []
    for m in range(MB):
        own, near, far = parts[3 * m : 3 * m + 3]
        made.append(
            copies(
                sems.at[m],
                [
                    (x.at[m, 0], xs.at[m]),
                    (mgrad.at[m], ms.at[m]),
                    (own.at[0], gs.at[m, 0]),
                    (near.at[0], gs.at[m, 1]),
                    (far, gs.at[m, 2]),
                ],
            )
        )
    sent = []
    for m in range(MB):
        wait(made[m])
        g = gs[m, 0].astype(F32) + gs[m, 1].astype(F32) + gs[m, 2].astype(F32)
        xf = xs[m].astype(F32)
        centered = xf - jnp.mean(xf, axis=-1, keepdims=True)
        spread = jnp.mean(centered * centered, axis=-1, keepdims=True)
        inv = lax.rsqrt(spread + EPS)
        xh = centered * inv
        e = g * gain[...]
        result[m] = ms[m] + inv * (
            e
            - jnp.mean(e, axis=-1, keepdims=True)
            - xh * jnp.mean(e * xh, axis=-1, keepdims=True)
        )
        sent += copies(sems.at[MB + m], [(result.at[m], out.at[m, 0])])
    wait(sent)


def pack_kernel(grad, own, far, out):
    count, rows = out.shape[0], out.shape[1] - 16
    sums = own[...] + far[...]
    row = lax.broadcasted_iota(jnp.int32, (8, D), 0)
    lane = lax.broadcasted_iota(jnp.int32, (8, D), 1)
    some, more = D // count, FF // count
    for n in range(count):
        out[n, 0:rows, :] = grad[n * rows : (n + 1) * rows, :]
        value = pltpu.roll(sums[0:8, :], (D - n * some) % D, 1)
        line, at = 8 + n * more // D, n * more % D
        line = jnp.broadcast_to(sums[line : line + 1, :], (8, D))
        line = pltpu.roll(line, (D + 128 - at) % D, 1)
        there = (row == 0) & (lane >= 128) & (lane < 128 + more)
        value = jnp.where(lane < some, value, jnp.where(there, line, 0.0))
        high = value.astype(BF).astype(F32)
        out[n, rows : rows + 16, :] = jnp.concatenate([high, value - high], axis=0).astype(BF)


def final_kernel(where, parts, gain, bias, *refs):
    ff, (gq, gk, gv, gr, up, down, out, mg, ms, heads, fg, fs, upb, downb) = refs[:-14], refs[-14:]
    rows = parts.shape[1] - 16
    total = parts[0].astype(F32)
    for n in range(1, parts.shape[0]):
        total = total + parts[n].astype(F32)
    for n, ref in enumerate((gq, gk, gv, gr)):
        ref[...] = total[0:rows, n * COLS : (n + 1) * COLS]
    sums = total[rows : rows + 8] + total[rows + 8 : rows + 16]
    total = ff[0][...].astype(F32)
    for v in ff[1:]:
        total = total + v[...].astype(F32)
    up[...] = total[:, 0:D]
    down[...] = total[:, D : 2 * D]
    out[...] = total[:, 2 * D :]
    each = mg.shape[1]

    def moved(value, at):
        return pltpu.roll(jnp.broadcast_to(value, (8, D)), jnp.where(at > 0, D - at, 0), 1)

    rows = moved(sums, where[1] * each)
    scale = moved(gain[...], where[0] * each)
    shift = moved(bias[...], where[0] * each)
    first = (rows[0:1] - shift[0:1] * rows[1:2]) / scale[0:1]
    mg[...] = first[:, 0:each]
    ms[...] = rows[1:2, 0:each]
    heads[...] = rows[2:4, 0:each]
    fg[...] = rows[4:5, 0:each]
    fs[...] = rows[5:6, 0:each]
    downb[...] = rows[6:7, 0:each]
    upb[...] = moved(sums[0:1], 128 + where[1] * 4 * each)[0:1, 0 : 4 * each]


def whole(shape):
    return pl.BlockSpec(shape, lambda i, *_: (0,) * len(shape))


def cost(flops, nbytes, trans=0):
    return pl.CostEstimate(flops=int(flops), bytes_accessed=int(nbytes), transcendentals=int(trans))


def struct(shape, dtype):
    return jax.ShapeDtypeStruct(shape, dtype)


def call(
    kernel, prefetch, in_specs, out_specs, out_shape, scratch, estimate, *, grid=(), alias=None,
    after=(),
):
    first, last = prefetch + len(in_specs), prefetch + len(in_specs) + len(after)

    def run(*refs):
        kernel(*refs[:first], *refs[last:])

    made = pl.pallas_call(
        run,
        out_shape=out_shape,
        grid_spec=pltpu.PrefetchScalarGridSpec(
            num_scalar_prefetch=prefetch,
            grid=grid,
            in_specs=list(in_specs) + [pl.BlockSpec(memory_space=pl.ANY)] * len(after),
            out_specs=out_specs,
            scratch_shapes=scratch,
        ),
        input_output_aliases=alias or {},
        cost_estimate=estimate,
        compiler_params=pltpu.CompilerParams(
            dimension_semantics=("arbitrary",) * len(grid), vmem_limit_bytes=56 << 20
        ),
    )
    return lambda *operands: made(*operands, *after)


ANY = pl.BlockSpec(memory_space=pl.ANY)


def dma(count):
    return pltpu.SemaphoreType.DMA((count,))


SAVED_SHAPES = [
    ((2, SAVED, QB), BF),
    ((2, 8, TREE), F32),
    ((3, TREE, COLS), BF),
    ((2, COLS, TREE), BF),
]


def of_tree(array, m):
    return array[min(m, 1)]


def attention_forward(m, ids, hosts, tokens, w_heads, head_bias, sincos, table, after=()):
    count = len(w_heads)
    return call(
        functools.partial(forward_kernel, m, count),
        2,
        [ANY] * (4 + count)
        + [pl.BlockSpec(memory_space=pltpu.VMEM), ANY, ANY],
        [ANY] * 8,
        [struct((QUARTER, COLS), BF)] * 4 + [struct(*v) for v in SAVED_SHAPES],
        [
            pltpu.VMEM((4, QUARTER, D), BF),
            pltpu.VMEM((D, D), BF),
            pltpu.VMEM((D, 128), F32),
            pltpu.VMEM((TREE, D + COLS), BF),
            pltpu.VMEM((COLS, TREE), BF),
            pltpu.VMEM((COLS, TREE), BF),
            pltpu.VMEM((D, TREE), F32),
            pltpu.VMEM((5, D + COLS, QB), BF),
            pltpu.VMEM((2, 1024, QB), F32),
            pltpu.VMEM((COLS, TREE), F32),
            *[pltpu.VMEM(*v) for v in SAVED_SHAPES],
            pltpu.VMEM((TREE, COLS), BF),
            dma(4 + count),
            dma(BRANCHES + LEAVES + 2),
            dma(6),
            dma(10),
        ],
        cost(15e9, 12e6, 2e6),
        after=after,
    )(ids, hosts, *tokens, *w_heads, head_bias, sincos, table)


def middle_part(ids, blocks, inputs, cotangent, w_all, gain, bias, down_bias):
    tall = MB * QUARTER
    third = pl.BlockSpec(
        (1, 1, QUARTER, D), lambda m, *_: (jnp.minimum(m, MB - 1), 0, 0, 0)
    )
    small = [(QUARTER, COLS)] * 4 + [(MB - 1, QUARTER, COLS)] * 4
    return call(
        middle_kernel,
        1,
        [ANY] * (4 * MB) + [third, third, ANY, whole((1, D)), whole((1, D)), whole((1, D))],
        [
            third,
            pl.BlockSpec((1, QUARTER, D), lambda m, *_: (jnp.minimum(m, MB - 1), 0, 0)),
            pl.BlockSpec((1, D, PACKED), lambda m, *_: (jnp.clip(m - MB, 0, 1), 0, 0)),
            pl.BlockSpec((1, D, PACKED), lambda m, *_: (jnp.clip(m - MB - 2, 0, 1), 0, 0)),
        ]
        + [whole(v) for v in small]
        + [whole((16, D))],
        [
            struct((MB, 1, QUARTER, D), F32),
            struct((MB, QUARTER, D), F32),
            struct((2, D, PACKED), BF),
            struct((2, D, PACKED), BF),
        ]
        + [struct(v, BF) for v in small]
        + [struct((16, D), F32)],
        [
            pltpu.VMEM((MB, 4, QUARTER, COLS), BF),
            pltpu.VMEM(w_all.shape, BF),
            pltpu.VMEM((tall, FF), BF),
            pltpu.VMEM((tall, FF), BF),
            pltpu.VMEM((tall, D), BF),
            pltpu.VMEM((tall, D), BF),
            pltpu.VMEM((tall, D), BF),
            pltpu.VMEM((tall, D), BF),
            pltpu.VMEM((D, tall), BF),
            pltpu.VMEM((D, tall), BF),
            pltpu.VMEM((D, tall), BF),
            pltpu.VMEM((QUARTER, D), F32),
            pltpu.VMEM((QUARTER, D), F32),
            pltpu.VMEM((QUARTER, 1), F32),
            pltpu.VMEM((QUARTER, D), F32),
            pltpu.VMEM((QUARTER, D), F32),
            pltpu.VMEM((3, QUARTER, 256), F32),
            pltpu.VMEM((3, QUARTER, 256), F32),
            dma(4 * MB + 5),
        ],
        cost(36e9, 36e6, 4e6),
        grid=(MB + 4,),
    )(ids, *blocks, inputs, cotangent, w_all, gain, bias, down_bias.reshape(1, D))


def attention_backward(m, ids, hosts, blocks, tokens, w_heads, sincos, saved, sums, after=()):
    count = len(w_heads)
    last = m == MB - 1
    vmem = pl.BlockSpec(memory_space=pltpu.VMEM)
    first = [struct((2, QUARTER, D), BF)] * 2
    return call(
        functools.partial(backward_kernel, m, count),
        2,
        [ANY] * (13 + count) + [vmem, ANY][: len(sums)],
        [ANY] * len(first) + [vmem, ANY],
        first + [struct((16, D), F32), struct((D, D), BF if last else F32)],
        [
            pltpu.VMEM((TREE, COLS), BF),
            pltpu.VMEM((D, D), BF),
            pltpu.VMEM((D, 128), F32),
            *[pltpu.VMEM(*v) for v in SAVED_SHAPES],
            pltpu.VMEM((COLS, TREE), BF),
            pltpu.VMEM((D + COLS, TREE), BF),
            pltpu.VMEM((D, TREE), F32),
            pltpu.VMEM((5, 1024, QB), BF),
            pltpu.VMEM((5, D, QB), F32),
            pltpu.VMEM((TREE, COLS), F32),
            pltpu.VMEM((TREE, COLS), F32),
            pltpu.VMEM((COLS, TREE), BF),
            pltpu.VMEM((COLS, 128), F32),
            pltpu.VMEM((COLS, 128), F32),
            pltpu.VMEM((TREE, 3 * COLS), BF),
            pltpu.VMEM((COLS, D), BF),
            pltpu.VMEM((D, TREE), BF),
            pltpu.VMEM((COLS, TREE), F32),
            pltpu.VMEM((D, COLS), F32),
            pltpu.VMEM((TREE, D), BF),
            pltpu.VMEM((D, D), F32),
            pltpu.VMEM((D, D) if last else (16, 128), BF),
            pltpu.VMEM((4, QUARTER, D), BF),
            pltpu.VMEM((3, 256, QB), F32),
            dma(9 + count),
            dma(10),
            dma(5),
            dma(4),
        ],
        cost(20e9, 16e6),
        after=after,
    )(ids, hosts, *blocks, *tokens, *w_heads, sincos, *saved, *sums)


def input_gradient(gain, inputs, mgrad, kept, after=()):
    return call(
        tail_kernel,
        0,
        [pl.BlockSpec(memory_space=pltpu.VMEM)] + [ANY] * (2 + 3 * MB),
        ANY,
        struct((MB, 1, QUARTER, D), F32),
        [
            pltpu.VMEM((MB, QUARTER, D), BF),
            pltpu.VMEM((MB, QUARTER, D), F32),
            pltpu.VMEM((MB, 3, QUARTER, D), BF),
            pltpu.VMEM((MB, QUARTER, D), F32),
            pltpu.SemaphoreType.DMA((2 * MB, 5)),
        ],
        cost(MB * QUARTER * D * 20, MB * QUARTER * D * 14),
        after=after,
    )(gain, inputs, mgrad, *kept)


def packed_sums(grad, own, far, n_dp, after):
    vmem = pl.BlockSpec(memory_space=pltpu.VMEM)
    return call(
        pack_kernel,
        0,
        [vmem] * 3,
        vmem,
        struct((n_dp, D // n_dp + 16, D), BF),
        [],
        cost(1e6, 2e6),
        after=after,
    )(grad, own, far)


def final_sums(where, parts, gain, bias, ff, after=()):
    rows = ff[0].shape[0]
    each = rows // 4
    vmem = pl.BlockSpec(memory_space=pltpu.VMEM)
    shapes = (
        [(rows, COLS)] * 4
        + [(rows, D), (rows, D), (rows, COLS), (1, each), (1, each), (2, each)]
        + [(1, each), (1, each), (1, 4 * each), (1, each)]
    )
    return call(
        final_kernel,
        1,
        [vmem] * (3 + len(ff)),
        [vmem] * len(shapes),
        [struct(v, F32) for v in shapes],
        [],
        cost(1e6, 4e6),
        after=after,
    )(where, parts, gain, bias, *ff)


def swap(value, bits):
    return lax.ppermute(value, "tensor", [(n, n ^ bits) for n in range(4)])


def dp_swap(value, bits):
    return lax.ppermute(value, "dp", [(n, n ^ bits) for n in range(lax.axis_size("dp"))])


def ordered(value, *others):
    return lax.optimization_barrier((value, *others))[0]


def body(
    inputs,
    attention_norm_gain,
    attention_norm_bias,
    query_weight,
    key_weight,
    value_weight,
    relative_weight,
    head_bias,
    output_weight,
    feedforward_norm_gain,
    feedforward_norm_bias,
    up_weight,
    up_bias,
    down_weight,
    down_bias,
    parents,
    positions,
    cotangent,
):
    del positions
    n_dp = lax.axis_size("dp")
    rows = query_weight.shape[0]
    me = lax.axis_index("tensor").astype(jnp.int32)
    place = lax.axis_index("dp").astype(jnp.int32)
    ids = jnp.where(jnp.arange(8) < 4, me ^ jnp.arange(8, dtype=jnp.int32), place)
    hosts = parents.reshape(MB, LEAVES)
    gain1 = attention_norm_gain.reshape(1, D)

    vmem = pl.BlockSpec(memory_space=pltpu.VMEM)
    shards, shard = call(
        prepare_kernel,
        1,
        [vmem] * 8,
        [vmem] * 2,
        [struct((n_dp, rows, 4 * COLS), BF), struct((rows, PACKED + COLS), BF)],
        [],
        cost(1e6, 1e6),
    )(
        ids, query_weight, key_weight, value_weight, relative_weight, up_weight, down_weight.T,
        output_weight.T, up_bias.reshape(1, D),
    )
    freq = 10000.0 ** (-2.0 * np.arange(D // 2) / D)[:, None]
    fine, coarse = (
        jnp.asarray(np.concatenate([np.sin(v), np.cos(v)]), F32)
        for v in (freq * np.arange(128), freq * (128.0 * np.arange(8)))
    )
    *normed, sincos, table = call(
        norm_kernel,
        0,
        [vmem] * 5,
        [vmem] * 4,
        [
            struct((QUARTER, D), BF),
            struct((MB - 1, QUARTER, D), BF),
            struct((D, DEPTH), F32),
            struct((DEPTH, D), BF),
        ],
        [],
        cost(MB * QUARTER * D * 10, MB * QUARTER * D * 4),
        after=(shards,),
    )(inputs, gain1, attention_norm_bias.reshape(1, D), fine, coarse)
    w_heads = (lax.all_to_all(shards, "dp", 0, 0, tiled=True).reshape(D, 4 * COLS),)
    first_far = swap(normed[0], 2)
    rest_far = swap(ordered(normed[1], first_far), 2)
    first_tokens = (normed[0], swap(normed[0], 1), first_far, swap(first_far, 1))

    w_all = lax.all_gather(shard, ("dp", "tensor"), axis=0, tiled=False)
    w_all = w_all.reshape(n_dp, 4, rows, PACKED + COLS)
    if rows % 16:
        w_all = jnp.swapaxes(w_all, 0, 1).reshape(1, 4, D, PACKED + COLS)

    forward = []
    tokens = (first_tokens,)
    for m in range(MB):
        if m == 1:
            rest_far = ordered(rest_far, forward[0][0])
            tokens += ((normed[1], swap(normed[1], 1), rest_far, swap(rest_far, 1)),)
        forward.append(
            attention_forward(
                m, ids, hosts, of_tree(tokens, m), w_heads, head_bias, sincos, table
            )
        )

    def spread(blocks):
        return [blocks[0], *(swap(blocks[k], k) for k in (1, 2, 3))]

    middle = middle_part(
        ids, sum((spread(v[:4]) for v in forward), []), inputs, cotangent, w_all,
        feedforward_norm_gain.reshape(1, D), feedforward_norm_bias.reshape(1, D), down_bias,
    )
    out, mgrad, send, keep = middle[:4]
    grads = (spread(middle[4:8]), spread(middle[8:12]))
    smalls = middle[12]

    other = swap(send, 1)
    half = n_dp // 2
    cut = 640
    low_bit = place & 1

    def pick(value, axis, index):
        return lax.dynamic_index_in_dim(value, index, axis, keepdims=False)

    def plus(a, b):
        return (a.astype(F32) + b.astype(F32)).astype(BF)

    both = plus(keep, other)
    first = both[..., :cut]
    second = both[..., cut:].reshape(2, half, 2, rows, PACKED - cut)
    first_away, second_away = first[1], pick(second, 2, 1 - low_bit)
    stage1 = (first_away, second_away)
    first = plus(first[0], swap(first_away, 2)).reshape(half, 2, rows, cut)
    second = plus(pick(second, 2, low_bit), dp_swap(second_away, 1))
    first_away, second_away = pick(first, 1, 1 - low_bit), second[1]
    stage2 = (first_away, second_away)
    first = plus(pick(first, 1, low_bit), dp_swap(first_away, 1))
    second = plus(second[0], swap(second_away, 2))
    third = jnp.concatenate([first, second], axis=-1)

    others = [dp_swap(pick(third, 0, (place >> 1) ^ k), 2 * k) for k in range(1, half)]
    sums = (smalls,)
    after = [stage1, stage2, (third,)]
    kept = []
    for m in range(MB):
        res = attention_backward(
            m, ids, hosts, of_tree(grads, m), of_tree(tokens, m), w_heads, sincos,
            forward[m][4:], tuple(sums), after[m],
        )
        sums = res[-2:]
        keep, send = res[:2]
        other = swap(send, 1)
        away = plus(keep[1], other[1])
        if m + 1 < MB:
            after[m + 1] += (away,)
        kept += [keep, other, swap(away, 2)]
        if m + 2 < MB:
            after[m + 2] += (kept[-1],)
    in_grad = input_gradient(gain1, inputs, mgrad, kept)

    vectors = sums[0] + swap(sums[0], 1)
    parts = packed_sums(sums[1], vectors, swap(vectors, 2), n_dp, (*others, kept[5]))
    parts = lax.all_to_all(parts, "dp", 0, 0, tiled=True)
    where = jnp.stack([place * 4 + me, me])
    gq, gk, gv, gr, up, down, o, mg, ms, heads, fg, fs, upb, downb = final_sums(
        where, parts, gain1, attention_norm_bias.reshape(1, D),
        [pick(third, 0, place >> 1), *others], (in_grad,),
    )
    return (
        out, in_grad, mg[0], ms[0], gq, gk, gv, gr, heads, o.T, fg[0], fs[0], up, upb[0], down.T,
        downb[0],
    )


def solution(mesh):
    placed = (
        P(None, "dp", "tensor", None),
        P(),
        P(),
        P("dp", "tensor"),
        P("dp", "tensor"),
        P("dp", "tensor"),
        P("dp", "tensor"),
        P(None, "tensor"),
        P("tensor", "dp"),
        P(),
        P(),
        P("dp", "tensor"),
        P("tensor"),
        P("tensor", "dp"),
        P(),
        P(None, "dp", None),
        P(None, "dp", None),
        P(None, "dp", "tensor", None),
    )
    return jax.shard_map(
        body,
        mesh=mesh,
        in_specs=placed,
        out_specs=(
            P(None, "dp", "tensor", None),
            P(None, "dp", "tensor", None),
            P(("dp", "tensor")),
            P(("dp", "tensor")),
            P("dp", "tensor"),
            P("dp", "tensor"),
            P("dp", "tensor"),
            P("dp", "tensor"),
            P(None, ("dp", "tensor")),
            P("tensor", "dp"),
            P(("dp", "tensor")),
            P(("dp", "tensor")),
            P("dp", "tensor"),
            P(("dp", "tensor")),
            P("tensor", "dp"),
            P(("dp", "tensor")),
        ),
        check_vma=False,
    )
```
